32 devices in a mesh: pipe: 4 (over x, core), ctx: 8 (over z, y).
Axes of the slice: x: 2, y: 2, z: 4, core: 2. Of those that a mesh axis runs over, the one named last changes fastest.
Arguments:
- features: bfloat16 [4, 1024, 4096], P('pipe', 'ctx'), may hold values from -6 to 6
- state_maps: bfloat16 [4, 1024, 256], P('pipe', 'ctx'), may hold values from -6 to 6
- step_raw: bfloat16 [4, 1024, 64], P('pipe', 'ctx'), may hold values from -6 to 6
- conv_weight: float32 [4, 4, 4352], P('pipe'), may hold values from -3 to 3
- conv_bias: float32 [4, 4352], P('pipe'), may hold values from -3 to 3
- decay_log: float32 [4, 64], P('pipe'), may hold values from -12 to 0
- step_bias: float32 [4, 64], P('pipe'), may hold values from -4 to -2
- skip_gain: float32 [4, 64], P('pipe'), may hold values from 0.5 to 1.5
- output_grads: bfloat16 [4, 1024, 4096], P('pipe', 'ctx'), may hold values from -6 to 6
Outputs:
- feature_grads: bfloat16 [4, 1024, 4096], P('pipe', 'ctx')
- map_grads: bfloat16 [4, 1024, 256], P('pipe', 'ctx')
- step_grads: bfloat16 [4, 1024, 64], P('pipe', 'ctx')
The draws below stay inside these ranges and needn't reach their ends.
All inputs are finite; a program needn't handle non-finite values.
Results may differ from the reference program's by a relative error of at most 0.001.
Values may be sent and summed in bfloat16 or wider, within the bound.
No kernel may reach another device: no remote copies, remote signals or barrier semaphores. Data moves between devices by JAX's collectives and lax.ppermute only.
A program may use at most 128 MiB of HBM per device.

```python
import math
import jax
import jax.numpy as jnp
from jax import lax

HEADS = 64
STATE = 128
KERNEL = 4
BLOCK = 128
INNER = 4096
CHANNELS = 4352
SEQ = 1024
SECTIONS = 4


def draw_decay_log(key, part):
    lower_end = math.log(2.0 / SEQ)
    upper_end = math.log(0.5)
    return jax.random.uniform(key, (SECTIONS, HEADS), jnp.float32, lower_end, upper_end)


def block_levels(own_key, shape, shards, smallest, top_value):
    def one(axis_at, parts):
        steps = jax.random.uniform(jax.random.fold_in(jax.random.fold_in(own_key, 6), axis_at), (parts,), jnp.float32, smallest / len(shards), top_value / len(shards))
        return jnp.repeat(jnp.exp(steps), shape[axis_at] // parts).reshape((-1,) + (1,) * (len(shape) - axis_at - 1))

    loudness = one(*shards[0])
    for cut in shards[1:]:
        loudness = loudness * one(*cut)
    return loudness


def gaussian(rng, shape, width, limit, pieces=(), dtype=jnp.bfloat16):
    array = width * jax.random.normal(rng, shape, jnp.float32)
    if pieces:
        array = array * block_levels(rng, shape, pieces, -0.22, 0.18)
    return jnp.clip(array, -limit, limit).astype(dtype)


def setup_inputs(seed: int = 0) -> dict:
    keys = jax.random.split(jax.random.key(seed), 10)
    return {
        "features": gaussian(keys[0], (SECTIONS, SEQ, INNER), 1.0, 6.0, ((0, 4), (1, 8))),
        "state_maps": gaussian(keys[1], (SECTIONS, SEQ, 2 * STATE), 1.0, 6.0, ((0, 4), (1, 8))),
        "step_raw": gaussian(keys[2], (SECTIONS, SEQ, HEADS), 1.0, 6.0, ((0, 4), (1, 8))),
        "conv_weight": gaussian(keys[3], (SECTIONS, KERNEL, CHANNELS), KERNEL ** -0.5, 3.0, ((0, 4),), jnp.float32),
        "conv_bias": gaussian(keys[4], (SECTIONS, CHANNELS), 0.5, 3.0, ((0, 4),), jnp.float32),
        "decay_log": draw_decay_log(jax.random.fold_in(keys[9], 71), 0),
        "step_bias": jnp.clip(-4.0 + 2.0 * jax.random.uniform(keys[6], (SECTIONS, HEADS), jnp.float32) ** block_levels(keys[6], (SECTIONS, HEADS), ((0, 4),), -0.2, 0.2), -4.0, -2.0),
        "skip_gain": jnp.clip(0.5 + 1.0 * jax.random.uniform(keys[7], (SECTIONS, HEADS), jnp.float32) ** block_levels(keys[7], (SECTIONS, HEADS), ((0, 4),), -0.2, 0.2), 0.5, 1.5),
        "output_grads": gaussian(keys[8], (SECTIONS, SEQ, INNER), 1.0, 6.0, ((0, 4), (1, 8))),
    }


def conv_silu(padded, weight, bias):
    taps = weight.shape[0]
    length = padded.shape[0] - taps + 1
    total = jnp.broadcast_to(bias[None, :], (length, bias.shape[0]))
    for offset in range(taps):
        first = taps - 1 - offset
        total = total + weight[offset][None, :] * padded[first:first + length]
    return jax.nn.silu(total)

def ssd_forward(x_conv, steps, rates, b_rows, c_rows, skips, initial, block):
    length, heads, head_dim = x_conv.shape
    blocks = length // block
    highest = lax.Precision.HIGHEST
    log_decay = (steps * rates[None, :]).reshape(blocks, block, heads)
    cumulative = jnp.cumsum(log_decay, axis=1)
    scaled = (x_conv * steps[:, :, None]).reshape(blocks, block, heads, head_dim)
    b_block = b_rows.reshape(blocks, block, -1)
    c_block = c_rows.reshape(blocks, block, -1)
    scores = jnp.einsum('cqn,ckn->cqk', c_block, b_block, precision=highest)
    causal = (jnp.arange(block)[:, None] >= jnp.arange(block)[None, :])[None, :, :, None]
    spread = cumulative[:, :, None, :] - cumulative[:, None, :, :]
    within = jnp.where(causal, jnp.exp(jnp.where(causal, spread, 0.0)), 0.0)
    mixing = scores[:, :, :, None] * within
    y_within = jnp.einsum('cqkh,ckhp->cqhp', mixing, scaled, precision=highest)
    to_end = jnp.exp(cumulative[:, -1:, :] - cumulative)
    weighted = scaled * to_end[:, :, :, None]
    states = jnp.einsum('ckn,ckhp->chpn', b_block, weighted, precision=highest)
    totals = cumulative[:, -1, :]
    running = jnp.cumsum(totals, axis=0)
    before_sum = running - totals
    earlier = (jnp.arange(blocks)[None, :] < jnp.arange(blocks)[:, None])[:, :, None]
    carry_decay = jnp.where(earlier, jnp.exp(jnp.where(earlier, before_sum[:, None, :] - running[None, :, :], 0.0)), 0.0)
    entering = jnp.einsum('cdh,dhpn->chpn', carry_decay, states, precision=highest)
    entering = entering + jnp.exp(before_sum)[:, :, None, None] * initial[None]
    y_across = jnp.einsum('cqn,chpn->cqhp', c_block, entering, precision=highest)
    y_across = y_across * jnp.exp(cumulative)[:, :, :, None]
    outputs = (y_within + y_across).reshape(length, heads, head_dim) + skips[None, :, None] * x_conv
    last_sum = running[-1]
    final = jnp.exp(last_sum)[:, None, None] * initial
    final = final + jnp.einsum('dh,dhpn->hpn', jnp.exp(last_sum[None, :] - running), states, precision=highest)
    return (outputs, final, jnp.exp(last_sum))

def section_grads(features, state_maps, step_raw, conv_weight, conv_bias, decay_log, step_bias, skip_gain, grad_rows):
    inner = features.shape[1]
    state = state_maps.shape[1] // 2
    heads = decay_log.shape[0]
    head_dim = inner // heads
    taps = conv_weight.shape[0]
    length = features.shape[0]

    def forward(feature_rows, map_rows, step_rows):
        joined = jnp.concatenate([feature_rows, map_rows], axis=1)
        padded = jnp.concatenate([jnp.zeros((taps - 1, joined.shape[1]), jnp.float32), joined], axis=0)
        conv_out = conv_silu(padded, conv_weight, conv_bias)
        x_conv = conv_out[:, :inner].reshape(length, heads, head_dim)
        steps = jax.nn.softplus(step_rows + step_bias[None, :])
        initial = jnp.zeros((heads, head_dim, state), jnp.float32)
        outputs, final, decay = ssd_forward(x_conv, steps, -jnp.exp(decay_log), conv_out[:, inner:inner + state], conv_out[:, inner + state:], skip_gain, initial, BLOCK)
        return outputs
    primal, pull = jax.vjp(forward, features.astype(jnp.float32), state_maps.astype(jnp.float32), step_raw.astype(jnp.float32))
    grad_f, grad_m, grad_s = pull(grad_rows.astype(jnp.float32).reshape(length, heads, head_dim))
    return (grad_f.astype(jnp.bfloat16), grad_m.astype(jnp.bfloat16), grad_s.astype(jnp.bfloat16))

def reference(features, state_maps, step_raw, conv_weight, conv_bias, decay_log, step_bias, skip_gain, output_grads):
    incoming = jnp.concatenate([output_grads[1:], output_grads[:1]], axis=0)

    def per_section(items):
        return section_grads(*items)
    feature_grads, map_grads, step_grads = lax.map(per_section, (features, state_maps, step_raw, conv_weight, conv_bias, decay_log, step_bias, skip_gain, incoming))
    return (feature_grads, map_grads, step_grads)
```

```python
import functools

import jax
import jax.numpy as jnp
from jax import lax
from jax.experimental import pallas as pl
from jax.experimental.pallas import tpu as pltpu
from jax.sharding import PartitionSpec as P

BLOCK = 128
LANES = 128
HEAD = 64
PAD = 8
F32 = jnp.float32
BF16 = jnp.bfloat16
NEG = -1e30
NN = (((1,), (0,)), ((), ()))
NT = (((1,), (1,)), ((), ()))
TN = (((0,), (0,)), ((), ()))


def mm(a, b, dims=NN):
    return lax.dot_general(a, b, dims, preferred_element_type=F32)


def split(a):
    high = a.astype(BF16)
    return high, (a - high.astype(F32)).astype(BF16)


def mm3(a, b, dims=NN):
    (ah, al), (bh, bl) = a, b
    return mm(ah, bh, dims) + (mm(ah, bl, dims) + mm(al, bh, dims))


def iota(shape, axis):
    return lax.broadcasted_iota(jnp.int32, shape, axis)


def expand(values, pair):
    rows = values.shape[0]
    first = jnp.broadcast_to(values[:, 2 * pair : 2 * pair + 1], (rows, LANES))
    second = jnp.broadcast_to(values[:, 2 * pair + 1 : 2 * pair + 2], (rows, LANES))
    return jnp.where(iota((rows, LANES), 1) < HEAD, first, second)


def head_sum(tile, pair):
    onto = (iota((LANES, LANES), 1) == 2 * pair + iota((LANES, LANES), 0) // HEAD).astype(F32).astype(BF16)
    high, low = split(tile)
    return mm(high, onto) + mm(low, onto)


def lanes(pair):
    return slice(pair * LANES, (pair + 1) * LANES)


class Plan:
    def __init__(self, devices, inner, state, heads):
        self.half = devices // 2
        self.inner = inner
        self.state = state
        self.heads = heads // self.half
        self.width = inner // self.half
        self.pairs = self.width // LANES
        self.blocks = self.half
        self.tokens = self.half * BLOCK
        self.conv = self.width + 2 * state
        self.pay = self.conv + LANES
        self.out = self.width + LANES
        self.edge = PAD * self.width // (2 * state)


def place(plan):
    rank = lax.axis_index("ctx")
    return lax.rem(rank, plan.half), lax.div(rank, plan.half)


def call(kernel, plan, out_shape, scratch=(), flops=0):
    return pl.pallas_call(
        functools.partial(kernel, plan),
        out_shape=out_shape,
        scratch_shapes=list(scratch),
        compiler_params=pltpu.CompilerParams(vmem_limit_bytes=56 * 1024 * 1024),
        cost_estimate=pl.CostEstimate(flops=flops, transcendentals=0, bytes_accessed=4 << 20),
    )


def struct(*shape, dtype=F32):
    return jax.ShapeDtypeStruct(shape, dtype)


def pack_kernel(plan, f_ref, m_ref, s_ref, o_ref, *outs):
    own, _ = place(plan)
    half, width = plan.half, plan.width
    pays, edges, grads = outs[:half], outs[half : 2 * half], outs[2 * half :]
    for k in range(half):
        start = pl.multiple_of(jnp.bitwise_xor(own, k) * width, LANES)
        pays[k][:, :width] = f_ref[:, pl.ds(start, width)]
        pays[k][:, width : plan.conv] = m_ref[...]
        pays[k][:, plan.conv :] = jnp.zeros((BLOCK, LANES), BF16)
        pays[k][:, plan.conv : plan.conv + s_ref.shape[1]] = s_ref[...]
        grads[k][...] = o_ref[:, pl.ds(start, width)]
        edges[k][:, :width] = f_ref[BLOCK - 16 :, k * width : (k + 1) * width]
        edges[k][:, width:] = m_ref[BLOCK - 16 :, :]


def forward_kernel(plan, *refs):
    half, width, conv, pairs = plan.half, plan.width, plan.conv, plan.pairs
    pays, edges = refs[:half], refs[half : 2 * half]
    (cw_ref, cb_ref, dl_ref, sb_ref, x_ref, ds_ref, st_ref, sg_ref, cum_ref, el_ref,
     raw, sraw, prm) = refs[2 * half :]
    own, _ = place(plan)
    halo = edges[0][...].astype(F32)
    for k in range(1, half):
        halo = halo + edges[k][...].astype(F32)
    raw[0:PAD, :] = halo[16 - PAD :, :]
    for k in range(half):
        block = jnp.bitwise_xor(own, k) * BLOCK
        raw[pl.ds(pl.multiple_of(block + PAD, 8), BLOCK), :] = pays[k][:, :conv].astype(F32)
        sraw[pl.ds(pl.multiple_of(block, 8), BLOCK), :] = pays[k][:, conv:].astype(F32)
    heads_all = dl_ref.shape[1]
    prm[...] = jnp.zeros_like(prm)
    prm[0:1, 0:heads_all] = -jnp.exp(dl_ref[...])
    prm[1:2, 0:heads_all] = sb_ref[...]
    shift = lax.rem(LANES - own * plan.heads, LANES)
    local = pltpu.roll(prm[...], shift, 1)
    rates, offsets = local[0:1, :], local[1:2, :]
    lower = (iota((BLOCK, BLOCK), 0) >= iota((BLOCK, BLOCK), 1)).astype(F32)
    el_ref[0:BLOCK, :] = jnp.zeros((BLOCK, width), F32)
    tile = 256 if width % 256 == 0 else LANES

    def body(b, carry):
        row = pl.multiple_of(b * BLOCK, BLOCK)
        rows = pl.ds(row, BLOCK)
        for c in range(0, conv, tile):
            window = raw[pl.ds(row, BLOCK + PAD), c : c + tile]
            if c < width:
                cols = pl.ds(pl.multiple_of(own * width + c, LANES), tile)
            else:
                cols = slice(plan.inner + c - width, plan.inner + c - width + tile)
            weight = cw_ref[:, cols]
            v = jnp.broadcast_to(cb_ref[:, cols], (BLOCK, tile))
            for k in range(weight.shape[0]):
                v = v + weight[k : k + 1, :] * window[PAD - k : PAD - k + BLOCK, :]
            s = 1.0 / (1.0 + jnp.exp(-v))
            x_ref[rows, c : c + tile] = v * s
            ds_ref[rows, c : c + tile] = s * (1.0 + v * (1.0 - s))
        a = pltpu.roll(sraw[rows, :], shift, 1) + offsets
        e = jnp.exp(-jnp.abs(a))
        u = 1.0 + e
        d = u - 1.0
        step = jnp.maximum(a, 0.0) + jnp.where(d == 0.0, e, jnp.log(u) * (e / jnp.where(d == 0.0, 1.0, d)))
        st_ref[rows, :] = step
        sg_ref[rows, :] = jnp.where(a >= 0.0, 1.0, e) / u
        cum = lax.dot_general(lower, step * rates, NN, precision=lax.Precision.HIGHEST, preferred_element_type=F32)
        cum_ref[rows, :] = cum
        total = cum[BLOCK - 1 :, :]
        weighted = jnp.exp(total - cum) * step
        decay = jnp.exp(total)
        b_maps = x_ref[rows, width : width + plan.state]
        bt = split(b_maps.T)
        nxt = pl.ds(pl.multiple_of(row + BLOCK, BLOCK), BLOCK)
        for i in range(pairs):
            wx = split(x_ref[rows, lanes(i)] * expand(weighted, i))
            el_ref[nxt, lanes(i)] = el_ref[rows, lanes(i)] * expand(decay, i) + mm3(bt, wx)
        return carry

    lax.fori_loop(0, plan.blocks, body, 0)


def gradient_kernel(plan, *refs):
    half, width, pairs, blocks = plan.half, plan.width, plan.pairs, plan.blocks
    grads = refs[:half]
    x_ref, cum_ref, el_ref, gy_ref, gl_ref, send_ref = refs[half:]
    own, late = place(plan)
    for k in range(half):
        block = pl.multiple_of(jnp.bitwise_xor(own, k) * BLOCK, BLOCK)
        gy_ref[pl.ds(block, BLOCK), :] = grads[k][...]
    gl_ref[blocks * BLOCK :, :] = jnp.zeros((BLOCK, width), F32)

    def body(t, carry):
        row = pl.multiple_of((blocks - 1 - t) * BLOCK, BLOCK)
        rows = pl.ds(row, BLOCK)
        nxt = pl.ds(pl.multiple_of(row + BLOCK, BLOCK), BLOCK)
        cum = cum_ref[rows, :]
        grown, decay = jnp.exp(cum), jnp.exp(cum[BLOCK - 1 :, :])
        ct = split(x_ref[rows, width + plan.state :].T)
        for i in range(pairs):
            ge = split(gy_ref[rows, lanes(i)].astype(F32) * expand(grown, i))
            gl_ref[rows, lanes(i)] = gl_ref[nxt, lanes(i)] * expand(decay, i) + mm3(ct, ge)
        return carry

    lax.fori_loop(0, blocks, body, 0)

    @pl.when(late == 0)
    def _():
        send_ref[...] = el_ref[blocks * BLOCK :, :]

    @pl.when(late != 0)
    def _():
        send_ref[...] = gl_ref[0:BLOCK, :]


def within_kernel(plan, x_ref, st_ref, cum_ref, gy_ref, yw_ref, dw_ref, dsc_ref):
    width, pairs = plan.width, plan.pairs
    causal = iota((BLOCK, BLOCK), 0) >= iota((BLOCK, BLOCK), 1)
    left = iota((BLOCK, LANES), 1) < HEAD

    def body(b, carry):
        rows = pl.ds(pl.multiple_of(b * BLOCK, BLOCK), BLOCK)
        cum = cum_ref[rows, :]
        cum_t = cum.T
        step = st_ref[rows, :]
        b_maps = split(x_ref[rows, width : width + plan.state])
        c_maps = split(x_ref[rows, width + plan.state :])
        scores = mm3(c_maps, b_maps, NT)
        total = jnp.zeros((BLOCK, BLOCK), F32)
        zero = jnp.zeros((BLOCK, LANES), BF16)
        for i in range(pairs):
            xs = x_ref[rows, lanes(i)] * expand(step, i)
            xh, xl = split(xs)
            gy = gy_ref[rows, lanes(i)]
            g0, g1 = jnp.where(left, gy, zero), jnp.where(left, zero, gy)
            decays, mh, ml = [], [], []
            for h in (2 * i, 2 * i + 1):
                spread = jnp.broadcast_to(cum[:, h : h + 1], (BLOCK, BLOCK)) - cum_t[h : h + 1, :]
                decay = jnp.exp(jnp.where(causal, spread, NEG))
                high, low = split(scores * decay)
                decays.append(decay)
                mh.append(high)
                ml.append(low)
            both = jnp.concatenate(
                [
                    jnp.concatenate([jnp.where(left, xh, zero), jnp.where(left, xl, zero)], axis=1),
                    jnp.concatenate([jnp.where(left, zero, xh), jnp.where(left, zero, xl)], axis=1),
                ],
                axis=0,
            )
            high = mm(jnp.concatenate(mh, axis=1), both)
            low = mm(jnp.concatenate(ml, axis=1), both[:, :LANES])
            yw_ref[rows, lanes(i)] = high[:, :LANES] + (high[:, LANES:] + low)
            gs = jnp.concatenate([g0, g1], axis=0)
            dw_ref[rows, lanes(i)] = mm(jnp.concatenate(mh, axis=0), gs, TN) + mm(jnp.concatenate(ml, axis=0), gs, TN)
            dm = mm(jnp.concatenate([gs, gs], axis=1), jnp.concatenate([xh, xl], axis=1), NT)
            total = total + dm[:BLOCK] * decays[0] + dm[BLOCK:] * decays[1]
        dsc_ref[rows, :] = total
        return carry

    lax.fori_loop(0, plan.blocks, body, 0)


def final_kernel(plan, *refs):
    half, width, conv, pairs, blocks, state = plan.half, plan.width, plan.conv, plan.pairs, plan.blocks, plan.state
    (got_ref, x_ref, ds_ref, st_ref, sg_ref, cum_ref, el_ref, gl_ref, gy_ref, yw_ref, dw_ref, dsc_ref,
     cw_ref, dl_ref, sk_ref) = refs[:15]
    outs, maps, halos = refs[15 : 15 + half], refs[15 + half : 15 + 2 * half], refs[15 + 2 * half]
    prm, dz, nxt_dz, carry_ref, o_sc, m_sc, e_sc, lc_sc = refs[16 + 2 * half :]
    own, late = place(plan)
    is_late = late.astype(F32)
    heads_all = dl_ref.shape[1]
    prm[...] = jnp.zeros_like(prm)
    prm[0:1, 0:heads_all] = -jnp.exp(dl_ref[...])
    prm[1:2, 0:heads_all] = sk_ref[...]
    shift = lax.rem(LANES - own * plan.heads, LANES)
    local = pltpu.roll(prm[...], shift, 1)
    rates, skips = local[0:1, :], local[1:2, :]
    upper = (iota((BLOCK, BLOCK), 0) <= iota((BLOCK, BLOCK), 1)).astype(F32)
    nxt_dz[...] = jnp.zeros_like(nxt_dz)
    lc_sc[...] = jnp.zeros_like(lc_sc)
    for b in range(1, blocks):
        lc_sc[b : b + 1, :] = lc_sc[b - 1 : b, :] + cum_ref[b * BLOCK - 1 : b * BLOCK, :]
    whole = lc_sc[blocks - 1 : blocks, :] + cum_ref[blocks * BLOCK - 1 :, :]
    ends = jnp.zeros((8, LANES), F32)
    for i in range(pairs):
        product = jnp.sum(got_ref[:, lanes(i)] * el_ref[blocks * BLOCK :, lanes(i)], axis=0, keepdims=True)
        ends = ends + head_sum(jnp.broadcast_to(product, (8, LANES)), i)
    carry_ref[...] = ends * (1.0 - is_late)

    def body(t, carry):
        b = blocks - 1 - t
        row = pl.multiple_of(b * BLOCK, BLOCK)
        rows = pl.ds(row, BLOCK)
        nxt = pl.ds(pl.multiple_of(row + BLOCK, BLOCK), BLOCK)
        cum, step = cum_ref[rows, :], st_ref[rows, :]
        total = cum[BLOCK - 1 :, :]
        grown, shrunk = jnp.exp(cum), jnp.exp(total - cum)
        before = lc_sc[pl.ds(b, 1), :]
        from_first = jnp.exp(before) * is_late
        to_last = jnp.exp(whole - before - total) * (1.0 - is_late)
        b_f32, c_f32 = x_ref[rows, width : width + state], x_ref[rows, width + state : conv]
        b_maps, c_maps = split(b_f32), split(c_f32)
        dsc = split(dsc_ref[rows, :])
        d_c = mm3(dsc, b_maps)
        d_b = mm3(dsc, c_maps, TN)
        sums = jnp.zeros((BLOCK, LANES), F32)
        direct = jnp.zeros((BLOCK, LANES), F32)
        for i in range(pairs):
            got = got_ref[:, lanes(i)]
            entering = split(el_ref[rows, lanes(i)] + got * expand(from_first, i))
            leaving = split(gl_ref[nxt, lanes(i)] + got * expand(to_last, i))
            x = x_ref[rows, lanes(i)]
            step_x, shrunk_x, grown_x = expand(step, i), expand(shrunk, i), expand(grown, i)
            xs = x * step_x
            gy = gy_ref[rows, lanes(i)].astype(F32)
            y = yw_ref[rows, lanes(i)] + grown_x * mm3(c_maps, entering)
            dxs = dw_ref[rows, lanes(i)] + shrunk_x * mm3(b_maps, leaving)
            d_c = d_c + mm3(split(gy * grown_x), entering, NT)
            d_b = d_b + mm3(split(xs * shrunk_x), leaving, NT)
            sums = sums + head_sum(gy * y - xs * dxs, i)
            direct = direct + head_sum(dxs * x, i)
            dz[0:BLOCK, lanes(i)] = (dxs * step_x + expand(skips, i) * gy) * ds_ref[rows, lanes(i)]
        dz[0:BLOCK, width : width + state] = d_b * ds_ref[rows, width : width + state]
        dz[0:BLOCK, width + state :] = d_c * ds_ref[rows, width + state :]
        dz[BLOCK:, :] = nxt_dz[...]
        d_log = lax.dot_general(upper, sums, NN, precision=lax.Precision.HIGHEST, preferred_element_type=F32)
        d_log = d_log + carry_ref[0:1, :]
        carry_ref[...] = jnp.broadcast_to(d_log[0:1, :], (8, LANES))
        d_step = (d_log * rates + direct) * sg_ref[rows, :]
        valid = iota((BLOCK, LANES), 1) < plan.heads
        o_sc[rows, width:] = jnp.where(valid, d_step, 0.0).astype(BF16)
        for c in range(0, conv, LANES):
            window = dz[:, c : c + LANES]
            if c < width:
                cols = pl.ds(pl.multiple_of(own * width + c, LANES), LANES)
            else:
                cols = slice(plan.inner + c - width, plan.inner + c - width + LANES)
            weight = cw_ref[:, cols]
            grad = weight[0:1, :] * window[0:BLOCK, :]
            for k in range(1, weight.shape[0]):
                grad = grad + weight[k : k + 1, :] * window[k : k + BLOCK, :]
            if c < width:
                o_sc[rows, c : c + LANES] = grad.astype(BF16)
                e_sc[pl.ds(pl.multiple_of(b * PAD, PAD), PAD), c : c + LANES] = grad[BLOCK - PAD :, :]
            else:
                m_sc[rows, c - width : c - width + LANES] = grad

            @pl.when(b == 0)
            def _():
                padded = jnp.concatenate([jnp.zeros((PAD, LANES), F32), window[0:PAD, :]], axis=0)
                spill = jnp.zeros((PAD, LANES), F32)
                for k in range(1, weight.shape[0]):
                    spill = spill + weight[k : k + 1, :] * padded[k : k + PAD, :]
                halos[:, c : c + LANES] = spill

        nxt_dz[...] = dz[0:PAD, :]
        return carry

    lax.fori_loop(0, blocks, body, 0)
    for k in range(half):
        b = jnp.bitwise_xor(own, k)
        rows = pl.ds(pl.multiple_of(b * BLOCK, BLOCK), BLOCK)
        outs[k][...] = o_sc[rows, :]
        maps[k][0:BLOCK, :] = m_sc[rows, :]
        step = 2 * state
        for part in range(width // step):
            maps[k][BLOCK + part * PAD : BLOCK + (part + 1) * PAD, :] = e_sc[
                pl.ds(pl.multiple_of(b * PAD, PAD), PAD), part * step : (part + 1) * step
            ]


def owner_kernel(plan, *refs):
    half, width, state = plan.half, plan.width, plan.state
    outs, maps, halos = refs[:half], refs[half : 2 * half], refs[2 * half : 3 * half]
    f_ref, m_ref, s_ref, edge = refs[3 * half :]
    own, _ = place(plan)
    total = maps[0][0:BLOCK, :]
    spill = halos[0][:, width:]
    steps = jnp.zeros((BLOCK, LANES), F32)
    span = 2 * state
    for k in range(half):
        part = jnp.bitwise_xor(own, k)
        start = pl.multiple_of(part * width, LANES)
        f_ref[:, pl.ds(start, width)] = outs[k][:, :width]
        for piece in range(width // span):
            edge[:, pl.ds(pl.multiple_of(start + piece * span, LANES), span)] = maps[k][
                BLOCK + piece * PAD : BLOCK + (piece + 1) * PAD, :
            ]
        steps = steps + pltpu.roll(outs[k][:, width:].astype(F32), part * plan.heads, 1)
        if k:
            total = total + maps[k][0:BLOCK, :]
            spill = spill + halos[k][:, width:]
    for k in range(half):
        cols = slice(k * width, (k + 1) * width)
        fixed = edge[:, cols] + halos[k][:, :width]
        tail = f_ref[BLOCK - 16 :, cols].astype(F32)
        f_ref[BLOCK - 16 :, cols] = jnp.concatenate([tail[:PAD], fixed], axis=0).astype(BF16)
    m_ref[0 : BLOCK - 16, :] = total[0 : BLOCK - 16].astype(BF16)
    m_ref[BLOCK - 16 :, :] = jnp.concatenate(
        [total[BLOCK - 16 : BLOCK - PAD], total[BLOCK - PAD :] + spill], axis=0
    ).astype(BF16)
    s_ref[...] = steps[:, : s_ref.shape[1]].astype(BF16)


def per_device(sections, devices, features, state_maps, step_raw, conv_weight, conv_bias, decay_log, step_bias, skip_gain, output_grads):
    state = state_maps.shape[2] // 2
    heads = decay_log.shape[1]
    plan = Plan(devices, features.shape[2], state, heads)
    half, width, conv, tokens = plan.half, plan.width, plan.conv, plan.tokens
    weight = conv_weight[0]

    def partner(array, k):
        return lax.ppermute(array, "ctx", [(i, i ^ k) for i in range(devices)])

    packed = call(
        pack_kernel,
        plan,
        [struct(BLOCK, plan.pay, dtype=BF16)] * half
        + [struct(16, conv, dtype=BF16)] * half
        + [struct(BLOCK, width, dtype=BF16)] * half,
    )(features[0], state_maps[0], step_raw[0], output_grads[0])
    pays, edges, grads = packed[:half], packed[half : 2 * half], packed[2 * half :]
    edges = [lax.ppermute(e, "ctx", [(half - 1, half + k)]) for k, e in enumerate(edges)]
    pays = [pays[0]] + [partner(pays[k], k) for k in range(1, half)]

    def shifted(array, k):
        route = [
            (((p + 1) % sections) * devices + i, p * devices + (i ^ k))
            for p in range(sections)
            for i in range(devices)
        ]
        return lax.ppermute(array, ("pipe", "ctx"), route)

    grads = [shifted(g, k) for k, g in enumerate(grads)]
    big = 2 * tokens * state * width
    x_conv, dsilu, steps, sigmoids, cums, states = call(
        forward_kernel,
        plan,
        [struct(tokens, conv), struct(tokens, conv), struct(tokens, LANES), struct(tokens, LANES),
         struct(tokens, LANES), struct(tokens + BLOCK, width)],
        [pltpu.VMEM((tokens + PAD, conv), F32), pltpu.VMEM((tokens, LANES), F32), pltpu.VMEM((8, LANES), F32)],
        flops=6 * big,
    )(*pays, *edges, weight, conv_bias, decay_log, step_bias)
    gy, back, send = call(
        gradient_kernel,
        plan,
        [struct(tokens, width, dtype=BF16), struct(tokens + BLOCK, width), struct(BLOCK, width)],
        flops=3 * big,
    )(*grads, x_conv, cums, states)
    got = partner(send, half)
    y_within, d_within, d_scores = call(
        within_kernel,
        plan,
        [struct(tokens, width), struct(tokens, width), struct(tokens, BLOCK)],
        flops=50 * big,
    )(x_conv, steps, cums, gy)
    results = call(
        final_kernel,
        plan,
        [struct(BLOCK, plan.out, dtype=BF16)] * half
        + [struct(BLOCK + plan.edge, 2 * state)] * half
        + [struct(PAD, conv)],
        [pltpu.VMEM((8, LANES), F32), pltpu.VMEM((BLOCK + PAD, conv), F32), pltpu.VMEM((PAD, conv), F32),
         pltpu.VMEM((8, LANES), F32), pltpu.VMEM((tokens, plan.out), BF16), pltpu.VMEM((tokens, 2 * state), F32),
         pltpu.VMEM((PAD * plan.blocks, width), F32), pltpu.VMEM((max(8, plan.blocks), LANES), F32)],
        flops=12 * big,
    )(got, x_conv, dsilu, steps, sigmoids, cums, states, back, gy, y_within, d_within, d_scores,
      weight, decay_log, skip_gain)
    outs, maps, halo = results[:half], results[half : 2 * half], results[2 * half]
    outs = [outs[0]] + [partner(outs[k], k) for k in range(1, half)]
    maps = [maps[0]] + [partner(maps[k], k) for k in range(1, half)]
    halos = [lax.ppermute(halo, "ctx", [(half + k, half - 1)]) for k in range(half)]
    feature_grads, map_grads, step_grads = call(
        owner_kernel,
        plan,
        [struct(BLOCK, plan.inner, dtype=BF16), struct(BLOCK, 2 * state, dtype=BF16), struct(BLOCK, heads, dtype=BF16)],
        [pltpu.VMEM((PAD, plan.inner), F32)],
    )(*outs, *maps, *halos)
    return (feature_grads[None], map_grads[None], step_grads[None])


def solution(mesh):
    return jax.shard_map(
        functools.partial(per_device, mesh.shape["pipe"], mesh.shape["ctx"]),
        mesh=mesh,
        in_specs=(
            P("pipe", "ctx", None),
            P("pipe", "ctx", None),
            P("pipe", "ctx", None),
            P("pipe", None, None),
            P("pipe", None),
            P("pipe", None),
            P("pipe", None),
            P("pipe", None),
            P("pipe", "ctx", None),
        ),
        out_specs=(P("pipe", "ctx", None), P("pipe", "ctx", None), P("pipe", "ctx", None)),
        check_vma=False,
    )
```

```python
import functools

import jax
import jax.numpy as jnp
from jax import lax
from jax.experimental import pallas as pl
from jax.experimental.pallas import tpu as pltpu
from jax.sharding import PartitionSpec as P

BLOCK = 128
LANES = 128
HEAD = 64
PAD = 8
F32 = jnp.float32
BF16 = jnp.bfloat16
NEG = -1e30
NN = (((1,), (0,)), ((), ()))
NT = (((1,), (1,)), ((), ()))
TN = (((0,), (0,)), ((), ()))


def mm(a, b, dims=NN):
    return lax.dot_general(a, b, dims, preferred_element_type=F32)


def split(a):
    high = a.astype(BF16)
    return high, (a - high.astype(F32)).astype(BF16)


def mm3(a, b, dims=NN):
    (ah, al), (bh, bl) = a, b
    return mm(ah, bh, dims) + (mm(ah, bl, dims) + mm(al, bh, dims))


def iota(shape, axis):
    return lax.broadcasted_iota(jnp.int32, shape, axis)


def expand(values, pair):
    rows = values.shape[0]
    first = jnp.broadcast_to(values[:, 2 * pair : 2 * pair + 1], (rows, LANES))
    second = jnp.broadcast_to(values[:, 2 * pair + 1 : 2 * pair + 2], (rows, LANES))
    return jnp.where(iota((rows, LANES), 1) < HEAD, first, second)


def head_sum(tile, pair):
    onto = (iota((LANES, LANES), 1) == 2 * pair + iota((LANES, LANES), 0) // HEAD).astype(F32).astype(BF16)
    high, low = split(tile)
    return mm(high, onto) + mm(low, onto)


def lanes(pair):
    return slice(pair * LANES, (pair + 1) * LANES)


class Plan:
    def __init__(self, devices, inner, state, heads):
        self.half = devices // 2
        self.inner = inner
        self.state = state
        self.heads = heads // self.half
        self.width = inner // self.half
        self.pairs = self.width // LANES
        self.blocks = self.half
        self.tokens = self.half * BLOCK
        self.conv = self.width + 2 * state
        self.pay = self.conv + LANES
        self.out = self.width + LANES


def place(plan):
    rank = lax.axis_index("ctx")
    return lax.rem(rank, plan.half), lax.div(rank, plan.half)


def call(kernel, plan, out_shape, scratch=(), flops=0):
    return pl.pallas_call(
        functools.partial(kernel, plan),
        out_shape=out_shape,
        scratch_shapes=list(scratch),
        compiler_params=pltpu.CompilerParams(vmem_limit_bytes=32 * 1024 * 1024),
        cost_estimate=pl.CostEstimate(flops=flops, transcendentals=0, bytes_accessed=4 << 20),
    )


def struct(*shape, dtype=F32):
    return jax.ShapeDtypeStruct(shape, dtype)


def near(*shape, dtype=F32):
    return pltpu.VMEM(shape, dtype)


def head_rows(plan, prm, refs, own):
    prm[...] = jnp.zeros_like(prm)
    for row, values in enumerate(refs):
        prm[row : row + 1, 0 : values.shape[1]] = values
    local = pltpu.roll(prm[...], lax.rem(LANES - own * plan.heads, LANES), 1)
    return [local[row : row + 1, :] for row in range(len(refs))]


def pack_kernel(plan, f_ref, m_ref, s_ref, o_ref, *outs):
    own, _ = place(plan)
    half, width = plan.half, plan.width
    steps = s_ref[...].astype(F32).T.astype(BF16)
    pays, edges, grads = outs[:half], outs[half : 2 * half], outs[2 * half :]
    for k in range(half):
        start = pl.multiple_of(jnp.bitwise_xor(own, k) * width, LANES)
        pays[k][:, :width] = f_ref[:, pl.ds(start, width)]
        pays[k][:, width : plan.conv] = m_ref[...]
        pays[k][:, plan.conv :] = jnp.zeros((BLOCK, LANES), BF16)
        pays[k][:, plan.conv : plan.conv + s_ref.shape[0]] = steps
        grads[k][...] = o_ref[:, pl.ds(start, width)]
        edges[k][:, :width] = f_ref[BLOCK - 16 :, k * width : (k + 1) * width]
        edges[k][:, width:] = m_ref[BLOCK - 16 :, :]


def forward_kernel(plan, *refs):
    half, width, conv, pairs = plan.half, plan.width, plan.conv, plan.pairs
    pays, edges = refs[:half], refs[half : 2 * half]
    (cw_ref, cb_ref, dl_ref, sb_ref, x_ref, ds_ref, st_ref, sg_ref, cum_ref, el_ref,
     raw, sraw, prm) = refs[2 * half :]
    own, _ = place(plan)
    halo = edges[0][...].astype(F32)
    for k in range(1, half):
        halo = halo + edges[k][...].astype(F32)
    raw[0:PAD, :] = halo[16 - PAD :, :]
    for k in range(half):
        block = jnp.bitwise_xor(own, k) * BLOCK
        raw[pl.ds(pl.multiple_of(block + PAD, 8), BLOCK), :] = pays[k][:, :conv].astype(F32)
        sraw[pl.ds(pl.multiple_of(block, 8), BLOCK), :] = pays[k][:, conv:].astype(F32)
    rates, offsets = head_rows(plan, prm, [-jnp.exp(dl_ref[...]), sb_ref[...]], own)
    shift = lax.rem(LANES - own * plan.heads, LANES)
    lower = (iota((BLOCK, BLOCK), 0) >= iota((BLOCK, BLOCK), 1)).astype(F32)
    el_ref[0:BLOCK, :] = jnp.zeros((BLOCK, width), F32)
    tile = 256 if width % 256 == 0 else LANES

    def body(b, carry):
        row = pl.multiple_of(b * BLOCK, BLOCK)
        rows = pl.ds(row, BLOCK)
        for c in range(0, conv, tile):
            window = raw[pl.ds(row, BLOCK + PAD), c : c + tile]
            if c < width:
                cols = pl.ds(pl.multiple_of(own * width + c, LANES), tile)
            else:
                cols = slice(plan.inner + c - width, plan.inner + c - width + tile)
            weight = cw_ref[:, cols]
            v = jnp.broadcast_to(cb_ref[:, cols], (BLOCK, tile))
            for k in range(weight.shape[0]):
                v = v + weight[k : k + 1, :] * window[PAD - k : PAD - k + BLOCK, :]
            s = 1.0 / (1.0 + jnp.exp(-v))
            x_ref[rows, c : c + tile] = v * s
            ds_ref[rows, c : c + tile] = s * (1.0 + v * (1.0 - s))
        a = pltpu.roll(sraw[rows, :], shift, 1) + offsets
        e = jnp.exp(-jnp.abs(a))
        u = 1.0 + e
        d = u - 1.0
        step = jnp.maximum(a, 0.0) + jnp.where(d == 0.0, e, jnp.log(u) * (e / jnp.where(d == 0.0, 1.0, d)))
        st_ref[rows, :] = step
        sg_ref[rows, :] = jnp.where(a >= 0.0, 1.0, e) / u
        cum = lax.dot_general(lower, step * rates, NN, precision=lax.Precision.HIGHEST, preferred_element_type=F32)
        cum_ref[rows, :] = cum
        total = cum[BLOCK - 1 :, :]
        weighted = jnp.exp(total - cum) * step
        decay = jnp.exp(total)
        b_maps = x_ref[rows, width : width + plan.state]
        bt = split(b_maps.T)
        nxt = pl.ds(pl.multiple_of(row + BLOCK, BLOCK), BLOCK)
        for i in range(pairs):
            wx = split(x_ref[rows, lanes(i)] * expand(weighted, i))
            el_ref[nxt, lanes(i)] = el_ref[rows, lanes(i)] * expand(decay, i) + mm3(bt, wx)
        return carry

    lax.fori_loop(0, plan.blocks, body, 0)


def gradient_kernel(plan, *refs):
    half, width, pairs, blocks = plan.half, plan.width, plan.pairs, plan.blocks
    grads = refs[:half]
    x_ref, cum_ref, el_ref, gy_ref, gl_ref, send_ref = refs[half:]
    own, late = place(plan)
    for k in range(half):
        block = pl.multiple_of(jnp.bitwise_xor(own, k) * BLOCK, BLOCK)
        gy_ref[pl.ds(block, BLOCK), :] = grads[k][...]
    gl_ref[blocks * BLOCK :, :] = jnp.zeros((BLOCK, width), F32)

    def body(t, carry):
        row = pl.multiple_of((blocks - 1 - t) * BLOCK, BLOCK)
        rows = pl.ds(row, BLOCK)
        nxt = pl.ds(pl.multiple_of(row + BLOCK, BLOCK), BLOCK)
        cum = cum_ref[rows, :]
        grown, decay = jnp.exp(cum), jnp.exp(cum[BLOCK - 1 :, :])
        ct = split(x_ref[rows, width + plan.state :].T)
        for i in range(pairs):
            ge = split(gy_ref[rows, lanes(i)].astype(F32) * expand(grown, i))
            gl_ref[rows, lanes(i)] = gl_ref[nxt, lanes(i)] * expand(decay, i) + mm3(ct, ge)
        return carry

    lax.fori_loop(0, blocks, body, 0)

    @pl.when(late == 0)
    def _():
        send_ref[...] = el_ref[blocks * BLOCK :, :]

    @pl.when(late != 0)
    def _():
        send_ref[...] = gl_ref[0:BLOCK, :]


def within_kernel(plan, x_ref, ds_ref, st_ref, cum_ref, gy_ref, gl_ref, sk_ref, yw_ref, dw_ref, dsc_ref, edge_ref, prm):
    width, pairs, state = plan.width, plan.pairs, plan.state
    own, _ = place(plan)
    (skips,) = head_rows(plan, prm, [sk_ref[...]], own)
    causal = iota((BLOCK, BLOCK), 0) >= iota((BLOCK, BLOCK), 1)
    left = iota((BLOCK, LANES), 1) < HEAD

    def body(b, carry):
        rows = pl.ds(pl.multiple_of(b * BLOCK, BLOCK), BLOCK)
        cum = cum_ref[rows, :]
        cum_t = cum.T
        step = st_ref[rows, :]
        b_maps = split(x_ref[rows, width : width + plan.state])
        c_maps = split(x_ref[rows, width + plan.state :])
        scores = mm3(c_maps, b_maps, NT)
        total = jnp.zeros((BLOCK, BLOCK), F32)
        zero = jnp.zeros((BLOCK, LANES), BF16)
        for i in range(pairs):
            xs = x_ref[rows, lanes(i)] * expand(step, i)
            xh, xl = split(xs)
            gy = gy_ref[rows, lanes(i)]
            g0, g1 = jnp.where(left, gy, zero), jnp.where(left, zero, gy)
            decays, mh, ml = [], [], []
            for h in (2 * i, 2 * i + 1):
                spread = jnp.broadcast_to(cum[:, h : h + 1], (BLOCK, BLOCK)) - cum_t[h : h + 1, :]
                decay = jnp.exp(jnp.where(causal, spread, NEG))
                high, low = split(scores * decay)
                decays.append(decay)
                mh.append(high)
                ml.append(low)
            both = jnp.concatenate(
                [
                    jnp.concatenate([jnp.where(left, xh, zero), jnp.where(left, xl, zero)], axis=1),
                    jnp.concatenate([jnp.where(left, zero, xh), jnp.where(left, zero, xl)], axis=1),
                ],
                axis=0,
            )
            high = mm(jnp.concatenate(mh, axis=1), both)
            low = mm(jnp.concatenate(ml, axis=1), both[:, :LANES])
            yw_ref[rows, lanes(i)] = high[:, :LANES] + (high[:, LANES:] + low)
            gs = jnp.concatenate([g0, g1], axis=0)
            dw_ref[rows, lanes(i)] = mm(jnp.concatenate(mh, axis=0), gs, TN) + mm(jnp.concatenate(ml, axis=0), gs, TN)
            dm = mm(jnp.concatenate([gs, gs], axis=1), jnp.concatenate([xh, xl], axis=1), NT)
            total = total + dm[:BLOCK] * decays[0] + dm[BLOCK:] * decays[1]
        dsc_ref[rows, :] = total
        return carry

    lax.fori_loop(0, plan.blocks, body, 0)
    top = slice(0, 16)
    cum, step = cum_ref[top, :], st_ref[top, :]
    shrunk, grown = jnp.exp(cum_ref[BLOCK - 1 : BLOCK, :] - cum), jnp.exp(cum)
    dsc = split(dsc_ref[0:BLOCK, :])
    first_b = split(x_ref[top, width : width + state])
    d_b = mm3(tuple(part.T for part in split(dsc_ref[0:BLOCK, :])), split(x_ref[0:BLOCK, width + state :]))[top]
    d_c = mm3(dsc, split(x_ref[0:BLOCK, width : width + state]))[top]
    edge_ref[...] = jnp.zeros_like(edge_ref)
    for i in range(pairs):
        leaving = split(gl_ref[BLOCK : 2 * BLOCK, lanes(i)])
        xs = x_ref[top, lanes(i)] * expand(step, i)
        gy = gy_ref[top, lanes(i)].astype(F32)
        shrunk_x = expand(shrunk, i)
        dxs = dw_ref[top, lanes(i)] + shrunk_x * mm3(first_b, leaving)
        d_b = d_b + mm3(split(xs * shrunk_x), leaving, NT)
        dzx = (dxs * expand(step, i) + expand(skips, i) * gy) * ds_ref[top, lanes(i)]
        edge_ref[0:PAD, lanes(i)] = dzx[0:PAD]
        edge_ref[PAD : 2 * PAD, lanes(i)] = (gy * expand(grown, i))[0:PAD]
    edge_ref[2 * PAD : 3 * PAD, 0:state] = (d_b * ds_ref[top, width : width + state])[0:PAD]
    edge_ref[2 * PAD : 3 * PAD, state : 2 * state] = d_c[0:PAD]
    edge_ref[3 * PAD : 4 * PAD, 0:state] = ds_ref[0:PAD, width + state :]


def final_kernel(plan, *refs):
    half, width, conv, pairs, blocks, state = plan.half, plan.width, plan.conv, plan.pairs, plan.blocks, plan.state
    (got_ref, edge_ref, x_ref, ds_ref, st_ref, sg_ref, cum_ref, el_ref, gl_ref, gy_ref, yw_ref, dw_ref, dsc_ref,
     cw_ref, dl_ref, sk_ref) = refs[:16]
    outs, maps = refs[16 : 16 + half], refs[16 + half : 16 + 2 * half]
    prm, dz, nxt_dz, carry_ref, o_sc, m_sc, lc_sc = refs[16 + 2 * half :]
    own, late = place(plan)
    is_late = late.astype(F32)
    rates, skips = head_rows(plan, prm, [-jnp.exp(dl_ref[...]), sk_ref[...]], own)
    upper = (iota((BLOCK, BLOCK), 0) <= iota((BLOCK, BLOCK), 1)).astype(F32)
    after_c = jnp.zeros((2 * PAD, state), F32)
    for i in range(pairs):
        leaving_s = split(el_ref[blocks * BLOCK :, lanes(i)])
        after_c = after_c + mm3(split(edge_ref[PAD : 3 * PAD, lanes(i)]), leaving_s, NT)
    after_c = (after_c[0:PAD] + edge_ref[2 * PAD : 3 * PAD, state : 2 * state]) * edge_ref[3 * PAD : 4 * PAD, 0:state]
    early = iota((PAD, LANES), 0) * 0 + late == 0
    for i in range(pairs):
        nxt_dz[:, lanes(i)] = jnp.where(early, edge_ref[0:PAD, lanes(i)], 0.0)
    nxt_dz[:, width : width + state] = jnp.where(early, edge_ref[2 * PAD : 3 * PAD, 0:state], 0.0)
    nxt_dz[:, width + state :] = jnp.where(early, after_c, 0.0)
    lc_sc[...] = jnp.zeros_like(lc_sc)
    for b in range(1, blocks):
        lc_sc[b : b + 1, :] = lc_sc[b - 1 : b, :] + cum_ref[b * BLOCK - 1 : b * BLOCK, :]
    whole = lc_sc[blocks - 1 : blocks, :] + cum_ref[blocks * BLOCK - 1 :, :]
    ends = jnp.zeros((8, LANES), F32)
    for i in range(pairs):
        product = jnp.sum(got_ref[:, lanes(i)] * el_ref[blocks * BLOCK :, lanes(i)], axis=0, keepdims=True)
        ends = ends + head_sum(jnp.broadcast_to(product, (8, LANES)), i)
    carry_ref[...] = ends * (1.0 - is_late)

    def body(t, carry):
        b = blocks - 1 - t
        row = pl.multiple_of(b * BLOCK, BLOCK)
        rows = pl.ds(row, BLOCK)
        nxt = pl.ds(pl.multiple_of(row + BLOCK, BLOCK), BLOCK)
        cum, step = cum_ref[rows, :], st_ref[rows, :]
        total = cum[BLOCK - 1 :, :]
        grown, shrunk = jnp.exp(cum), jnp.exp(total - cum)
        before = lc_sc[pl.ds(b, 1), :]
        from_first = jnp.exp(before) * is_late
        to_last = jnp.exp(whole - before - total) * (1.0 - is_late)
        b_f32, c_f32 = x_ref[rows, width : width + state], x_ref[rows, width + state : conv]
        b_maps, c_maps = split(b_f32), split(c_f32)
        dsc = split(dsc_ref[rows, :])
        d_c = mm3(dsc, b_maps)
        d_b = mm3(dsc, c_maps, TN)
        sums = jnp.zeros((BLOCK, LANES), F32)
        direct = jnp.zeros((BLOCK, LANES), F32)
        for i in range(pairs):
            got = got_ref[:, lanes(i)]
            entering = split(el_ref[rows, lanes(i)] + got * expand(from_first, i))
            leaving = split(gl_ref[nxt, lanes(i)] + got * expand(to_last, i))
            x = x_ref[rows, lanes(i)]
            step_x, shrunk_x, grown_x = expand(step, i), expand(shrunk, i), expand(grown, i)
            xs = x * step_x
            gy = gy_ref[rows, lanes(i)].astype(F32)
            y = yw_ref[rows, lanes(i)] + grown_x * mm3(c_maps, entering)
            dxs = dw_ref[rows, lanes(i)] + shrunk_x * mm3(b_maps, leaving)
            d_c = d_c + mm3(split(gy * grown_x), entering, NT)
            d_b = d_b + mm3(split(xs * shrunk_x), leaving, NT)
            sums = sums + head_sum(gy * y - xs * dxs, i)
            direct = direct + head_sum(dxs * x, i)
            dz[0:BLOCK, lanes(i)] = (dxs * step_x + expand(skips, i) * gy) * ds_ref[rows, lanes(i)]
        dz[0:BLOCK, width : width + state] = d_b * ds_ref[rows, width : width + state]
        dz[0:BLOCK, width + state :] = d_c * ds_ref[rows, width + state :]
        dz[BLOCK:, :] = nxt_dz[...]
        d_log = lax.dot_general(upper, sums, NN, precision=lax.Precision.HIGHEST, preferred_element_type=F32)
        d_log = d_log + carry_ref[0:1, :]
        carry_ref[...] = jnp.broadcast_to(d_log[0:1, :], (8, LANES))
        d_step = (d_log * rates + direct) * sg_ref[rows, :]
        valid = iota((BLOCK, LANES), 1) < plan.heads
        o_sc[rows, width:] = jnp.where(valid, d_step, 0.0).astype(BF16)
        for c in range(0, conv, LANES):
            window = dz[:, c : c + LANES]
            if c < width:
                cols = pl.ds(pl.multiple_of(own * width + c, LANES), LANES)
            else:
                cols = slice(plan.inner + c - width, plan.inner + c - width + LANES)
            weight = cw_ref[:, cols]
            grad = weight[0:1, :] * window[0:BLOCK, :]
            for k in range(1, weight.shape[0]):
                grad = grad + weight[k : k + 1, :] * window[k : k + BLOCK, :]
            if c < width:
                o_sc[rows, c : c + LANES] = grad.astype(BF16)
            else:
                m_sc[rows, c - width : c - width + LANES] = grad

        nxt_dz[...] = dz[0:PAD, :]
        return carry

    lax.fori_loop(0, blocks, body, 0)
    for k in range(half):
        b = jnp.bitwise_xor(own, k)
        rows = pl.ds(pl.multiple_of(b * BLOCK, BLOCK), BLOCK)
        outs[k][...] = o_sc[rows, :]
        maps[k][...] = m_sc[rows, :]


def owner_kernel(plan, *refs):
    half, width = plan.half, plan.width
    outs, maps = refs[:half], refs[half : 2 * half]
    f_ref, m_ref, s_ref = refs[2 * half :]
    own, _ = place(plan)
    total = maps[0][...]
    steps = jnp.zeros((BLOCK, LANES), F32)
    for k in range(half):
        part = jnp.bitwise_xor(own, k)
        f_ref[:, pl.ds(pl.multiple_of(part * width, LANES), width)] = outs[k][:, :width]
        steps = steps + pltpu.roll(outs[k][:, width:].astype(F32), part * plan.heads, 1)
        if k:
            total = total + maps[k][...]
    m_ref[...] = total.astype(BF16)
    s_ref[...] = steps.T[: s_ref.shape[0]].astype(BF16)


def per_device(sections, devices, features, state_maps, step_raw, conv_weight, conv_bias, decay_log, step_bias, skip_gain, output_grads):
    state = state_maps.shape[2] // 2
    heads = decay_log.shape[1]
    plan = Plan(devices, features.shape[2], state, heads)
    half, width, conv, tokens = plan.half, plan.width, plan.conv, plan.tokens
    weight = conv_weight[0]

    def partner(array, k):
        return lax.ppermute(array, "ctx", [(i, i ^ k) for i in range(devices)])

    packed = call(
        pack_kernel,
        plan,
        [struct(BLOCK, plan.pay, dtype=BF16)] * half
        + [struct(16, conv, dtype=BF16)] * half
        + [struct(BLOCK, width, dtype=BF16)] * half,
    )(features[0], state_maps[0], step_raw[0].T, output_grads[0])
    pays, edges, grads = packed[:half], packed[half : 2 * half], packed[2 * half :]
    edges = [lax.ppermute(e, "ctx", [(half - 1, half + k)]) for k, e in enumerate(edges)]
    pays = [pays[0]] + [partner(pays[k], k) for k in range(1, half)]

    def shifted(array, k):
        route = [
            (((p + 1) % sections) * devices + i, p * devices + (i ^ k))
            for p in range(sections)
            for i in range(devices)
        ]
        return lax.ppermute(array, ("pipe", "ctx"), route)

    grads = [shifted(g, k) for k, g in enumerate(grads)]
    big = 2 * tokens * state * width
    x_conv, dsilu, steps, sigmoids, cums, states = call(
        forward_kernel,
        plan,
        [near(tokens, conv), near(tokens, conv), near(tokens, LANES), near(tokens, LANES),
         near(tokens, LANES), near(tokens + BLOCK, width)],
        [pltpu.VMEM((tokens + PAD, conv), F32), pltpu.VMEM((tokens, LANES), F32), pltpu.VMEM((8, LANES), F32)],
        flops=6 * big,
    )(*pays, *edges, weight, conv_bias, decay_log, step_bias)
    gy, back, send = call(
        gradient_kernel,
        plan,
        [near(tokens, width, dtype=BF16), near(tokens + BLOCK, width), struct(BLOCK, width)],
        flops=3 * big,
    )(*grads, x_conv, cums, states)
    got = partner(send, half)
    y_within, d_within, d_scores, edge = call(
        within_kernel,
        plan,
        [near(tokens, width), near(tokens, width), near(tokens, BLOCK), struct(4 * PAD, width)],
        [pltpu.VMEM((8, LANES), F32)],
        flops=50 * big,
    )(x_conv, dsilu, steps, cums, gy, back, skip_gain)
    edge = partner(edge, half)
    results = call(
        final_kernel,
        plan,
        [struct(BLOCK, plan.out, dtype=BF16)] * half + [struct(BLOCK, 2 * state)] * half,
        [pltpu.VMEM((8, LANES), F32), pltpu.VMEM((BLOCK + PAD, conv), F32), pltpu.VMEM((PAD, conv), F32),
         pltpu.VMEM((8, LANES), F32), pltpu.VMEM((tokens, plan.out), BF16), pltpu.VMEM((tokens, 2 * state), F32),
         pltpu.VMEM((max(8, plan.blocks), LANES), F32)],
        flops=12 * big,
    )(got, edge, x_conv, dsilu, steps, sigmoids, cums, states, back, gy, y_within, d_within, d_scores,
      weight, decay_log, skip_gain)
    outs, maps = results[:half], results[half:]
    outs = [outs[0]] + [partner(outs[k], k) for k in range(1, half)]
    maps = [maps[0]] + [partner(maps[k], k) for k in range(1, half)]
    feature_grads, map_grads, step_grads = call(
        owner_kernel,
        plan,
        [struct(BLOCK, plan.inner, dtype=BF16), struct(BLOCK, 2 * state, dtype=BF16), struct(heads, BLOCK, dtype=BF16)],
    )(*outs, *maps)
    return (feature_grads[None], map_grads[None], step_grads.T[None])


def solution(mesh):
    return jax.shard_map(
        functools.partial(per_device, mesh.shape["pipe"], mesh.shape["ctx"]),
        mesh=mesh,
        in_specs=(
            P("pipe", "ctx", None),
            P("pipe", "ctx", None),
            P("pipe", "ctx", None),
            P("pipe", None, None),
            P("pipe", None),
            P("pipe", None),
            P("pipe", None),
            P("pipe", None),
            P("pipe", "ctx", None),
        ),
        out_specs=(P("pipe", "ctx", None), P("pipe", "ctx", None), P("pipe", "ctx", None)),
        check_vma=False,
    )
```

```python
import functools

import jax
import jax.numpy as jnp
from jax import lax
from jax.experimental import pallas as pl
from jax.experimental.pallas import tpu as pltpu
from jax.sharding import PartitionSpec as P

BLOCK = 128
LANES = 128
HEAD = 64
PAD = 8
PARTS = 2
F32 = jnp.float32
BF16 = jnp.bfloat16
NEG = -1e30
NN = (((1,), (0,)), ((), ()))
NT = (((1,), (1,)), ((), ()))
TN = (((0,), (0,)), ((), ()))


def mm(a, b, dims=NN):
    return lax.dot_general(a, b, dims, preferred_element_type=F32)


def split(a):
    high = a.astype(BF16)
    return high, (a - high.astype(F32)).astype(BF16)


def mm3(a, b, dims=NN):
    (ah, al), (bh, bl) = a, b
    return mm(ah, bh, dims) + (mm(ah, bl, dims) + mm(al, bh, dims))


def iota(shape, axis):
    return lax.broadcasted_iota(jnp.int32, shape, axis)


def wide(a):
    high, low = a
    return jnp.concatenate([high, low], axis=1), high


def mm_wide(a, b):
    (both, high), (bh, bl) = a, b
    return mm(both, jnp.concatenate([bh, bh], axis=0)) + mm(high, bl)


def mm_over(a, b):
    (ah, al), (bh, bl) = a, b
    n = bh.shape[0]
    both = mm(ah, jnp.concatenate([bh, bl], axis=0), NT)
    return both[:, :n] + (both[:, n:] + mm(al, bh, NT))


def expand(values, head, count=LANES):
    rows = values.shape[0]
    left = iota((rows, LANES), 1) < HEAD
    tiles = []
    for h in range(head, head + count // HEAD, 2):
        first = jnp.broadcast_to(values[:, h : h + 1], (rows, LANES))
        second = jnp.broadcast_to(values[:, h + 1 : h + 2], (rows, LANES))
        tiles.append(jnp.where(left, first, second))
    return tiles[0] if len(tiles) == 1 else jnp.concatenate(tiles, axis=1)


def head_sum(tile, head):
    shape = (tile.shape[1], LANES)
    onto = (iota(shape, 1) == head + iota(shape, 0) // HEAD).astype(F32).astype(BF16)
    high, low = split(tile)
    return mm(high, onto) + mm(low, onto)


class Plan:
    def __init__(self, devices, inner, state, heads):
        self.half = devices // 2
        self.inner = inner
        self.state = state
        self.maps = 2 * state
        self.heads = heads // self.half
        self.all = inner // self.half
        self.parts = PARTS
        self.width = self.all // PARTS
        self.tile = 2 * LANES if self.width % (2 * LANES) == 0 else LANES
        self.tiles = self.width // self.tile
        self.blocks = self.half
        self.tokens = self.half * BLOCK


class Stage:
    def __init__(self, plan, part):
        self.plan = plan
        self.part = part
        self.first = part == 0
        self.last = part == plan.parts - 1
        self.head = part * plan.width // HEAD
        self.start = part * plan.width

    def steps(self):
        tile = self.plan.tile
        for i in range(self.plan.tiles):
            lane = self.start + i * tile
            yield slice(i * tile, (i + 1) * tile), slice(lane, lane + tile), lane // HEAD


def place(plan):
    rank = lax.axis_index("ctx")
    return lax.rem(rank, plan.half), lax.div(rank, plan.half)


def call(kernel, stage, out_shape, scratch=(), flops=0):
    return pl.pallas_call(
        functools.partial(kernel, stage),
        out_shape=out_shape,
        scratch_shapes=list(scratch),
        compiler_params=pltpu.CompilerParams(vmem_limit_bytes=32 * 1024 * 1024),
        cost_estimate=pl.CostEstimate(flops=flops, transcendentals=0, bytes_accessed=4 << 20),
    )


def struct(*shape, dtype=F32):
    return jax.ShapeDtypeStruct(shape, dtype)


def near(*shape, dtype=F32):
    return pltpu.VMEM(shape, dtype)


def head_rows(plan, prm, refs, own):
    prm[...] = jnp.zeros_like(prm)
    for row, values in enumerate(refs):
        prm[row : row + 1, 0 : values.shape[1]] = values
    local = pltpu.roll(prm[...], lax.rem(LANES - own * plan.heads, LANES), 1)
    return [local[row : row + 1, :] for row in range(len(refs))]


def run_copies(pairs, sems):
    copies = [pltpu.make_async_copy(source, target, sems.at[n]) for n, (source, target) in enumerate(pairs)]
    for copy in copies:
        copy.start()
    for copy in copies:
        copy.wait()


def pack_kernel(plan, f_ref, m_ref, s_ref, *refs):
    pays, edges, sems = refs[: plan.half], refs[plan.half : -1], refs[-1]
    own, _ = place(plan)
    whole, heads = plan.all, s_ref.shape[0]
    pairs = []
    for k in range(plan.half):
        start = pl.multiple_of(jnp.bitwise_xor(own, k) * whole, LANES)
        pairs.append((f_ref.at[:, pl.ds(start, whole)], pays[k].at[:, pl.ds(0, whole)]))
        pairs.append((m_ref, pays[k].at[:, pl.ds(whole, plan.maps)]))
        for row in range(0, BLOCK, heads):
            pairs.append((s_ref, pays[k].at[pl.ds(row, heads), pl.ds(whole + plan.maps, LANES)]))
        tail = pl.ds(BLOCK - 16, 16)
        pairs.append((f_ref.at[tail, pl.ds(k * whole, whole)], edges[k].at[:, pl.ds(0, whole)]))
        pairs.append((m_ref.at[tail, :], edges[k].at[:, pl.ds(whole, plan.maps)]))
    run_copies(pairs, sems)


def cut_kernel(plan, o_ref, *refs):
    own, _ = place(plan)
    pairs = []
    for k in range(plan.half):
        start = pl.multiple_of(jnp.bitwise_xor(own, k) * plan.all, LANES)
        pairs.append((o_ref.at[:, pl.ds(start, plan.all)], refs[k]))
    run_copies(pairs, refs[-1])


def forward_kernel(plan, *refs):
    half, width, maps, tile = plan.half, plan.all, plan.maps, plan.tile
    conv = width + maps
    pays, edges = refs[:half], refs[half : 2 * half]
    (cw_ref, cb_ref, dl_ref, sb_ref, x_ref, ds_ref, el_ref, xm_ref, dm_ref, st_ref, sg_ref, cum_ref,
     raw, sraw, prm) = refs[2 * half :]
    own, _ = place(plan)
    heads = dl_ref.shape[1]
    halo = edges[0][...].astype(F32)
    for k in range(1, half):
        halo = halo + edges[k][...].astype(F32)
    raw[0:PAD, :] = halo[16 - PAD :, :]
    sraw[...] = jnp.zeros_like(sraw)
    for k in range(half):
        block = jnp.bitwise_xor(own, k) * BLOCK
        raw[pl.ds(pl.multiple_of(block + PAD, 8), BLOCK), :] = pays[k][:, :conv].astype(F32)
        sraw[pl.ds(pl.multiple_of(block, 8), BLOCK), 0:heads] = pays[k][0:heads, conv:].astype(F32).T
    rates, offsets = head_rows(plan, prm, [-jnp.exp(dl_ref[...]), sb_ref[...]], own)
    shift = lax.rem(LANES - own * plan.heads, LANES)
    lower = (iota((BLOCK, BLOCK), 0) >= iota((BLOCK, BLOCK), 1)).astype(F32)
    el_ref[0:BLOCK, :] = jnp.zeros((BLOCK, width), F32)

    def body(b, carry):
        row = pl.multiple_of(b * BLOCK, BLOCK)
        rows = pl.ds(row, BLOCK)
        for c in range(0, conv, tile):
            window = raw[pl.ds(row, BLOCK + PAD), c : c + tile]
            if c < width:
                cols = pl.ds(pl.multiple_of(own * width + c, LANES), tile)
                to_x, to_d, at = x_ref, ds_ref, c
            else:
                cols = slice(plan.inner + c - width, plan.inner + c - width + tile)
                to_x, to_d, at = xm_ref, dm_ref, c - width
            weight = cw_ref[:, cols]
            v = jnp.broadcast_to(cb_ref[:, cols], (BLOCK, tile))
            for k in range(weight.shape[0]):
                v = v + weight[k : k + 1, :] * window[PAD - k : PAD - k + BLOCK, :]
            s = 1.0 / (1.0 + jnp.exp(-v))
            to_x[rows, at : at + tile] = v * s
            to_d[rows, at : at + tile] = s * (1.0 + v * (1.0 - s))
        a = pltpu.roll(sraw[rows, :], shift, 1) + offsets
        e = jnp.exp(-jnp.abs(a))
        u = 1.0 + e
        d = u - 1.0
        step = jnp.maximum(a, 0.0) + jnp.where(d == 0.0, e, jnp.log(u) * (e / jnp.where(d == 0.0, 1.0, d)))
        st_ref[rows, :] = step
        sg_ref[rows, :] = jnp.where(a >= 0.0, 1.0, e) / u
        cum = lax.dot_general(lower, step * rates, NN, precision=lax.Precision.HIGHEST, preferred_element_type=F32)
        cum_ref[rows, :] = cum
        total = cum[BLOCK - 1 :, :]
        weighted = jnp.exp(total - cum) * step
        decay = jnp.exp(total)
        bt = wide(split(xm_ref[rows, : plan.state].T))
        nxt = pl.ds(pl.multiple_of(row + BLOCK, BLOCK), BLOCK)
        for c in range(0, width, tile):
            at, head = slice(c, c + tile), c // HEAD
            wx = split(x_ref[rows, at] * expand(weighted, head, tile))
            el_ref[nxt, at] = el_ref[rows, at] * expand(decay, head, tile) + mm_wide(bt, wx)
        return carry

    lax.fori_loop(0, plan.blocks, body, 0)


def gradient_kernel(stage, *refs):
    plan, first, last = stage.plan, stage.first, stage.last
    half, width, blocks, tile, state = plan.half, plan.width, plan.blocks, plan.tile, plan.state
    grads = refs[:half]
    xm_ref, cum_ref, el_ref, x_ref, ds_ref, dm_ref, st_ref, sk_ref = refs[half : half + 8]
    refs = refs[half + 8 :]
    if not first:
        top_old, refs = refs[0], refs[1:]
    gy_ref, gl_ref, send_ref = refs[:3]
    if not last:
        top_ref = refs[3]
    prm = refs[-1]
    own, late = place(plan)
    for k in range(half):
        block = pl.multiple_of(jnp.bitwise_xor(own, k) * BLOCK, BLOCK)
        gy_ref[pl.ds(block, BLOCK), :] = grads[k][:, stage.start : stage.start + width]
    gl_ref[blocks * BLOCK :, :] = jnp.zeros((BLOCK, width), F32)

    def body(t, carry):
        row = pl.multiple_of((blocks - 1 - t) * BLOCK, BLOCK)
        rows = pl.ds(row, BLOCK)
        nxt = pl.ds(pl.multiple_of(row + BLOCK, BLOCK), BLOCK)
        cum = cum_ref[rows, :]
        grown, decay = jnp.exp(cum), jnp.exp(cum[BLOCK - 1 :, :])
        ct = wide(split(xm_ref[rows, plan.state :].T))
        for at, _, head in stage.steps():
            ge = split(gy_ref[rows, at].astype(F32) * expand(grown, head, tile))
            gl_ref[rows, at] = gl_ref[nxt, at] * expand(decay, head, tile) + mm_wide(ct, ge)
        return carry

    lax.fori_loop(0, blocks, body, 0)

    @pl.when(late == 0)
    def _():
        send_ref[0:BLOCK, :] = el_ref[blocks * BLOCK :, stage.start : stage.start + width]
        send_ref[BLOCK:, :] = jnp.zeros((16, width), F32)
        if not last:
            top_ref[...] = jnp.zeros_like(top_ref)

    @pl.when(late != 0)
    def _():
        send_ref[0:BLOCK, :] = gl_ref[0:BLOCK, :]
        (skips,) = head_rows(plan, prm, [sk_ref[...]], own)
        top = slice(0, 16)
        edge = send_ref.at[BLOCK : BLOCK + 16, :]
        cum, step, cum_t = cum_ref[top, :], st_ref[top, :], cum_ref[0:BLOCK, :].T
        shrunk, grown = jnp.exp(cum_ref[BLOCK - 1 : BLOCK, :] - cum), jnp.exp(cum)
        top_b, first_c = split(xm_ref[top, :state]), split(xm_ref[0:BLOCK, state:])
        wide_b = wide(top_b)
        scores = mm3(top_b, first_c, NT)
        causal = iota((16, BLOCK), 0) <= iota((16, BLOCK), 1)
        if first:
            d_b, dsc = jnp.zeros((16, state), F32), jnp.zeros((16, BLOCK), F32)
        else:
            d_b, dsc = top_old[:, :state], top_old[:, state:]
        zero, blank = jnp.zeros((BLOCK, LANES), BF16), jnp.zeros((16, LANES), BF16)
        left, left_top = iota((BLOCK, LANES), 1) < HEAD, iota((16, LANES), 1) < HEAD
        for i in range(width // LANES):
            at, head = slice(i * LANES, (i + 1) * LANES), stage.head + 2 * i
            among = slice(head * HEAD, head * HEAD + LANES)
            step_x, shrunk_x = expand(step, head), expand(shrunk, head)
            xs = x_ref[top, among] * step_x
            gy = gy_ref[0:BLOCK, at]
            decays, mh, ml = [], [], []
            for h in (head, head + 1):
                spread = cum_t[h : h + 1, :] - jnp.broadcast_to(cum[:, h : h + 1], (16, BLOCK))
                decay = jnp.exp(jnp.where(causal, spread, NEG))
                high, low = split(scores * decay)
                decays.append(decay)
                mh.append(high)
                ml.append(low)
            gs = jnp.concatenate([jnp.where(left, gy, zero), jnp.where(left, zero, gy)], axis=0)
            dxs = mm(jnp.concatenate(mh, axis=1), gs) + mm(jnp.concatenate(ml, axis=1), gs)
            xh, xl = split(xs)
            rows = [jnp.where(left_top, xh, blank), jnp.where(left_top, blank, xh)]
            rows += [jnp.where(left_top, xl, blank), jnp.where(left_top, blank, xl)]
            dm = mm(jnp.concatenate(rows, axis=0), gy, NT)
            dsc = dsc + (dm[0:16] + dm[32:48]) * decays[0] + (dm[16:32] + dm[48:64]) * decays[1]
            leaving = split(gl_ref[BLOCK : 2 * BLOCK, at])
            dxs = dxs + shrunk_x * mm_wide(wide_b, leaving)
            d_b = d_b + mm_over(split(xs * shrunk_x), leaving)
            top_gy = gy[0:16].astype(F32)
            edge[0:PAD, at] = ((dxs * step_x + expand(skips, head) * top_gy) * ds_ref[top, among])[0:PAD]
            edge[PAD:, at] = (top_gy * expand(grown, head))[0:PAD]
        if last:
            parts = split(dsc)
            d_b = (d_b + mm3(parts, first_c)) * dm_ref[top, :state]
            d_c = mm3(parts, top_b, TN)
            silu_c = dm_ref[top, state:]
            edge[3:6, 0:state] = d_b[0:3]
            edge[6:8, 0:state] = silu_c[0:2]
            edge[11:14, 0:state] = d_c[0:3]
            edge[14:15, 0:state] = silu_c[2:3]
        else:
            top_ref[:, :state] = d_b
            top_ref[:, state:] = dsc


def within_kernel(stage, *refs):
    plan, first = stage.plan, stage.first
    x_ref, xm_ref, st_ref, cum_ref, gy_ref = refs[:5]
    refs = refs[5:]
    if not first:
        dsc_old, refs = refs[0], refs[1:]
    yw_ref, dw_ref, dsc_ref = refs
    width, state = plan.width, plan.state
    causal = iota((BLOCK, BLOCK), 0) >= iota((BLOCK, BLOCK), 1)
    left = iota((BLOCK, LANES), 1) < HEAD

    def body(b, carry):
        rows = pl.ds(pl.multiple_of(b * BLOCK, BLOCK), BLOCK)
        cum = cum_ref[rows, :]
        cum_t = cum.T
        step = st_ref[rows, :]
        b_maps = split(xm_ref[rows, :state])
        c_maps = split(xm_ref[rows, state:])
        scores = mm3(c_maps, b_maps, NT)
        total = jnp.zeros((BLOCK, BLOCK), F32) if first else dsc_old[rows, :]
        zero = jnp.zeros((BLOCK, LANES), BF16)
        for i in range(width // LANES):
            at, head = slice(i * LANES, (i + 1) * LANES), stage.head + 2 * i
            xs = x_ref[rows, head * HEAD : head * HEAD + LANES] * expand(step, head)
            xh, xl = split(xs)
            gy = gy_ref[rows, at]
            g0, g1 = jnp.where(left, gy, zero), jnp.where(left, zero, gy)
            decays, mh, ml = [], [], []
            for h in (head, head + 1):
                spread = jnp.broadcast_to(cum[:, h : h + 1], (BLOCK, BLOCK)) - cum_t[h : h + 1, :]
                decay = jnp.exp(jnp.where(causal, spread, NEG))
                high, low = split(scores * decay)
                decays.append(decay)
                mh.append(high)
                ml.append(low)
            both = jnp.concatenate(
                [
                    jnp.concatenate([jnp.where(left, xh, zero), jnp.where(left, xl, zero)], axis=1),
                    jnp.concatenate([jnp.where(left, zero, xh), jnp.where(left, zero, xl)], axis=1),
                ],
                axis=0,
            )
            high = mm(jnp.concatenate(mh, axis=1), both)
            low = mm(jnp.concatenate(ml, axis=1), both[:, :LANES])
            yw_ref[rows, at] = high[:, :LANES] + (high[:, LANES:] + low)
            gs = jnp.concatenate([g0, g1], axis=0)
            dw_ref[rows, at] = mm(jnp.concatenate(mh, axis=0), gs, TN) + mm(jnp.concatenate(ml, axis=0), gs, TN)
            dm = mm(jnp.concatenate([gs, gs], axis=1), jnp.concatenate([xh, xl], axis=1), NT)
            total = total + dm[:BLOCK] * decays[0] + dm[BLOCK:] * decays[1]
        dsc_ref[rows, :] = total
        return carry

    lax.fori_loop(0, plan.blocks, body, 0)


def final_kernel(stage, *refs):
    plan, first, last = stage.plan, stage.first, stage.last
    half, width, blocks, state, tile, maps = plan.half, plan.width, plan.blocks, plan.state, plan.tile, plan.maps
    (both_ref, x_ref, xm_ref, ds_ref, st_ref, sg_ref, cum_ref, el_ref, gl_ref, gy_ref, yw_ref, dw_ref,
     cw_ref, dl_ref, sk_ref) = refs[:15]
    refs = refs[15:]
    got_ref, edge_ref = both_ref.at[0:BLOCK, :], both_ref.at[BLOCK : BLOCK + 16, :]
    if last:
        dsc_ref, dm_ref, refs = refs[0], refs[1], refs[2:]
    if not first:
        bc_old, ac_old, dst_old, refs = refs[0], refs[1], refs[2], refs[3:]
    outs, refs = refs[:half], refs[half:]
    if last:
        map_outs, refs = refs[:half], refs[half:]
        m_sc = refs[-1]
    else:
        bc_ref, ac_ref, dst_ref, refs = refs[0], refs[1], refs[2], refs[3:]
    prm, dz, nxt_dz, carry_ref, o_sc, lc_sc = refs[:6]
    conv = width + maps if last else width
    own, late = place(plan)
    is_late = late.astype(F32)
    rates, skips = head_rows(plan, prm, [-jnp.exp(dl_ref[...]), sk_ref[...]], own)
    upper = (iota((BLOCK, BLOCK), 0) <= iota((BLOCK, BLOCK), 1)).astype(F32)
    after_c = jnp.zeros((16, state), F32) if first else ac_old[...]
    for at, among, _ in stage.steps():
        after_c = after_c + mm_over(split(edge_ref[:, at]), split(el_ref[blocks * BLOCK :, among]))
    early = iota((PAD, LANES), 0) * 0 + late == 0
    for c in range(0, width, LANES):
        nxt_dz[:, c : c + LANES] = jnp.where(early, edge_ref[0:PAD, c : c + LANES], 0.0)
    if last:
        rest = jnp.zeros((PAD - 3, state), F32)
        nxt_dz[:, width : width + state] = jnp.where(early, jnp.concatenate([edge_ref[3:6, 0:state], rest], axis=0), 0.0)
        silu_c = jnp.concatenate([edge_ref[6:8, 0:state], edge_ref[14:15, 0:state]], axis=0)
        after_c = (after_c[PAD : PAD + 3] + edge_ref[11:14, 0:state]) * silu_c
        nxt_dz[:, width + state :] = jnp.where(early, jnp.concatenate([after_c, rest], axis=0), 0.0)
    else:
        ac_ref[...] = after_c
    lc_sc[...] = jnp.zeros_like(lc_sc)
    for b in range(1, blocks):
        lc_sc[b : b + 1, :] = lc_sc[b - 1 : b, :] + cum_ref[b * BLOCK - 1 : b * BLOCK, :]
    whole = lc_sc[blocks - 1 : blocks, :] + cum_ref[blocks * BLOCK - 1 :, :]
    ends = jnp.zeros((8, LANES), F32)
    for at, among, head in stage.steps():
        product = jnp.sum(got_ref[:, at] * el_ref[blocks * BLOCK :, among], axis=0, keepdims=True)
        ends = ends + head_sum(jnp.broadcast_to(product, (8, tile)), head)
    carry_ref[...] = ends * (1.0 - is_late)

    def body(t, carry):
        b = blocks - 1 - t
        row = pl.multiple_of(b * BLOCK, BLOCK)
        rows = pl.ds(row, BLOCK)
        nxt = pl.ds(pl.multiple_of(row + BLOCK, BLOCK), BLOCK)
        cum, step = cum_ref[rows, :], st_ref[rows, :]
        total = cum[BLOCK - 1 :, :]
        grown, shrunk = jnp.exp(cum), jnp.exp(total - cum)
        before = lc_sc[pl.ds(b, 1), :]
        from_first = jnp.exp(before) * is_late
        to_last = jnp.exp(whole - before - total) * (1.0 - is_late)
        b_maps, c_maps = split(xm_ref[rows, :state]), split(xm_ref[rows, state:])
        b_wide, c_wide = wide(b_maps), wide(c_maps)
        if first:
            d_b = d_c = jnp.zeros((BLOCK, state), F32)
        else:
            d_b, d_c = bc_old[rows, :state], bc_old[rows, state:]
        if last:
            dsc = dsc_ref[rows, :]
            d_c = d_c + mm3(split(dsc), b_maps)
            d_b = d_b + mm3(split(dsc.T), c_maps)
        sums = jnp.zeros((BLOCK, LANES), F32)
        direct = jnp.zeros((BLOCK, LANES), F32)
        for at, among, head in stage.steps():
            got = got_ref[:, at]
            entering = split(el_ref[rows, among] + got * expand(from_first, head, tile))
            leaving = split(gl_ref[nxt, at] + got * expand(to_last, head, tile))
            x = x_ref[rows, among]
            step_x, shrunk_x, grown_x = expand(step, head, tile), expand(shrunk, head, tile), expand(grown, head, tile)
            xs = x * step_x
            gy = gy_ref[rows, at].astype(F32)
            y = yw_ref[rows, at] + grown_x * mm_wide(c_wide, entering)
            dxs = dw_ref[rows, at] + shrunk_x * mm_wide(b_wide, leaving)
            d_c = d_c + mm_over(split(gy * grown_x), entering)
            d_b = d_b + mm_over(split(xs * shrunk_x), leaving)
            sums = sums + head_sum(gy * y - xs * dxs, head)
            direct = direct + head_sum(dxs * x, head)
            dz[0:BLOCK, at] = (dxs * step_x + expand(skips, head, tile) * gy) * ds_ref[rows, among]
        d_log = lax.dot_general(upper, sums, NN, precision=lax.Precision.HIGHEST, preferred_element_type=F32)
        d_log = d_log + carry_ref[0:1, :]
        carry_ref[...] = jnp.broadcast_to(d_log[0:1, :], (8, LANES))
        d_step = (d_log * rates + direct) * sg_ref[rows, :]
        lane = iota((BLOCK, LANES), 1)
        d_step = jnp.where((lane >= stage.head) & (lane < stage.head + width // HEAD), d_step, 0.0)
        if not first:
            d_step = d_step + dst_old[rows, :]
        if last:
            o_sc[rows, width:] = d_step.astype(BF16)
            dz[0:BLOCK, width : width + state] = d_b * dm_ref[rows, :state]
            dz[0:BLOCK, width + state :] = d_c * dm_ref[rows, state:]
        else:
            dst_ref[rows, :] = d_step
            bc_ref[rows, :state] = d_b
            bc_ref[rows, state:] = d_c
        dz[BLOCK:, :] = nxt_dz[...]
        for c in range(0, conv, LANES):
            window = dz[:, c : c + LANES]
            if c < width:
                cols = pl.ds(pl.multiple_of(own * plan.all + stage.start + c, LANES), LANES)
            else:
                cols = slice(plan.inner + c - width, plan.inner + c - width + LANES)
            weight = cw_ref[:, cols]
            grad = weight[0:1, :] * window[0:BLOCK, :]
            for k in range(1, weight.shape[0]):
                grad = grad + weight[k : k + 1, :] * window[k : k + BLOCK, :]
            if c < width:
                o_sc[rows, c : c + LANES] = grad.astype(BF16)
            else:
                m_sc[rows, c - width : c - width + LANES] = grad
        nxt_dz[...] = dz[0:PAD, :]
        return carry

    lax.fori_loop(0, blocks, body, 0)
    for k in range(half):
        rows = pl.ds(pl.multiple_of(jnp.bitwise_xor(own, k) * BLOCK, BLOCK), BLOCK)
        outs[k][...] = o_sc[rows, :]
        if last:
            map_outs[k][...] = m_sc[rows, :]


def owner_kernel(plan, *refs):
    half, width, parts = plan.half, plan.width, plan.parts
    outs, maps = refs[: half * parts], refs[half * parts : half * (parts + 1)]
    f_ref, m_ref, s_ref = refs[half * (parts + 1) :]
    own, _ = place(plan)
    total = maps[0][...]
    steps = jnp.zeros((BLOCK, LANES), F32)
    for k in range(half):
        part = jnp.bitwise_xor(own, k)
        for p in range(parts):
            start = pl.multiple_of(part * plan.all + p * width, LANES)
            f_ref[:, pl.ds(start, width)] = outs[p * half + k][:, :width]
        steps = steps + pltpu.roll(outs[(parts - 1) * half + k][:, width:].astype(F32), part * plan.heads, 1)
        if k:
            total = total + maps[k][...]
    m_ref[...] = total.astype(BF16)
    s_ref[...] = steps.T[: s_ref.shape[0]].astype(BF16)


def per_device(sections, devices, features, state_maps, step_raw, conv_weight, conv_bias, decay_log, step_bias, skip_gain, output_grads):
    state = state_maps.shape[2] // 2
    heads = decay_log.shape[1]
    plan = Plan(devices, features.shape[2], state, heads)
    half, width, tokens, parts, maps = plan.half, plan.width, plan.tokens, plan.parts, plan.maps
    weight = conv_weight[0]
    stages = [Stage(plan, p) for p in range(parts)]

    def partner(array, k):
        return lax.ppermute(array, "ctx", [(i, i ^ k) for i in range(devices)])

    def shifted(array, k):
        route = [
            (((p + 1) % sections) * devices + i, p * devices + (i ^ k))
            for p in range(sections)
            for i in range(devices)
        ]
        return lax.ppermute(array, ("pipe", "ctx"), route)

    conv = plan.all + maps
    away = pl.BlockSpec(memory_space=pl.ANY)
    packed = pl.pallas_call(
        functools.partial(pack_kernel, plan),
        out_shape=[struct(BLOCK, conv + LANES, dtype=BF16)] * half + [struct(16, conv, dtype=BF16)] * half,
        in_specs=[away] * 3,
        scratch_shapes=[pltpu.SemaphoreType.DMA((half * (4 + BLOCK // heads),))],
    )(features[0], state_maps[0], step_raw[0].T)
    cuts = pl.pallas_call(
        functools.partial(cut_kernel, plan),
        out_shape=[struct(BLOCK, plan.all, dtype=BF16)] * half,
        in_specs=[away],
        scratch_shapes=[pltpu.SemaphoreType.DMA((half,))],
    )(output_grads[0])
    pays = [packed[0]] + [partner(packed[k], k) for k in range(1, half)]
    edges = [lax.ppermute(e, "ctx", [(half - 1, half + k)]) for k, e in enumerate(packed[half:])]
    grads = [shifted(cuts[k], k) for k in range(half)]
    big = 2 * tokens * state * width
    done = []
    small = pltpu.VMEM((8, LANES), F32)
    x_conv, dsilu, states, x_maps, d_maps, steps, sigmoids, cums = call(
        forward_kernel,
        plan,
        [near(tokens, plan.all), near(tokens, plan.all), near(tokens + BLOCK, plan.all), near(tokens, maps),
         near(tokens, maps)] + [near(tokens, LANES)] * 3,
        [pltpu.VMEM((tokens + PAD, conv), F32), pltpu.VMEM((tokens, LANES), F32), small],
        flops=6 * big * parts,
    )(*pays, *edges, weight, conv_bias, decay_log, step_bias)
    for stage in stages:
        first = stage.first
        args = [*grads, x_maps, cums, states, x_conv, dsilu, d_maps, steps, skip_gain]
        outs = [near(tokens, width, dtype=BF16), near(tokens + BLOCK, width), struct(BLOCK + 16, width)]
        if not first:
            args += [top]
        if not stage.last:
            outs += [near(16, state + BLOCK)]
        gy, back, send, *rest = call(gradient_kernel, stage, outs, [small], flops=3 * big)(*args)
        if rest:
            top = rest[0]
        got = partner(send, half)
        outs = [near(tokens, width), near(tokens, width), near(tokens, BLOCK)]
        args = [x_conv, x_maps, steps, cums, gy] + ([] if first else [scores])
        y_within, d_within, scores = call(within_kernel, stage, outs, flops=30 * big)(*args)
        done.append((got, x_conv, x_maps, dsilu, steps, sigmoids, cums, states, back, gy, y_within, d_within))
    feature_parts = []
    for stage, arrays in zip(stages, done):
        first, last = stage.first, stage.last
        conv = width + maps if last else width
        out = width + LANES if last else width
        args = [*arrays, weight, decay_log, skip_gain]
        outs = [struct(BLOCK, out, dtype=BF16)] * half
        scratch = [small, pltpu.VMEM((BLOCK + PAD, conv), F32), pltpu.VMEM((PAD, conv), F32), small,
                   pltpu.VMEM((tokens, out), BF16), pltpu.VMEM((max(8, plan.blocks), LANES), F32)]
        if last:
            args += [scores, d_maps]
            outs += [struct(BLOCK, maps)] * half
            scratch += [pltpu.VMEM((tokens, maps), F32)]
        else:
            outs += [near(tokens, maps), near(16, state), near(tokens, LANES)]
        if not first:
            args += carried
        result = call(final_kernel, stage, outs, scratch, flops=12 * big)(*args)
        feature_parts += [result[0]] + [partner(result[k], k) for k in range(1, half)]
        carried = result[half:]
    map_parts = [carried[0]] + [partner(carried[k], k) for k in range(1, half)]
    feature_grads, map_grads, step_grads = call(
        owner_kernel,
        plan,
        [struct(BLOCK, plan.inner, dtype=BF16), struct(BLOCK, maps, dtype=BF16), struct(heads, BLOCK, dtype=BF16)],
    )(*feature_parts, *map_parts)
    return (feature_grads[None], map_grads[None], step_grads.T[None])


def solution(mesh):
    return jax.shard_map(
        functools.partial(per_device, mesh.shape["pipe"], mesh.shape["ctx"]),
        mesh=mesh,
        in_specs=(
            P("pipe", "ctx", None),
            P("pipe", "ctx", None),
            P("pipe", "ctx", None),
            P("pipe", None, None),
            P("pipe", None),
            P("pipe", None),
            P("pipe", None),
            P("pipe", None),
            P("pipe", "ctx", None),
        ),
        out_specs=(P("pipe", "ctx", None), P("pipe", "ctx", None), P("pipe", "ctx", None)),
        check_vma=False,
    )
```

```python
import functools

import jax
import jax.numpy as jnp
from jax import lax
from jax.experimental import pallas as pl
from jax.experimental.pallas import tpu as pltpu
from jax.sharding import PartitionSpec as P

BLOCK = 128
LANES = 128
HEAD = 64
PAD = 8
PARTS = 2
F32 = jnp.float32
BF16 = jnp.bfloat16
NEG = -1e30
NN = (((1,), (0,)), ((), ()))
NT = (((1,), (1,)), ((), ()))
TN = (((0,), (0,)), ((), ()))


def mm(a, b, dims=NN):
    return lax.dot_general(a, b, dims, preferred_element_type=F32)


def split(a):
    high = a.astype(BF16)
    return high, (a - high.astype(F32)).astype(BF16)


def mm3(a, b, dims=NN):
    (ah, al), (bh, bl) = a, b
    return mm(ah, bh, dims) + (mm(ah, bl, dims) + mm(al, bh, dims))


def iota(shape, axis):
    return lax.broadcasted_iota(jnp.int32, shape, axis)


def wide(a):
    high, low = a
    return jnp.concatenate([high, low], axis=1), high


def mm_wide(a, b):
    (both, high), (bh, bl) = a, b
    return mm(both, jnp.concatenate([bh, bh], axis=0)) + mm(high, bl)


def mm_over(a, b):
    (ah, al), (bh, bl) = a, b
    n = bh.shape[0]
    both = mm(ah, jnp.concatenate([bh, bl], axis=0), NT)
    return both[:, :n] + (both[:, n:] + mm(al, bh, NT))


def expand(values, head, count=LANES):
    rows = values.shape[0]
    left = iota((rows, LANES), 1) < HEAD
    tiles = []
    for h in range(head, head + count // HEAD, 2):
        first = jnp.broadcast_to(values[:, h : h + 1], (rows, LANES))
        second = jnp.broadcast_to(values[:, h + 1 : h + 2], (rows, LANES))
        tiles.append(jnp.where(left, first, second))
    return tiles[0] if len(tiles) == 1 else jnp.concatenate(tiles, axis=1)


def onto_heads(head, count):
    shape = (count, LANES)
    return (iota(shape, 1) == head + iota(shape, 0) // HEAD).astype(F32).astype(BF16)


def head_sums(values, onto):
    rows = values[0].shape[0]
    sums = mm(jnp.concatenate([part for value in values for part in split(value)], axis=0), onto)
    return [sums[2 * n * rows : (2 * n + 1) * rows] + sums[(2 * n + 1) * rows : (2 * n + 2) * rows] for n in range(len(values))]


class Plan:
    def __init__(self, devices, inner, state, heads):
        self.half = devices // 2
        self.inner = inner
        self.state = state
        self.maps = 2 * state
        self.heads = heads // self.half
        self.all = inner // self.half
        self.parts = PARTS
        self.width = self.all // PARTS
        self.tile = 2 * LANES if self.width % (2 * LANES) == 0 else LANES
        self.tiles = self.width // self.tile
        self.blocks = self.half
        self.tokens = self.half * BLOCK


class Stage:
    def __init__(self, plan, part):
        self.plan = plan
        self.part = part
        self.first = part == 0
        self.last = part == plan.parts - 1
        self.head = part * plan.width // HEAD
        self.start = part * plan.width

    def steps(self):
        tile = self.plan.tile
        for i in range(self.plan.tiles):
            lane = self.start + i * tile
            yield slice(i * tile, (i + 1) * tile), slice(lane, lane + tile), lane // HEAD


def place(plan):
    rank = lax.axis_index("ctx")
    return lax.rem(rank, plan.half), lax.div(rank, plan.half)


def call(kernel, stage, out_shape, scratch=(), work=1.0, **more):
    return pl.pallas_call(
        functools.partial(kernel, stage),
        out_shape=out_shape,
        scratch_shapes=list(scratch),
        compiler_params=pltpu.CompilerParams(vmem_limit_bytes=32 * 1024 * 1024),
        cost_estimate=pl.CostEstimate(flops=int(work * 1.15e9), transcendentals=0, bytes_accessed=1 << 20),
        **more,
    )


def struct(*shape, dtype=F32):
    return jax.ShapeDtypeStruct(shape, dtype)


def near(*shape, dtype=F32):
    return pltpu.VMEM(shape, dtype)


def head_rows(plan, prm, refs, own):
    prm[...] = jnp.zeros_like(prm)
    for row, values in enumerate(refs):
        prm[row : row + 1, 0 : values.shape[1]] = values
    local = pltpu.roll(prm[...], lax.rem(LANES - own * plan.heads, LANES), 1)
    return [local[row : row + 1, :] for row in range(len(refs))]


def run_copies(pairs, sems):
    copies = [pltpu.make_async_copy(source, target, sems.at[n]) for n, (source, target) in enumerate(pairs)]
    for copy in copies:
        copy.start()
    for copy in copies:
        copy.wait()


def pack_kernel(plan, f_ref, m_ref, s_ref, *refs):
    pays, edges, sems = refs[: plan.half], refs[plan.half : -1], refs[-1]
    own, _ = place(plan)
    whole, heads = plan.all, s_ref.shape[0]
    pairs = []
    for k in range(plan.half):
        start = pl.multiple_of(jnp.bitwise_xor(own, k) * whole, LANES)
        pairs.append((f_ref.at[:, pl.ds(start, whole)], pays[k].at[:, pl.ds(0, whole)]))
        pairs.append((m_ref, pays[k].at[:, pl.ds(whole, plan.maps)]))
        for row in range(0, BLOCK, heads):
            pairs.append((s_ref, pays[k].at[pl.ds(row, heads), pl.ds(whole + plan.maps, LANES)]))
        tail = pl.ds(BLOCK - 16, 16)
        pairs.append((f_ref.at[tail, pl.ds(k * whole, whole)], edges[k].at[:, pl.ds(0, whole)]))
        pairs.append((m_ref.at[tail, :], edges[k].at[:, pl.ds(whole, plan.maps)]))
    run_copies(pairs, sems)


def cut_kernel(plan, o_ref, *refs):
    own, _ = place(plan)
    pairs = []
    for k in range(plan.half):
        start = pl.multiple_of(jnp.bitwise_xor(own, k) * plan.all, LANES)
        pairs.append((o_ref.at[:, pl.ds(start, plan.all)], refs[k]))
    run_copies(pairs, refs[-1])


def forward_kernel(plan, *refs):
    half, width, maps, tile = plan.half, plan.all, plan.maps, plan.tile
    conv = width + maps
    pays, edges = refs[:half], refs[half : 2 * half]
    (cw_ref, cb_ref, dl_ref, sb_ref, x_ref, ds_ref, el_ref, xm_ref, dm_ref, st_ref, sg_ref, cum_ref,
     raw, sraw, prm) = refs[2 * half :]
    own, _ = place(plan)
    heads = dl_ref.shape[1]
    halo = edges[0][...].astype(F32)
    for k in range(1, half):
        halo = halo + edges[k][...].astype(F32)
    raw[0:PAD, :] = halo[16 - PAD :, :]
    sraw[...] = jnp.zeros_like(sraw)
    for k in range(half):
        block = jnp.bitwise_xor(own, k) * BLOCK
        raw[pl.ds(pl.multiple_of(block + PAD, 8), BLOCK), :] = pays[k][:, :conv].astype(F32)
        sraw[pl.ds(pl.multiple_of(block, 8), BLOCK), 0:heads] = pays[k][0:heads, conv:].astype(F32).T
    rates, offsets = head_rows(plan, prm, [-jnp.exp(dl_ref[...]), sb_ref[...]], own)
    shift = lax.rem(LANES - own * plan.heads, LANES)
    lower = (iota((BLOCK, BLOCK), 0) >= iota((BLOCK, BLOCK), 1)).astype(F32)
    el_ref[0:BLOCK, :] = jnp.zeros((BLOCK, width), F32)

    def body(b, carry):
        row = pl.multiple_of(b * BLOCK, BLOCK)
        rows = pl.ds(row, BLOCK)
        for c in range(0, conv, tile):
            window = raw[pl.ds(row, BLOCK + PAD), c : c + tile]
            if c < width:
                cols = pl.ds(pl.multiple_of(own * width + c, LANES), tile)
                to_x, to_d, at = x_ref, ds_ref, c
            else:
                cols = slice(plan.inner + c - width, plan.inner + c - width + tile)
                to_x, to_d, at = xm_ref, dm_ref, c - width
            weight = cw_ref[:, cols]
            v = jnp.broadcast_to(cb_ref[:, cols], (BLOCK, tile))
            for k in range(weight.shape[0]):
                v = v + weight[k : k + 1, :] * window[PAD - k : PAD - k + BLOCK, :]
            s = 1.0 / (1.0 + jnp.exp(-v))
            to_x[rows, at : at + tile] = v * s
            to_d[rows, at : at + tile] = s * (1.0 + v * (1.0 - s))
        a = pltpu.roll(sraw[rows, :], shift, 1) + offsets
        e = jnp.exp(-jnp.abs(a))
        u = 1.0 + e
        d = u - 1.0
        step = jnp.maximum(a, 0.0) + jnp.where(d == 0.0, e, jnp.log(u) * (e / jnp.where(d == 0.0, 1.0, d)))
        st_ref[rows, :] = step
        sg_ref[rows, :] = jnp.where(a >= 0.0, 1.0, e) / u
        cum = lax.dot_general(lower, step * rates, NN, precision=lax.Precision.HIGHEST, preferred_element_type=F32)
        cum_ref[rows, :] = cum
        total = cum[BLOCK - 1 :, :]
        weighted = jnp.exp(total - cum) * step
        decay = jnp.exp(total)
        bt = wide(split(xm_ref[rows, : plan.state].T))
        nxt = pl.ds(pl.multiple_of(row + BLOCK, BLOCK), BLOCK)
        for c in range(0, width, tile):
            at, head = slice(c, c + tile), c // HEAD
            wx = split(x_ref[rows, at] * expand(weighted, head, tile))
            el_ref[nxt, at] = el_ref[rows, at] * expand(decay, head, tile) + mm_wide(bt, wx)
        return carry

    lax.fori_loop(0, plan.blocks, body, 0)


def gradient_kernel(stage, *refs):
    plan, first, last = stage.plan, stage.first, stage.last
    half, width, blocks, tile, state = plan.half, plan.width, plan.blocks, plan.tile, plan.state
    if first:
        grads, refs = refs[:half], refs[half:]
    else:
        gy_ref, top_old, after, refs = refs[0], refs[1], refs[2], refs[3:]
    xm_ref, cum_ref, el_ref, x_ref, ds_ref, dm_ref, st_ref, sk_ref, gl_ref, send_ref = refs[:10]
    if not last:
        top_ref = refs[10]
    if first:
        gy_ref = refs[11]
    prm = refs[-1]
    own, late = place(plan)
    if first:
        for k in range(half):
            block = pl.multiple_of(jnp.bitwise_xor(own, k) * BLOCK, BLOCK)
            gy_ref[pl.ds(block, BLOCK), :] = grads[k][...]
    gl_ref[blocks * BLOCK :, :] = jnp.zeros((BLOCK, width), F32)

    def body(t, carry):
        row = pl.multiple_of((blocks - 1 - t) * BLOCK, BLOCK)
        rows = pl.ds(row, BLOCK)
        nxt = pl.ds(pl.multiple_of(row + BLOCK, BLOCK), BLOCK)
        cum = cum_ref[rows, :]
        grown, decay = jnp.exp(cum), jnp.exp(cum[BLOCK - 1 :, :])
        ct = wide(split(xm_ref[rows, plan.state :].T))
        for at, among, head in stage.steps():
            ge = split(gy_ref[rows, among].astype(F32) * expand(grown, head, tile))
            gl_ref[rows, at] = gl_ref[nxt, at] * expand(decay, head, tile) + mm_wide(ct, ge)
        return carry

    lax.fori_loop(0, blocks, body, 0)

    @pl.when(late == 0)
    def _():
        send_ref[0:BLOCK, :] = el_ref[blocks * BLOCK :, stage.start : stage.start + width]
        send_ref[BLOCK:, :] = jnp.zeros((16, width), F32)
        if not last:
            top_ref[...] = jnp.zeros_like(top_ref)

    @pl.when(late != 0)
    def _():
        send_ref[0:BLOCK, :] = gl_ref[0:BLOCK, :]
        (skips,) = head_rows(plan, prm, [sk_ref[...]], own)
        top = slice(0, 16)
        edge = send_ref.at[BLOCK : BLOCK + 16, :]
        cum, step, cum_t = cum_ref[top, :], st_ref[top, :], cum_ref[0:BLOCK, :].T
        shrunk, grown = jnp.exp(cum_ref[BLOCK - 1 : BLOCK, :] - cum), jnp.exp(cum)
        top_b, first_c = split(xm_ref[top, :state]), split(xm_ref[0:BLOCK, state:])
        wide_b = wide(top_b)
        scores = mm3(top_b, first_c, NT)
        causal = iota((16, BLOCK), 0) <= iota((16, BLOCK), 1)
        if first:
            d_b, dsc = jnp.zeros((16, state), F32), jnp.zeros((16, BLOCK), F32)
        else:
            d_b, dsc = top_old[:, :state], top_old[:, state:]
        zero, blank = jnp.zeros((BLOCK, LANES), BF16), jnp.zeros((16, LANES), BF16)
        left, left_top = iota((BLOCK, LANES), 1) < HEAD, iota((16, LANES), 1) < HEAD
        for i in range(width // LANES):
            at, head = slice(i * LANES, (i + 1) * LANES), stage.head + 2 * i
            among = slice(head * HEAD, head * HEAD + LANES)
            step_x, shrunk_x = expand(step, head), expand(shrunk, head)
            xs = x_ref[top, among] * step_x
            gy = gy_ref[0:BLOCK, among]
            decays, mh, ml = [], [], []
            for h in (head, head + 1):
                spread = cum_t[h : h + 1, :] - jnp.broadcast_to(cum[:, h : h + 1], (16, BLOCK))
                decay = jnp.exp(jnp.where(causal, spread, NEG))
                high, low = split(scores * decay)
                decays.append(decay)
                mh.append(high)
                ml.append(low)
            gs = jnp.concatenate([jnp.where(left, gy, zero), jnp.where(left, zero, gy)], axis=0)
            dxs = mm(jnp.concatenate(mh, axis=1), gs) + mm(jnp.concatenate(ml, axis=1), gs)
            xh, xl = split(xs)
            rows = [jnp.where(left_top, xh, blank), jnp.where(left_top, blank, xh)]
            rows += [jnp.where(left_top, xl, blank), jnp.where(left_top, blank, xl)]
            dm = mm(jnp.concatenate(rows, axis=0), gy, NT)
            dsc = dsc + (dm[0:16] + dm[32:48]) * decays[0] + (dm[16:32] + dm[48:64]) * decays[1]
            leaving = split(gl_ref[BLOCK : 2 * BLOCK, at])
            dxs = dxs + shrunk_x * mm_wide(wide_b, leaving)
            d_b = d_b + mm_over(split(xs * shrunk_x), leaving)
            top_gy = gy[0:16].astype(F32)
            edge[0:PAD, at] = ((dxs * step_x + expand(skips, head) * top_gy) * ds_ref[top, among])[0:PAD]
            edge[PAD:, at] = (top_gy * expand(grown, head))[0:PAD]
        if last:
            parts = split(dsc)
            d_b = (d_b + mm3(parts, first_c)) * dm_ref[top, :state]
            d_c = mm3(parts, top_b, TN)
            silu_c = dm_ref[top, state:]
            edge[3:6, 0:state] = d_b[0:3]
            edge[6:8, 0:state] = silu_c[0:2]
            edge[11:14, 0:state] = d_c[0:3]
            edge[14:15, 0:state] = silu_c[2:3]
        else:
            top_ref[:, :state] = d_b
            top_ref[:, state:] = dsc


def within_kernel(stage, *refs):
    plan, first = stage.plan, stage.first
    x_ref, xm_ref, st_ref, cum_ref, gy_ref = refs[:5]
    refs = refs[5:]
    if not first:
        dsc_old, refs = refs[0], refs[1:]
    yw_ref, dw_ref, dsc_ref = refs
    width, state = plan.width, plan.state
    causal = iota((BLOCK, BLOCK), 0) >= iota((BLOCK, BLOCK), 1)
    left = iota((BLOCK, LANES), 1) < HEAD

    def body(b, carry):
        rows = pl.ds(pl.multiple_of(b * BLOCK, BLOCK), BLOCK)
        cum = cum_ref[rows, :]
        cum_t = cum.T
        step = st_ref[rows, :]
        b_maps = split(xm_ref[rows, :state])
        c_maps = split(xm_ref[rows, state:])
        scores = mm3(c_maps, b_maps, NT)
        total = jnp.zeros((BLOCK, BLOCK), F32) if first else dsc_old[rows, :]
        zero = jnp.zeros((BLOCK, LANES), BF16)
        for i in range(width // LANES):
            at, head = slice(i * LANES, (i + 1) * LANES), stage.head + 2 * i
            xs = x_ref[rows, head * HEAD : head * HEAD + LANES] * expand(step, head)
            xh, xl = split(xs)
            gy = gy_ref[rows, head * HEAD : head * HEAD + LANES]
            g0, g1 = jnp.where(left, gy, zero), jnp.where(left, zero, gy)
            decays, mh, ml = [], [], []
            for h in (head, head + 1):
                spread = jnp.broadcast_to(cum[:, h : h + 1], (BLOCK, BLOCK)) - cum_t[h : h + 1, :]
                decay = jnp.exp(jnp.where(causal, spread, NEG))
                high, low = split(scores * decay)
                decays.append(decay)
                mh.append(high)
                ml.append(low)
            both = jnp.concatenate(
                [
                    jnp.concatenate([jnp.where(left, xh, zero), jnp.where(left, xl, zero)], axis=1),
                    jnp.concatenate([jnp.where(left, zero, xh), jnp.where(left, zero, xl)], axis=1),
                ],
                axis=0,
            )
            high = mm(jnp.concatenate(mh, axis=1), both)
            low = mm(jnp.concatenate(ml, axis=1), both[:, :LANES])
            yw_ref[rows, at] = high[:, :LANES] + (high[:, LANES:] + low)
            gs = jnp.concatenate([g0, g1], axis=0)
            dw_ref[rows, at] = mm(jnp.concatenate(mh, axis=0), gs, TN) + mm(jnp.concatenate(ml, axis=0), gs, TN)
            dm = mm(jnp.concatenate([gs, gs], axis=1), jnp.concatenate([xh, xl], axis=1), NT)
            total = total + dm[:BLOCK] * decays[0] + dm[BLOCK:] * decays[1]
        dsc_ref[rows, :] = total
        return carry

    lax.fori_loop(0, plan.blocks, body, 0)


def final_kernel(stage, *refs):
    plan, first, last = stage.plan, stage.first, stage.last
    half, width, blocks, state, tile, maps = plan.half, plan.width, plan.blocks, plan.state, plan.tile, plan.maps
    (both_ref, x_ref, xm_ref, ds_ref, st_ref, sg_ref, cum_ref, el_ref, gl_ref, gy_ref, yw_ref, dw_ref,
     cw_ref, dl_ref, sk_ref) = refs[:15]
    refs = refs[15:]
    got_ref, edge_ref = both_ref.at[0:BLOCK, :], both_ref.at[BLOCK : BLOCK + 16, :]
    if last:
        dsc_ref, dm_ref, refs = refs[0], refs[1], refs[2:]
    if not first:
        bc_old, ac_old, dst_old, refs = refs[0], refs[1], refs[2], refs[3:]
    outs, refs = refs[:half], refs[half:]
    if not last:
        bc_ref, ac_ref, dst_ref, refs = refs[0], refs[1], refs[2], refs[3:]
    prm, dz, nxt_dz, carry_ref, o_sc, lc_sc = refs[:6]
    conv = width + maps if last else width
    own, late = place(plan)
    is_late = late.astype(F32)
    rates, skips = head_rows(plan, prm, [-jnp.exp(dl_ref[...]), sk_ref[...]], own)
    upper = (iota((BLOCK, BLOCK), 0) <= iota((BLOCK, BLOCK), 1)).astype(F32).astype(BF16)
    after_c = jnp.zeros((16, state), F32) if first else ac_old[...]
    for at, among, _ in stage.steps():
        after_c = after_c + mm_over(split(edge_ref[:, at]), split(el_ref[blocks * BLOCK :, among]))
    early = iota((PAD, LANES), 0) * 0 + late == 0
    for c in range(0, width, LANES):
        nxt_dz[:, c : c + LANES] = jnp.where(early, edge_ref[0:PAD, c : c + LANES], 0.0)
    if last:
        rest = jnp.zeros((PAD - 3, state), F32)
        nxt_dz[:, width : width + state] = jnp.where(early, jnp.concatenate([edge_ref[3:6, 0:state], rest], axis=0), 0.0)
        silu_c = jnp.concatenate([edge_ref[6:8, 0:state], edge_ref[14:15, 0:state]], axis=0)
        after_c = (after_c[PAD : PAD + 3] + edge_ref[11:14, 0:state]) * silu_c
        nxt_dz[:, width + state :] = jnp.where(early, jnp.concatenate([after_c, rest], axis=0), 0.0)
    else:
        ac_ref[...] = after_c
    lc_sc[...] = jnp.zeros_like(lc_sc)
    for b in range(1, blocks):
        lc_sc[b : b + 1, :] = lc_sc[b - 1 : b, :] + cum_ref[b * BLOCK - 1 : b * BLOCK, :]
    whole = lc_sc[blocks - 1 : blocks, :] + cum_ref[blocks * BLOCK - 1 :, :]
    ends = jnp.zeros((8, LANES), F32)
    ontos = {head: onto_heads(head, tile) for _, _, head in stage.steps()}
    for at, among, head in stage.steps():
        product = jnp.sum(got_ref[:, at] * el_ref[blocks * BLOCK :, among], axis=0, keepdims=True)
        ends = ends + head_sums([jnp.broadcast_to(product, (16, tile))], ontos[head])[0][0:8]
    carry_ref[...] = ends * (1.0 - is_late)

    def body(t, carry):
        b = blocks - 1 - t
        row = pl.multiple_of(b * BLOCK, BLOCK)
        rows = pl.ds(row, BLOCK)
        nxt = pl.ds(pl.multiple_of(row + BLOCK, BLOCK), BLOCK)
        cum, step = cum_ref[rows, :], st_ref[rows, :]
        total = cum[BLOCK - 1 :, :]
        grown, shrunk = jnp.exp(cum), jnp.exp(total - cum)
        before = lc_sc[pl.ds(b, 1), :]
        from_first = jnp.exp(before) * is_late
        to_last = jnp.exp(whole - before - total) * (1.0 - is_late)
        b_maps, c_maps = split(xm_ref[rows, :state]), split(xm_ref[rows, state:])
        b_wide, c_wide = wide(b_maps), wide(c_maps)
        if first:
            d_b = d_c = jnp.zeros((BLOCK, state), F32)
        else:
            d_b, d_c = bc_old[rows, :state], bc_old[rows, state:]
        if last:
            dsc = dsc_ref[rows, :]
            d_c = d_c + mm3(split(dsc), b_maps)
            d_b = d_b + mm3(split(dsc.T), c_maps)
        sums = jnp.zeros((BLOCK, LANES), F32)
        direct = jnp.zeros((BLOCK, LANES), F32)
        for at, among, head in stage.steps():
            got = got_ref[:, at]
            entering = split(el_ref[rows, among] + got * expand(from_first, head, tile))
            leaving = split(gl_ref[nxt, at] + got * expand(to_last, head, tile))
            x = x_ref[rows, among]
            step_x, shrunk_x, grown_x = expand(step, head, tile), expand(shrunk, head, tile), expand(grown, head, tile)
            xs = x * step_x
            gy = gy_ref[rows, among].astype(F32)
            y = yw_ref[rows, at] + grown_x * mm_wide(c_wide, entering)
            dxs = dw_ref[rows, at] + shrunk_x * mm_wide(b_wide, leaving)
            d_c = d_c + mm_over(split(gy * grown_x), entering)
            d_b = d_b + mm_over(split(xs * shrunk_x), leaving)
            both = head_sums([gy * y - xs * dxs, dxs * x], ontos[head])
            sums, direct = sums + both[0], direct + both[1]
            dz[0:BLOCK, at] = (dxs * step_x + expand(skips, head, tile) * gy) * ds_ref[rows, among]
        sums_high, sums_low = split(sums)
        d_log = mm(upper, sums_high) + mm(upper, sums_low) + carry_ref[0:1, :]
        carry_ref[...] = jnp.broadcast_to(d_log[0:1, :], (8, LANES))
        d_step = (d_log * rates + direct) * sg_ref[rows, :]
        lane = iota((BLOCK, LANES), 1)
        d_step = jnp.where((lane >= stage.head) & (lane < stage.head + width // HEAD), d_step, 0.0)
        if not first:
            d_step = d_step + dst_old[rows, :]
        if last:
            o_sc[rows, width : width + LANES] = d_step.astype(BF16)
            dz[0:BLOCK, width : width + state] = d_b * dm_ref[rows, :state]
            dz[0:BLOCK, width + state :] = d_c * dm_ref[rows, state:]
        else:
            dst_ref[rows, :] = d_step
            bc_ref[rows, :state] = d_b
            bc_ref[rows, state:] = d_c
        dz[BLOCK:, :] = nxt_dz[...]
        for c in range(0, conv, LANES):
            window = dz[:, c : c + LANES]
            if c < width:
                cols = pl.ds(pl.multiple_of(own * plan.all + stage.start + c, LANES), LANES)
            else:
                cols = slice(plan.inner + c - width, plan.inner + c - width + LANES)
            weight = cw_ref[:, cols]
            grad = weight[0:1, :] * window[0:BLOCK, :]
            for k in range(1, weight.shape[0]):
                grad = grad + weight[k : k + 1, :] * window[k : k + BLOCK, :]
            if c < width:
                o_sc[rows, c : c + LANES] = grad.astype(BF16)
            else:
                high, low = split(grad)
                o_sc[rows, LANES + c : 2 * LANES + c] = high
                o_sc[rows, LANES + maps + c : 2 * LANES + maps + c] = low
        nxt_dz[...] = dz[0:PAD, :]
        return carry

    lax.fori_loop(0, blocks, body, 0)
    for k in range(half):
        rows = pl.ds(pl.multiple_of(jnp.bitwise_xor(own, k) * BLOCK, BLOCK), BLOCK)
        outs[k][...] = o_sc[rows, :]


def owner_kernel(stage, *refs):
    plan, last, maps = stage.plan, stage.last, stage.plan.maps
    half, width = plan.half, plan.width
    outs, refs = refs[:half], refs[half:]
    if stage.part:
        refs = refs[1:]
    f_ref = refs[0]
    own, _ = place(plan)
    pairs = []
    for k in range(half):
        start = pl.multiple_of(jnp.bitwise_xor(own, k) * plan.all + stage.start, LANES)
        pairs.append((outs[k].at[:, pl.ds(0, width)], f_ref.at[:, pl.ds(start, width)]))
    copies = [pltpu.make_async_copy(source, target, refs[-1].at[n]) for n, (source, target) in enumerate(pairs)]
    for copy in copies:
        copy.start()
    if last:
        m_ref, s_ref = refs[1:3]
        total = jnp.zeros((BLOCK, maps), F32)
        steps = jnp.zeros((BLOCK, LANES), F32)
        for k in range(half):
            part, end = jnp.bitwise_xor(own, k), outs[k]
            steps = steps + pltpu.roll(end[:, width : width + LANES].astype(F32), part * plan.heads, 1)
            high, low = end[:, width + LANES : width + LANES + maps], end[:, width + LANES + maps :]
            total = total + (high.astype(F32) + low.astype(F32))
        m_ref[...] = total.astype(BF16)
        s_ref[...] = steps.T[: s_ref.shape[0]].astype(BF16)
    for copy in copies:
        copy.wait()


def per_device(sections, devices, features, state_maps, step_raw, conv_weight, conv_bias, decay_log, step_bias, skip_gain, output_grads):
    state = state_maps.shape[2] // 2
    heads = decay_log.shape[1]
    plan = Plan(devices, features.shape[2], state, heads)
    half, width, tokens, parts, maps = plan.half, plan.width, plan.tokens, plan.parts, plan.maps
    weight = conv_weight[0]
    stages = [Stage(plan, p) for p in range(parts)]

    def partner(array, k):
        return lax.ppermute(array, "ctx", [(i, i ^ k) for i in range(devices)])

    def shifted(array, k):
        route = [
            (((p + 1) % sections) * devices + i, p * devices + (i ^ k))
            for p in range(sections)
            for i in range(devices)
        ]
        return lax.ppermute(array, ("pipe", "ctx"), route)

    conv = plan.all + maps
    away = pl.BlockSpec(memory_space=pl.ANY)
    far = pl.BlockSpec(memory_space=pltpu.HBM)

    def hold(array):
        return pltpu.with_memory_space_constraint(array, pltpu.HBM)

    packed = call(
        pack_kernel,
        plan,
        [struct(BLOCK, conv + LANES, dtype=BF16)] * half + [struct(16, conv, dtype=BF16)] * half,
        [pltpu.SemaphoreType.DMA((half * (4 + BLOCK // heads),))],
        work=3.0,
        in_specs=[far] * 3,
    )(hold(features[0]), hold(state_maps[0]), hold(step_raw[0].T))
    cuts = call(
        cut_kernel,
        plan,
        [struct(BLOCK, plan.all, dtype=BF16)] * half,
        [pltpu.SemaphoreType.DMA((half,))],
        work=2.2,
        in_specs=[far],
    )(hold(output_grads[0]))
    pays = [packed[0]] + [partner(packed[k], k) for k in range(1, half)]
    edges = [lax.ppermute(e, "ctx", [(half - 1, half + k)]) for k, e in enumerate(packed[half:])]
    grads = [shifted(cuts[k], k) for k in range(half)]
    done = []
    small = pltpu.VMEM((8, LANES), F32)
    x_conv, dsilu, states, x_maps, d_maps, steps, sigmoids, cums = call(
        forward_kernel,
        plan,
        [near(tokens, plan.all), near(tokens, plan.all), near(tokens + BLOCK, plan.all), near(tokens, maps),
         near(tokens, maps)] + [near(tokens, LANES)] * 3,
        [pltpu.VMEM((tokens + PAD, conv), F32), pltpu.VMEM((tokens, LANES), F32), small],
        work=5.0,
    )(*pays, *edges, weight, conv_bias, decay_log, step_bias)
    for stage in stages:
        first = stage.first
        args = [] if first else [gy, top, scores]
        args += [*(grads if first else ()), x_maps, cums, states, x_conv, dsilu, d_maps, steps, skip_gain]
        outs = [near(tokens + BLOCK, width), struct(BLOCK + 16, width)]
        if not stage.last:
            outs += [near(16, state + BLOCK)]
        if first:
            outs += [near(tokens, plan.all, dtype=BF16)]
        back, send, *rest = call(gradient_kernel, stage, outs, [small], work=2.1)(*args)
        if first:
            top, gy = rest
            within = []
            for other in stages:
                outs = [near(tokens, width), near(tokens, width), near(tokens, BLOCK)]
                args = [x_conv, x_maps, steps, cums, gy] + ([] if other.first else [scores])
                y_within, d_within, scores = call(within_kernel, other, outs, work=2.0)(*args)
                within.append((y_within, d_within))
        got = partner(send, half)
        done.append((got, x_conv, x_maps, dsilu, steps, sigmoids, cums, states, back, gy, *within[stage.part]))
    feature_parts = []
    for stage, arrays in zip(stages, done):
        first, last = stage.first, stage.last
        conv = width + maps if last else width
        out = width + LANES + 2 * maps if last else width
        args = [*arrays, weight, decay_log, skip_gain]
        outs = [struct(BLOCK, out, dtype=BF16)] * half
        scratch = [small, pltpu.VMEM((BLOCK + PAD, conv), F32), pltpu.VMEM((PAD, conv), F32), small,
                   pltpu.VMEM((tokens, out), BF16), pltpu.VMEM((max(8, plan.blocks), LANES), F32)]
        if last:
            args += [scores, d_maps]
        else:
            outs += [near(tokens, maps), near(16, state), near(tokens, LANES)]
        if not first:
            args += carried
        result = call(final_kernel, stage, outs, scratch, work=5.8)(*args)
        feature_parts += [result[0]] + [partner(result[k], k) for k in range(1, half)]
        carried = result[half:]
    inside = pl.BlockSpec(memory_space=pltpu.VMEM)
    for stage in stages:
        more = [feature_grads] if stage.part else []
        outs = [struct(BLOCK, plan.inner, dtype=BF16)]
        if stage.last:
            outs += [struct(BLOCK, maps, dtype=BF16), struct(heads, BLOCK, dtype=BF16)]
        feature_grads, *others = call(
            owner_kernel,
            stage,
            outs,
            [pltpu.SemaphoreType.DMA((half,))],
            work=2.0,
            in_specs=[inside] * half + [away] * len(more),
            out_specs=[away] + [inside] * (len(outs) - 1),
            input_output_aliases={half: 0} if more else {},
        )(*feature_parts[stage.part * half : (stage.part + 1) * half], *more)
    map_grads, step_grads = others
    return (feature_grads[None], map_grads[None], step_grads.T[None])


def solution(mesh):
    return jax.shard_map(
        functools.partial(per_device, mesh.shape["pipe"], mesh.shape["ctx"]),
        mesh=mesh,
        in_specs=(
            P("pipe", "ctx", None),
            P("pipe", "ctx", None),
            P("pipe", "ctx", None),
            P("pipe", None, None),
            P("pipe", None),
            P("pipe", None),
            P("pipe", None),
            P("pipe", None),
            P("pipe", "ctx", None),
        ),
        out_specs=(P("pipe", "ctx", None), P("pipe", "ctx", None), P("pipe", "ctx", None)),
        check_vma=False,
    )
```

```python
import functools

import jax
import jax.numpy as jnp
from jax import lax
from jax.experimental import pallas as pl
from jax.experimental.pallas import tpu as pltpu
from jax.sharding import PartitionSpec as P

BLOCK = 128
LANES = 128
HEAD = 64
PAD = 8
PARTS = 2
UNROLL = 4
F32 = jnp.float32
BF16 = jnp.bfloat16
NEG = -1e30
NN = (((1,), (0,)), ((), ()))
NT = (((1,), (1,)), ((), ()))
TN = (((0,), (0,)), ((), ()))


def mm(a, b, dims=NN):
    return lax.dot_general(a, b, dims, preferred_element_type=F32)


def split(a):
    high = a.astype(BF16)
    return high, (a - high.astype(F32)).astype(BF16)


def mm3(a, b, dims=NN):
    (ah, al), (bh, bl) = a, b
    return mm(ah, bh, dims) + (mm(ah, bl, dims) + mm(al, bh, dims))


def iota(shape, axis):
    return lax.broadcasted_iota(jnp.int32, shape, axis)


def wide(a):
    high, low = a
    return jnp.concatenate([high, low], axis=1), high


def mm_wide(a, b):
    (both, high), (bh, bl) = a, b
    return mm(both, jnp.concatenate([bh, bh], axis=0)) + mm(high, bl)


def mm_over(a, b):
    (ah, al), (bh, bl) = a, b
    n = bh.shape[0]
    both = mm(ah, jnp.concatenate([bh, bl], axis=0), NT)
    return both[:, :n] + (both[:, n:] + mm(al, bh, NT))


def expand(values, head, count=LANES):
    rows = values.shape[0]
    left = iota((rows, LANES), 1) < HEAD
    tiles = []
    for h in range(head, head + count // HEAD, 2):
        first = jnp.broadcast_to(values[:, h : h + 1], (rows, LANES))
        second = jnp.broadcast_to(values[:, h + 1 : h + 2], (rows, LANES))
        tiles.append(jnp.where(left, first, second))
    return tiles[0] if len(tiles) == 1 else jnp.concatenate(tiles, axis=1)


def onto_heads(head, count):
    shape = (count, LANES)
    return (iota(shape, 1) == head + iota(shape, 0) // HEAD).astype(F32).astype(BF16)


def head_sums(values, onto):
    rows = values[0].shape[0]
    sums = mm(jnp.concatenate([part for value in values for part in split(value)], axis=0), onto)
    return [sums[2 * n * rows : (2 * n + 1) * rows] + sums[(2 * n + 1) * rows : (2 * n + 2) * rows] for n in range(len(values))]


class Plan:
    def __init__(self, devices, inner, state, heads):
        self.half = devices // 2
        self.inner = inner
        self.state = state
        self.maps = 2 * state
        self.heads = heads // self.half
        self.all = inner // self.half
        self.parts = PARTS
        self.width = self.all // PARTS
        self.tile = 2 * LANES if self.width % (2 * LANES) == 0 else LANES
        self.tiles = self.width // self.tile
        self.blocks = self.half
        self.tokens = self.half * BLOCK


class Stage:
    def __init__(self, plan, part):
        self.plan = plan
        self.part = part
        self.first = part == 0
        self.last = part == plan.parts - 1
        self.head = part * plan.width // HEAD
        self.start = part * plan.width

    def steps(self):
        tile = self.plan.tile
        for i in range(self.plan.tiles):
            lane = self.start + i * tile
            yield slice(i * tile, (i + 1) * tile), slice(lane, lane + tile), lane // HEAD


def each_block(blocks, body):
    if blocks <= UNROLL:
        for b in range(blocks):
            body(b, 0)
    else:
        lax.fori_loop(0, blocks, body, 0)


def place(plan):
    rank = lax.axis_index("ctx")
    return lax.rem(rank, plan.half), lax.div(rank, plan.half)


def call(kernel, stage, out_shape, scratch=(), work=1.0, **more):
    return pl.pallas_call(
        functools.partial(kernel, stage),
        out_shape=out_shape,
        scratch_shapes=list(scratch),
        compiler_params=pltpu.CompilerParams(vmem_limit_bytes=32 * 1024 * 1024),
        cost_estimate=pl.CostEstimate(flops=int(work * 1.15e9), transcendentals=0, bytes_accessed=1 << 20),
        **more,
    )


def struct(*shape, dtype=F32):
    return jax.ShapeDtypeStruct(shape, dtype)


def near(*shape, dtype=F32):
    return pltpu.VMEM(shape, dtype)


def head_rows(plan, prm, refs, own):
    prm[...] = jnp.zeros_like(prm)
    for row, values in enumerate(refs):
        prm[row : row + 1, 0 : values.shape[1]] = values
    local = pltpu.roll(prm[...], lax.rem(LANES - own * plan.heads, LANES), 1)
    return [local[row : row + 1, :] for row in range(len(refs))]


def run_copies(pairs, sems):
    copies = [pltpu.make_async_copy(source, target, sems.at[n]) for n, (source, target) in enumerate(pairs)]
    for copy in copies:
        copy.start()
    for copy in copies:
        copy.wait()


def pack_kernel(plan, f_ref, m_ref, s_ref, *refs):
    pays, edges, sems = refs[: plan.half], refs[plan.half : -1], refs[-1]
    own, _ = place(plan)
    whole, heads = plan.all, s_ref.shape[0]
    pairs = []
    for k in range(plan.half):
        start = pl.multiple_of(jnp.bitwise_xor(own, k) * whole, LANES)
        pairs.append((f_ref.at[:, pl.ds(start, whole)], pays[k].at[:, pl.ds(0, whole)]))
        pairs.append((m_ref, pays[k].at[:, pl.ds(whole, plan.maps)]))
        for row in range(0, BLOCK, heads):
            pairs.append((s_ref, pays[k].at[pl.ds(row, heads), pl.ds(whole + plan.maps, LANES)]))
        tail = pl.ds(BLOCK - 16, 16)
        pairs.append((f_ref.at[tail, pl.ds(k * whole, whole)], edges[k].at[:, pl.ds(0, whole)]))
        pairs.append((m_ref.at[tail, :], edges[k].at[:, pl.ds(whole, plan.maps)]))
    run_copies(pairs, sems)


def cut_kernel(plan, o_ref, *refs):
    own, _ = place(plan)
    pairs = []
    for k in range(plan.half):
        start = pl.multiple_of(jnp.bitwise_xor(own, k) * plan.all, LANES)
        pairs.append((o_ref.at[:, pl.ds(start, plan.all)], refs[k]))
    run_copies(pairs, refs[-1])


def forward_kernel(plan, *refs):
    half, width, maps, tile = plan.half, plan.all, plan.maps, plan.tile
    conv = width + maps
    pays, edges = refs[:half], refs[half : 2 * half]
    (cw_ref, cb_ref, dl_ref, sb_ref, x_ref, ds_ref, el_ref, xm_ref, dm_ref, st_ref, sg_ref, cum_ref,
     raw, sraw, prm) = refs[2 * half :]
    own, _ = place(plan)
    heads = dl_ref.shape[1]
    halo = edges[0][...].astype(F32)
    for k in range(1, half):
        halo = halo + edges[k][...].astype(F32)
    raw[0:PAD, :] = halo[16 - PAD :, :]
    sraw[...] = jnp.zeros_like(sraw)
    for k in range(half):
        block = jnp.bitwise_xor(own, k) * BLOCK
        raw[pl.ds(pl.multiple_of(block + PAD, 8), BLOCK), :] = pays[k][:, :conv].astype(F32)
        sraw[pl.ds(pl.multiple_of(block, 8), BLOCK), 0:heads] = pays[k][0:heads, conv:].astype(F32).T
    rates, offsets = head_rows(plan, prm, [-jnp.exp(dl_ref[...]), sb_ref[...]], own)
    shift = lax.rem(LANES - own * plan.heads, LANES)
    lower = (iota((BLOCK, BLOCK), 0) >= iota((BLOCK, BLOCK), 1)).astype(F32)
    el_ref[0:BLOCK, :] = jnp.zeros((BLOCK, width), F32)

    def body(b, carry):
        row = pl.multiple_of(b * BLOCK, BLOCK)
        rows = pl.ds(row, BLOCK)
        for c in range(0, conv, tile):
            window = raw[pl.ds(row, BLOCK + PAD), c : c + tile]
            if c < width:
                cols = pl.ds(pl.multiple_of(own * width + c, LANES), tile)
                to_x, to_d, at = x_ref, ds_ref, c
            else:
                cols = slice(plan.inner + c - width, plan.inner + c - width + tile)
                to_x, to_d, at = xm_ref, dm_ref, c - width
            weight = cw_ref[:, cols]
            v = jnp.broadcast_to(cb_ref[:, cols], (BLOCK, tile))
            for k in range(weight.shape[0]):
                v = v + weight[k : k + 1, :] * window[PAD - k : PAD - k + BLOCK, :]
            s = 1.0 / (1.0 + jnp.exp(-v))
            to_x[rows, at : at + tile] = v * s
            to_d[rows, at : at + tile] = s * (1.0 + v * (1.0 - s))
        a = pltpu.roll(sraw[rows, :], shift, 1) + offsets
        e = jnp.exp(-jnp.abs(a))
        u = 1.0 + e
        d = u - 1.0
        step = jnp.maximum(a, 0.0) + jnp.where(d == 0.0, e, jnp.log(u) * (e / jnp.where(d == 0.0, 1.0, d)))
        st_ref[rows, :] = step
        sg_ref[rows, :] = jnp.where(a >= 0.0, 1.0, e) / u
        cum = lax.dot_general(lower, step * rates, NN, precision=lax.Precision.HIGHEST, preferred_element_type=F32)
        cum_ref[rows, :] = cum
        total = cum[BLOCK - 1 :, :]
        weighted = jnp.exp(total - cum) * step
        decay = jnp.exp(total)
        bt = wide(split(xm_ref[rows, : plan.state].T))
        nxt = pl.ds(pl.multiple_of(row + BLOCK, BLOCK), BLOCK)
        for c in range(0, width, tile):
            at, head = slice(c, c + tile), c // HEAD
            wx = split(x_ref[rows, at] * expand(weighted, head, tile))
            el_ref[nxt, at] = el_ref[rows, at] * expand(decay, head, tile) + mm_wide(bt, wx)
        return carry

    lax.fori_loop(0, plan.blocks, body, 0)


def gradient_kernel(stage, *refs):
    plan, first, last = stage.plan, stage.first, stage.last
    half, width, blocks, tile, state = plan.half, plan.width, plan.blocks, plan.tile, plan.state
    if first:
        grads, refs = refs[:half], refs[half:]
    else:
        gy_ref, top_old, after, refs = refs[0], refs[1], refs[2], refs[3:]
    xm_ref, cum_ref, el_ref, x_ref, ds_ref, dm_ref, st_ref, sk_ref, gl_ref, send_ref = refs[:10]
    if not last:
        top_ref = refs[10]
    if first:
        gy_ref = refs[11]
    prm = refs[-1]
    own, late = place(plan)
    if first:
        for k in range(half):
            block = pl.multiple_of(jnp.bitwise_xor(own, k) * BLOCK, BLOCK)
            gy_ref[pl.ds(block, BLOCK), :] = grads[k][...]
    gl_ref[blocks * BLOCK :, :] = jnp.zeros((BLOCK, width), F32)

    def body(t, carry):
        row = pl.multiple_of((blocks - 1 - t) * BLOCK, BLOCK)
        rows = pl.ds(row, BLOCK)
        nxt = pl.ds(pl.multiple_of(row + BLOCK, BLOCK), BLOCK)
        cum = cum_ref[rows, :]
        grown, decay = jnp.exp(cum), jnp.exp(cum[BLOCK - 1 :, :])
        ct = wide(split(xm_ref[rows, plan.state :].T))
        for at, among, head in stage.steps():
            ge = split(gy_ref[rows, among].astype(F32) * expand(grown, head, tile))
            gl_ref[rows, at] = gl_ref[nxt, at] * expand(decay, head, tile) + mm_wide(ct, ge)
        return carry

    each_block(blocks, body)

    @pl.when(late == 0)
    def _():
        send_ref[0:BLOCK, :] = el_ref[blocks * BLOCK :, stage.start : stage.start + width]
        send_ref[BLOCK:, :] = jnp.zeros((16, width), F32)
        if not last:
            top_ref[...] = jnp.zeros_like(top_ref)

    @pl.when(late != 0)
    def _():
        send_ref[0:BLOCK, :] = gl_ref[0:BLOCK, :]
        (skips,) = head_rows(plan, prm, [sk_ref[...]], own)
        top = slice(0, 16)
        edge = send_ref.at[BLOCK : BLOCK + 16, :]
        cum, step, cum_t = cum_ref[top, :], st_ref[top, :], cum_ref[0:BLOCK, :].T
        shrunk, grown = jnp.exp(cum_ref[BLOCK - 1 : BLOCK, :] - cum), jnp.exp(cum)
        top_b, first_c = split(xm_ref[top, :state]), split(xm_ref[0:BLOCK, state:])
        wide_b = wide(top_b)
        scores = mm3(top_b, first_c, NT)
        causal = iota((16, BLOCK), 0) <= iota((16, BLOCK), 1)
        if first:
            d_b, dsc = jnp.zeros((16, state), F32), jnp.zeros((16, BLOCK), F32)
        else:
            d_b, dsc = top_old[:, :state], top_old[:, state:]
        zero, blank = jnp.zeros((BLOCK, LANES), BF16), jnp.zeros((16, LANES), BF16)
        left, left_top = iota((BLOCK, LANES), 1) < HEAD, iota((16, LANES), 1) < HEAD
        for i in range(width // LANES):
            at, head = slice(i * LANES, (i + 1) * LANES), stage.head + 2 * i
            among = slice(head * HEAD, head * HEAD + LANES)
            step_x, shrunk_x = expand(step, head), expand(shrunk, head)
            xs = x_ref[top, among] * step_x
            gy = gy_ref[0:BLOCK, among]
            decays, mh, ml = [], [], []
            for h in (head, head + 1):
                spread = cum_t[h : h + 1, :] - jnp.broadcast_to(cum[:, h : h + 1], (16, BLOCK))
                decay = jnp.exp(jnp.where(causal, spread, NEG))
                high, low = split(scores * decay)
                decays.append(decay)
                mh.append(high)
                ml.append(low)
            gs = jnp.concatenate([jnp.where(left, gy, zero), jnp.where(left, zero, gy)], axis=0)
            dxs = mm(jnp.concatenate(mh, axis=1), gs) + mm(jnp.concatenate(ml, axis=1), gs)
            xh, xl = split(xs)
            rows = [jnp.where(left_top, xh, blank), jnp.where(left_top, blank, xh)]
            rows += [jnp.where(left_top, xl, blank), jnp.where(left_top, blank, xl)]
            dm = mm(jnp.concatenate(rows, axis=0), gy, NT)
            dsc = dsc + (dm[0:16] + dm[32:48]) * decays[0] + (dm[16:32] + dm[48:64]) * decays[1]
            leaving = split(gl_ref[BLOCK : 2 * BLOCK, at])
            dxs = dxs + shrunk_x * mm_wide(wide_b, leaving)
            d_b = d_b + mm_over(split(xs * shrunk_x), leaving)
            top_gy = gy[0:16].astype(F32)
            edge[0:PAD, at] = ((dxs * step_x + expand(skips, head) * top_gy) * ds_ref[top, among])[0:PAD]
            edge[PAD:, at] = (top_gy * expand(grown, head))[0:PAD]
        if last:
            parts = split(dsc)
            d_b = (d_b + mm3(parts, first_c)) * dm_ref[top, :state]
            d_c = mm3(parts, top_b, TN)
            silu_c = dm_ref[top, state:]
            edge[3:6, 0:state] = d_b[0:3]
            edge[6:8, 0:state] = silu_c[0:2]
            edge[11:14, 0:state] = d_c[0:3]
            edge[14:15, 0:state] = silu_c[2:3]
        else:
            top_ref[:, :state] = d_b
            top_ref[:, state:] = dsc


def within_kernel(stage, *refs):
    plan, first = stage.plan, stage.first
    x_ref, xm_ref, st_ref, cum_ref, gy_ref = refs[:5]
    refs = refs[5:]
    if not first:
        dsc_old, refs = refs[0], refs[1:]
    yw_ref, dw_ref, dsc_ref = refs
    width, state = plan.width, plan.state
    causal = iota((BLOCK, BLOCK), 0) >= iota((BLOCK, BLOCK), 1)
    left = iota((BLOCK, LANES), 1) < HEAD

    def body(b, carry):
        rows = pl.ds(pl.multiple_of(b * BLOCK, BLOCK), BLOCK)
        cum = cum_ref[rows, :]
        cum_t = cum.T
        step = st_ref[rows, :]
        b_maps = split(xm_ref[rows, :state])
        c_maps = split(xm_ref[rows, state:])
        scores = mm3(c_maps, b_maps, NT)
        total = jnp.zeros((BLOCK, BLOCK), F32) if first else dsc_old[rows, :]
        zero = jnp.zeros((BLOCK, LANES), BF16)
        for i in range(width // LANES):
            at, head = slice(i * LANES, (i + 1) * LANES), stage.head + 2 * i
            xs = x_ref[rows, head * HEAD : head * HEAD + LANES] * expand(step, head)
            xh, xl = split(xs)
            gy = gy_ref[rows, head * HEAD : head * HEAD + LANES]
            g0, g1 = jnp.where(left, gy, zero), jnp.where(left, zero, gy)
            decays, mh, ml = [], [], []
            for h in (head, head + 1):
                spread = jnp.broadcast_to(cum[:, h : h + 1], (BLOCK, BLOCK)) - cum_t[h : h + 1, :]
                decay = jnp.exp(jnp.where(causal, spread, NEG))
                high, low = split(scores * decay)
                decays.append(decay)
                mh.append(high)
                ml.append(low)
            both = jnp.concatenate(
                [
                    jnp.concatenate([jnp.where(left, xh, zero), jnp.where(left, xl, zero)], axis=1),
                    jnp.concatenate([jnp.where(left, zero, xh), jnp.where(left, zero, xl)], axis=1),
                ],
                axis=0,
            )
            high = mm(jnp.concatenate(mh, axis=1), both)
            low = mm(jnp.concatenate(ml, axis=1), both[:, :LANES])
            yw_ref[rows, at] = high[:, :LANES] + (high[:, LANES:] + low)
            gs = jnp.concatenate([g0, g1], axis=0)
            dw_ref[rows, at] = mm(jnp.concatenate(mh, axis=0), gs, TN) + mm(jnp.concatenate(ml, axis=0), gs, TN)
            dm = mm(jnp.concatenate([gs, gs], axis=1), jnp.concatenate([xh, xl], axis=1), NT)
            total = total + dm[:BLOCK] * decays[0] + dm[BLOCK:] * decays[1]
        dsc_ref[rows, :] = total
        return carry

    lax.fori_loop(0, plan.blocks, body, 0)


def final_kernel(stage, *refs):
    plan, first, last = stage.plan, stage.first, stage.last
    half, width, blocks, state, tile, maps = plan.half, plan.width, plan.blocks, plan.state, plan.tile, plan.maps
    (both_ref, x_ref, xm_ref, ds_ref, st_ref, sg_ref, cum_ref, el_ref, gl_ref, gy_ref, yw_ref, dw_ref,
     cw_ref, dl_ref, sk_ref) = refs[:15]
    refs = refs[15:]
    got_ref, edge_ref = both_ref.at[0:BLOCK, :], both_ref.at[BLOCK : BLOCK + 16, :]
    if last:
        dsc_ref, dm_ref, refs = refs[0], refs[1], refs[2:]
    if not first:
        bc_old, ac_old, dst_old, refs = refs[0], refs[1], refs[2], refs[3:]
    outs, refs = refs[:half], refs[half:]
    if not last:
        bc_ref, ac_ref, dst_ref, refs = refs[0], refs[1], refs[2], refs[3:]
    prm, dz, nxt_dz, carry_ref, o_sc, lc_sc = refs[:6]
    conv = width + maps if last else width
    own, late = place(plan)
    is_late = late.astype(F32)
    rates, skips = head_rows(plan, prm, [-jnp.exp(dl_ref[...]), sk_ref[...]], own)
    upper = (iota((BLOCK, BLOCK), 0) <= iota((BLOCK, BLOCK), 1)).astype(F32).astype(BF16)
    after_c = jnp.zeros((16, state), F32) if first else ac_old[...]
    for at, among, _ in stage.steps():
        after_c = after_c + mm_over(split(edge_ref[:, at]), split(el_ref[blocks * BLOCK :, among]))
    early = iota((PAD, LANES), 0) * 0 + late == 0
    for c in range(0, width, LANES):
        nxt_dz[:, c : c + LANES] = jnp.where(early, edge_ref[0:PAD, c : c + LANES], 0.0)
    if last:
        rest = jnp.zeros((PAD - 3, state), F32)
        nxt_dz[:, width : width + state] = jnp.where(early, jnp.concatenate([edge_ref[3:6, 0:state], rest], axis=0), 0.0)
        silu_c = jnp.concatenate([edge_ref[6:8, 0:state], edge_ref[14:15, 0:state]], axis=0)
        after_c = (after_c[PAD : PAD + 3] + edge_ref[11:14, 0:state]) * silu_c
        nxt_dz[:, width + state :] = jnp.where(early, jnp.concatenate([after_c, rest], axis=0), 0.0)
    else:
        ac_ref[...] = after_c
    lc_sc[...] = jnp.zeros_like(lc_sc)
    for b in range(1, blocks):
        lc_sc[b : b + 1, :] = lc_sc[b - 1 : b, :] + cum_ref[b * BLOCK - 1 : b * BLOCK, :]
    whole = lc_sc[blocks - 1 : blocks, :] + cum_ref[blocks * BLOCK - 1 :, :]
    ends = jnp.zeros((8, LANES), F32)
    ontos = {head: onto_heads(head, tile) for _, _, head in stage.steps()}
    for at, among, head in stage.steps():
        product = jnp.sum(got_ref[:, at] * el_ref[blocks * BLOCK :, among], axis=0, keepdims=True)
        ends = ends + head_sums([jnp.broadcast_to(product, (16, tile))], ontos[head])[0][0:8]
    carry_ref[...] = ends * (1.0 - is_late)

    def body(t, carry):
        b = blocks - 1 - t
        row = pl.multiple_of(b * BLOCK, BLOCK)
        rows = pl.ds(row, BLOCK)
        nxt = pl.ds(pl.multiple_of(row + BLOCK, BLOCK), BLOCK)
        cum, step = cum_ref[rows, :], st_ref[rows, :]
        total = cum[BLOCK - 1 :, :]
        grown, shrunk = jnp.exp(cum), jnp.exp(total - cum)
        before = lc_sc[pl.ds(b, 1), :]
        from_first = jnp.exp(before) * is_late
        to_last = jnp.exp(whole - before - total) * (1.0 - is_late)
        b_maps, c_maps = split(xm_ref[rows, :state]), split(xm_ref[rows, state:])
        b_wide, c_wide = wide(b_maps), wide(c_maps)
        if first:
            d_b = d_c = jnp.zeros((BLOCK, state), F32)
        else:
            d_b, d_c = bc_old[rows, :state], bc_old[rows, state:]
        if last:
            dsc = dsc_ref[rows, :]
            d_c = d_c + mm3(split(dsc), b_maps)
            d_b = d_b + mm3(split(dsc.T), c_maps)
        sums = jnp.zeros((BLOCK, LANES), F32)
        direct = jnp.zeros((BLOCK, LANES), F32)
        for at, among, head in stage.steps():
            got = got_ref[:, at]
            entering = split(el_ref[rows, among] + got * expand(from_first, head, tile))
            leaving = split(gl_ref[nxt, at] + got * expand(to_last, head, tile))
            x = x_ref[rows, among]
            step_x, shrunk_x, grown_x = expand(step, head, tile), expand(shrunk, head, tile), expand(grown, head, tile)
            xs = x * step_x
            gy = gy_ref[rows, among].astype(F32)
            y = yw_ref[rows, at] + grown_x * mm_wide(c_wide, entering)
            dxs = dw_ref[rows, at] + shrunk_x * mm_wide(b_wide, leaving)
            d_c = d_c + mm_over(split(gy * grown_x), entering)
            d_b = d_b + mm_over(split(xs * shrunk_x), leaving)
            both = head_sums([gy * y - xs * dxs, dxs * x], ontos[head])
            sums, direct = sums + both[0], direct + both[1]
            dz[0:BLOCK, at] = (dxs * step_x + expand(skips, head, tile) * gy) * ds_ref[rows, among]
        sums_high, sums_low = split(sums)
        d_log = mm(upper, sums_high) + mm(upper, sums_low) + carry_ref[0:1, :]
        carry_ref[...] = jnp.broadcast_to(d_log[0:1, :], (8, LANES))
        d_step = (d_log * rates + direct) * sg_ref[rows, :]
        lane = iota((BLOCK, LANES), 1)
        d_step = jnp.where((lane >= stage.head) & (lane < stage.head + width // HEAD), d_step, 0.0)
        if not first:
            d_step = d_step + dst_old[rows, :]
        if last:
            o_sc[rows, width : width + LANES] = d_step.astype(BF16)
            dz[0:BLOCK, width : width + state] = d_b * dm_ref[rows, :state]
            dz[0:BLOCK, width + state :] = d_c * dm_ref[rows, state:]
        else:
            dst_ref[rows, :] = d_step
            bc_ref[rows, :state] = d_b
            bc_ref[rows, state:] = d_c
        dz[BLOCK:, :] = nxt_dz[...]
        for c in range(0, conv, LANES):
            window = dz[:, c : c + LANES]
            if c < width:
                cols = pl.ds(pl.multiple_of(own * plan.all + stage.start + c, LANES), LANES)
            else:
                cols = slice(plan.inner + c - width, plan.inner + c - width + LANES)
            weight = cw_ref[:, cols]
            grad = weight[0:1, :] * window[0:BLOCK, :]
            for k in range(1, weight.shape[0]):
                grad = grad + weight[k : k + 1, :] * window[k : k + BLOCK, :]
            if c < width:
                o_sc[rows, c : c + LANES] = grad.astype(BF16)
            else:
                high, low = split(grad)
                o_sc[rows, LANES + c : 2 * LANES + c] = high
                o_sc[rows, LANES + maps + c : 2 * LANES + maps + c] = low
        nxt_dz[...] = dz[0:PAD, :]
        return carry

    each_block(blocks, body)
    for k in range(half):
        rows = pl.ds(pl.multiple_of(jnp.bitwise_xor(own, k) * BLOCK, BLOCK), BLOCK)
        outs[k][...] = o_sc[rows, :]


def owner_kernel(stage, *refs):
    plan, last, maps = stage.plan, stage.last, stage.plan.maps
    half, width = plan.half, plan.width
    outs, refs = refs[:half], refs[half:]
    if stage.part:
        refs = refs[1:]
    f_ref = refs[0]
    own, _ = place(plan)
    pairs = []
    for k in range(half):
        start = pl.multiple_of(jnp.bitwise_xor(own, k) * plan.all + stage.start, LANES)
        pairs.append((outs[k].at[:, pl.ds(0, width)], f_ref.at[:, pl.ds(start, width)]))
    copies = [pltpu.make_async_copy(source, target, refs[-1].at[n]) for n, (source, target) in enumerate(pairs)]
    for copy in copies:
        copy.start()
    if last:
        m_ref, s_ref = refs[1:3]
        total = jnp.zeros((BLOCK, maps), F32)
        steps = jnp.zeros((BLOCK, LANES), F32)
        for k in range(half):
            part, end = jnp.bitwise_xor(own, k), outs[k]
            steps = steps + pltpu.roll(end[:, width : width + LANES].astype(F32), part * plan.heads, 1)
            high, low = end[:, width + LANES : width + LANES + maps], end[:, width + LANES + maps :]
            total = total + (high.astype(F32) + low.astype(F32))
        m_ref[...] = total.astype(BF16)
        s_ref[...] = steps.T[: s_ref.shape[0]].astype(BF16)
    for copy in copies:
        copy.wait()


def per_device(sections, devices, features, state_maps, step_raw, conv_weight, conv_bias, decay_log, step_bias, skip_gain, output_grads):
    state = state_maps.shape[2] // 2
    heads = decay_log.shape[1]
    plan = Plan(devices, features.shape[2], state, heads)
    half, width, tokens, parts, maps = plan.half, plan.width, plan.tokens, plan.parts, plan.maps
    weight = conv_weight[0]
    stages = [Stage(plan, p) for p in range(parts)]

    def partner(array, k):
        return lax.ppermute(array, "ctx", [(i, i ^ k) for i in range(devices)])

    def shifted(array, k):
        route = [
            (((p + 1) % sections) * devices + i, p * devices + (i ^ k))
            for p in range(sections)
            for i in range(devices)
        ]
        return lax.ppermute(array, ("pipe", "ctx"), route)

    conv = plan.all + maps
    away = pl.BlockSpec(memory_space=pl.ANY)
    far = pl.BlockSpec(memory_space=pltpu.HBM)

    def hold(array):
        return pltpu.with_memory_space_constraint(array, pltpu.HBM)

    packed = call(
        pack_kernel,
        plan,
        [struct(BLOCK, conv + LANES, dtype=BF16)] * half + [struct(16, conv, dtype=BF16)] * half,
        [pltpu.SemaphoreType.DMA((half * (4 + BLOCK // heads),))],
        work=3.0,
        in_specs=[far] * 3,
    )(hold(features[0]), hold(state_maps[0]), hold(step_raw[0].T))
    cuts = call(
        cut_kernel,
        plan,
        [struct(BLOCK, plan.all, dtype=BF16)] * half,
        [pltpu.SemaphoreType.DMA((half,))],
        work=2.2,
        in_specs=[far],
    )(hold(output_grads[0]))
    pays = [packed[0]] + [partner(packed[k], k) for k in range(1, half)]
    edges = [lax.ppermute(e, "ctx", [(half - 1, half + k)]) for k, e in enumerate(packed[half:])]
    grads = [shifted(cuts[k], k) for k in range(half)]
    done = []
    small = pltpu.VMEM((8, LANES), F32)
    x_conv, dsilu, states, x_maps, d_maps, steps, sigmoids, cums = call(
        forward_kernel,
        plan,
        [near(tokens, plan.all), near(tokens, plan.all), near(tokens + BLOCK, plan.all), near(tokens, maps),
         near(tokens, maps)] + [near(tokens, LANES)] * 3,
        [pltpu.VMEM((tokens + PAD, conv), F32), pltpu.VMEM((tokens, LANES), F32), small],
        work=5.0,
    )(*pays, *edges, weight, conv_bias, decay_log, step_bias)
    for stage in stages:
        first = stage.first
        args = [] if first else [gy, top, scores]
        args += [*(grads if first else ()), x_maps, cums, states, x_conv, dsilu, d_maps, steps, skip_gain]
        outs = [near(tokens + BLOCK, width), struct(BLOCK + 16, width)]
        if not stage.last:
            outs += [near(16, state + BLOCK)]
        if first:
            outs += [near(tokens, plan.all, dtype=BF16)]
        back, send, *rest = call(gradient_kernel, stage, outs, [small], work=2.1)(*args)
        if first:
            top, gy = rest
            within = []
            for other in stages:
                outs = [near(tokens, width), near(tokens, width), near(tokens, BLOCK)]
                args = [x_conv, x_maps, steps, cums, gy] + ([] if other.first else [scores])
                y_within, d_within, scores = call(within_kernel, other, outs, work=2.0)(*args)
                within.append((y_within, d_within))
        got = partner(send, half)
        done.append((got, x_conv, x_maps, dsilu, steps, sigmoids, cums, states, back, gy, *within[stage.part]))
    feature_parts = []
    for stage, arrays in zip(stages, done):
        first, last = stage.first, stage.last
        conv = width + maps if last else width
        out = width + LANES + 2 * maps if last else width
        args = [*arrays, weight, decay_log, skip_gain]
        outs = [struct(BLOCK, out, dtype=BF16)] * half
        scratch = [small, pltpu.VMEM((BLOCK + PAD, conv), F32), pltpu.VMEM((PAD, conv), F32), small,
                   pltpu.VMEM((tokens, out), BF16), pltpu.VMEM((max(8, plan.blocks), LANES), F32)]
        if last:
            args += [scores, d_maps]
        else:
            outs += [near(tokens, maps), near(16, state), near(tokens, LANES)]
        if not first:
            args += carried
        result = call(final_kernel, stage, outs, scratch, work=5.8)(*args)
        feature_parts += [result[0]] + [partner(result[k], k) for k in range(1, half)]
        carried = result[half:]
    inside = pl.BlockSpec(memory_space=pltpu.VMEM)
    for stage in stages:
        more = [feature_grads] if stage.part else []
        outs = [struct(BLOCK, plan.inner, dtype=BF16)]
        if stage.last:
            outs += [struct(BLOCK, maps, dtype=BF16), struct(heads, BLOCK, dtype=BF16)]
        feature_grads, *others = call(
            owner_kernel,
            stage,
            outs,
            [pltpu.SemaphoreType.DMA((half,))],
            work=2.0,
            in_specs=[inside] * half + [away] * len(more),
            out_specs=[away] + [inside] * (len(outs) - 1),
            input_output_aliases={half: 0} if more else {},
        )(*feature_parts[stage.part * half : (stage.part + 1) * half], *more)
    map_grads, step_grads = others
    return (feature_grads[None], map_grads[None], step_grads.T[None])


def solution(mesh):
    return jax.shard_map(
        functools.partial(per_device, mesh.shape["pipe"], mesh.shape["ctx"]),
        mesh=mesh,
        in_specs=(
            P("pipe", "ctx", None),
            P("pipe", "ctx", None),
            P("pipe", "ctx", None),
            P("pipe", None, None),
            P("pipe", None),
            P("pipe", None),
            P("pipe", None),
            P("pipe", None),
            P("pipe", "ctx", None),
        ),
        out_specs=(P("pipe", "ctx", None), P("pipe", "ctx", None), P("pipe", "ctx", None)),
        check_vma=False,
    )
```

```python
import functools

import jax
import jax.numpy as jnp
from jax import lax
from jax.experimental import pallas as pl
from jax.experimental.pallas import tpu as pltpu
from jax.sharding import PartitionSpec as P

BLOCK = 128
LANES = 128
HEAD = 64
PAD = 8
PARTS = 2
UNROLL = 4
F32 = jnp.float32
BF16 = jnp.bfloat16
NEG = -1e30
NN = (((1,), (0,)), ((), ()))
NT = (((1,), (1,)), ((), ()))
TN = (((0,), (0,)), ((), ()))


def mm(a, b, dims=NN):
    return lax.dot_general(a, b, dims, preferred_element_type=F32)


def split(a):
    high = a.astype(BF16)
    return high, (a - high.astype(F32)).astype(BF16)


def mm3(a, b, dims=NN):
    (ah, al), (bh, bl) = a, b
    return mm(ah, bh, dims) + (mm(ah, bl, dims) + mm(al, bh, dims))


def iota(shape, axis):
    return lax.broadcasted_iota(jnp.int32, shape, axis)


def wide(a):
    high, low = a
    return jnp.concatenate([high, low], axis=1), high


def mm_wide(a, b):
    (both, high), (bh, bl) = a, b
    return mm(both, jnp.concatenate([bh, bh], axis=0)) + mm(high, bl)


def mm_over(a, b):
    (ah, al), (bh, bl) = a, b
    n = bh.shape[0]
    both = mm(ah, jnp.concatenate([bh, bl], axis=0), NT)
    return both[:, :n] + (both[:, n:] + mm(al, bh, NT))


def expand(values, head, count=LANES):
    rows = values.shape[0]
    left = iota((rows, LANES), 1) < HEAD
    tiles = []
    for h in range(head, head + count // HEAD, 2):
        first = jnp.broadcast_to(values[:, h : h + 1], (rows, LANES))
        second = jnp.broadcast_to(values[:, h + 1 : h + 2], (rows, LANES))
        tiles.append(jnp.where(left, first, second))
    return tiles[0] if len(tiles) == 1 else jnp.concatenate(tiles, axis=1)


def onto_heads(head, count):
    shape = (count, LANES)
    return (iota(shape, 1) == head + iota(shape, 0) // HEAD).astype(F32).astype(BF16)


def head_sums(values, onto):
    rows = values[0].shape[0]
    sums = mm(jnp.concatenate([part for value in values for part in split(value)], axis=0), onto)
    return [sums[2 * n * rows : (2 * n + 1) * rows] + sums[(2 * n + 1) * rows : (2 * n + 2) * rows] for n in range(len(values))]


class Plan:
    def __init__(self, devices, inner, state, heads):
        self.half = devices // 2
        self.inner = inner
        self.state = state
        self.maps = 2 * state
        self.heads = heads // self.half
        self.all = inner // self.half
        self.parts = PARTS
        self.width = self.all // PARTS
        self.tile = 2 * LANES if self.width % (2 * LANES) == 0 else LANES
        self.tiles = self.width // self.tile
        self.blocks = self.half
        self.spans = -(-self.heads // PAD)
        self.tokens = self.half * BLOCK


class Stage:
    def __init__(self, plan, part):
        self.plan = plan
        self.part = part
        self.first = part == 0
        self.last = part == plan.parts - 1
        self.head = part * plan.width // HEAD
        self.start = part * plan.width

        self.edge = 2 * PAD if self.last else PAD
        self.grown = PAD if self.last else 3

    def steps(self):
        tile = self.plan.tile
        for i in range(self.plan.tiles):
            lane = self.start + i * tile
            yield slice(i * tile, (i + 1) * tile), slice(lane, lane + tile), lane // HEAD


def each_block(blocks, body):
    if blocks <= UNROLL:
        for b in range(blocks):
            body(b, 0)
    else:
        lax.fori_loop(0, blocks, body, 0)


def place(plan):
    rank = lax.axis_index("ctx")
    return lax.rem(rank, plan.half), lax.div(rank, plan.half)


def call(kernel, stage, out_shape, scratch=(), work=1.0, **more):
    return pl.pallas_call(
        functools.partial(kernel, stage),
        out_shape=out_shape,
        scratch_shapes=list(scratch),
        compiler_params=pltpu.CompilerParams(vmem_limit_bytes=32 * 1024 * 1024),
        cost_estimate=pl.CostEstimate(flops=int(work * 1.15e9), transcendentals=0, bytes_accessed=1 << 20),
        **more,
    )


def struct(*shape, dtype=F32):
    return jax.ShapeDtypeStruct(shape, dtype)


def near(*shape, dtype=F32):
    return pltpu.VMEM(shape, dtype)


def head_rows(plan, prm, refs, own):
    prm[...] = jnp.zeros_like(prm)
    for row, values in enumerate(refs):
        prm[row : row + 1, 0 : values.shape[1]] = values
    local = pltpu.roll(prm[...], lax.rem(LANES - own * plan.heads, LANES), 1)
    return [local[row : row + 1, :] for row in range(len(refs))]


def run_copies(pairs, sems):
    copies = [pltpu.make_async_copy(source, target, sems.at[n]) for n, (source, target) in enumerate(pairs)]
    for copy in copies:
        copy.start()
    for copy in copies:
        copy.wait()


def pack_kernel(plan, f_ref, m_ref, s_ref, *refs):
    pays, edges, sems = refs[: plan.half], refs[plan.half : -1], refs[-1]
    own, _ = place(plan)
    whole, heads = plan.all, s_ref.shape[0]
    pairs = []
    for k in range(plan.half):
        start = pl.multiple_of(jnp.bitwise_xor(own, k) * whole, LANES)
        pairs.append((f_ref.at[:, pl.ds(start, whole)], pays[k].at[:, pl.ds(0, whole)]))
        pairs.append((m_ref, pays[k].at[:, pl.ds(whole, plan.maps)]))
        for row in range(0, BLOCK, heads):
            pairs.append((s_ref, pays[k].at[pl.ds(row, heads), pl.ds(whole + plan.maps, LANES)]))
        tail = pl.ds(BLOCK - 16, 16)
        pairs.append((f_ref.at[tail, pl.ds(k * whole, whole)], edges[k].at[:, pl.ds(0, whole)]))
        pairs.append((m_ref.at[tail, :], edges[k].at[:, pl.ds(whole, plan.maps)]))
    run_copies(pairs, sems)


def cut_kernel(plan, o_ref, *refs):
    own, _ = place(plan)
    pairs = []
    for k in range(plan.half):
        start = pl.multiple_of(jnp.bitwise_xor(own, k) * plan.all, LANES)
        pairs.append((o_ref.at[:, pl.ds(start, plan.all)], refs[k]))
    run_copies(pairs, refs[-1])


def forward_kernel(plan, *refs):
    half, width, maps, tile = plan.half, plan.all, plan.maps, plan.tile
    conv = width + maps
    pays, edges = refs[:half], refs[half : 2 * half]
    (cw_ref, cb_ref, dl_ref, sb_ref, x_ref, ds_ref, el_ref, xm_ref, dm_ref, st_ref, sg_ref, cum_ref,
     raw, sraw, prm) = refs[2 * half :]
    own, _ = place(plan)
    heads = dl_ref.shape[1]
    halo = edges[0][...].astype(F32)
    for k in range(1, half):
        halo = halo + edges[k][...].astype(F32)
    raw[0:PAD, :] = halo[16 - PAD :, :]
    sraw[...] = jnp.zeros_like(sraw)
    for k in range(half):
        block = jnp.bitwise_xor(own, k) * BLOCK
        raw[pl.ds(pl.multiple_of(block + PAD, 8), BLOCK), :] = pays[k][:, :conv].astype(F32)
        sraw[pl.ds(pl.multiple_of(block, 8), BLOCK), 0:heads] = pays[k][0:heads, conv:].astype(F32).T
    rates, offsets = head_rows(plan, prm, [-jnp.exp(dl_ref[...]), sb_ref[...]], own)
    shift = lax.rem(LANES - own * plan.heads, LANES)
    lower = (iota((BLOCK, BLOCK), 0) >= iota((BLOCK, BLOCK), 1)).astype(F32)
    el_ref[0:BLOCK, :] = jnp.zeros((BLOCK, width), F32)

    def body(b, carry):
        row = pl.multiple_of(b * BLOCK, BLOCK)
        rows = pl.ds(row, BLOCK)
        for c in range(0, conv, tile):
            window = raw[pl.ds(row, BLOCK + PAD), c : c + tile]
            if c < width:
                cols = pl.ds(pl.multiple_of(own * width + c, LANES), tile)
                to_x, to_d, at = x_ref, ds_ref, c
            else:
                cols = slice(plan.inner + c - width, plan.inner + c - width + tile)
                to_x, to_d, at = xm_ref, dm_ref, c - width
            weight = cw_ref[:, cols]
            v = jnp.broadcast_to(cb_ref[:, cols], (BLOCK, tile))
            for k in range(weight.shape[0]):
                v = v + weight[k : k + 1, :] * window[PAD - k : PAD - k + BLOCK, :]
            s = 1.0 / (1.0 + jnp.exp(-v))
            to_x[rows, at : at + tile] = v * s
            to_d[rows, at : at + tile] = s * (1.0 + v * (1.0 - s))
        a = pltpu.roll(sraw[rows, :], shift, 1) + offsets
        e = jnp.exp(-jnp.abs(a))
        u = 1.0 + e
        d = u - 1.0
        step = jnp.maximum(a, 0.0) + jnp.where(d == 0.0, e, jnp.log(u) * (e / jnp.where(d == 0.0, 1.0, d)))
        st_ref[rows, :] = step
        sg_ref[rows, :] = jnp.where(a >= 0.0, 1.0, e) / u
        cum = lax.dot_general(lower, step * rates, NN, precision=lax.Precision.HIGHEST, preferred_element_type=F32)
        cum_ref[rows, :] = cum
        total = cum[BLOCK - 1 :, :]
        weighted = jnp.exp(total - cum) * step
        decay = jnp.exp(total)
        bt = wide(split(xm_ref[rows, : plan.state].T))
        nxt = pl.ds(pl.multiple_of(row + BLOCK, BLOCK), BLOCK)
        for c in range(0, width, tile):
            at, head = slice(c, c + tile), c // HEAD
            wx = split(x_ref[rows, at] * expand(weighted, head, tile))
            el_ref[nxt, at] = el_ref[rows, at] * expand(decay, head, tile) + mm_wide(bt, wx)
        return carry

    lax.fori_loop(0, plan.blocks, body, 0)


def gradient_kernel(stage, *refs):
    plan, first, last = stage.plan, stage.first, stage.last
    half, width, blocks, tile, state = plan.half, plan.width, plan.blocks, plan.tile, plan.state
    if first:
        grads, refs = refs[:half], refs[half:]
    else:
        gy_ref, top_old, after, refs = refs[0], refs[1], refs[2], refs[3:]
    xm_ref, cum_ref, el_ref, x_ref, ds_ref, dm_ref, st_ref, sk_ref, gl_ref, send_ref = refs[:10]
    if not last:
        top_ref = refs[10]
    if first:
        gy_ref = refs[11]
    prm = refs[-1]
    own, late = place(plan)
    if first:
        for k in range(half):
            block = pl.multiple_of(jnp.bitwise_xor(own, k) * BLOCK, BLOCK)
            gy_ref[pl.ds(block, BLOCK), :] = grads[k][...]
    gl_ref[blocks * BLOCK :, :] = jnp.zeros((BLOCK, width), F32)

    def body(t, carry):
        row = pl.multiple_of((blocks - 1 - t) * BLOCK, BLOCK)
        rows = pl.ds(row, BLOCK)
        nxt = pl.ds(pl.multiple_of(row + BLOCK, BLOCK), BLOCK)
        cum = cum_ref[rows, :]
        grown, decay = jnp.exp(cum), jnp.exp(cum[BLOCK - 1 :, :])
        ct = wide(split(xm_ref[rows, plan.state :].T))
        for at, among, head in stage.steps():
            ge = split(gy_ref[rows, among].astype(F32) * expand(grown, head, tile))
            gl_ref[rows, at] = gl_ref[nxt, at] * expand(decay, head, tile) + mm_wide(ct, ge)
        return carry

    each_block(blocks, body)

    @pl.when(late == 0)
    def _():
        send_ref[0:BLOCK, :] = el_ref[blocks * BLOCK :, stage.start : stage.start + width]
        send_ref[BLOCK:, :] = jnp.zeros((stage.edge, width), F32)
        if not last:
            top_ref[...] = jnp.zeros_like(top_ref)

    @pl.when(late != 0)
    def _():
        send_ref[0:BLOCK, :] = gl_ref[0:BLOCK, :]
        (skips,) = head_rows(plan, prm, [sk_ref[...]], own)
        top = slice(0, 16)
        edge = send_ref.at[BLOCK : BLOCK + stage.edge, :]
        cum, step, cum_t = cum_ref[top, :], st_ref[top, :], cum_ref[0:BLOCK, :].T
        shrunk, grown = jnp.exp(cum_ref[BLOCK - 1 : BLOCK, :] - cum), jnp.exp(cum)
        top_b, first_c = split(xm_ref[top, :state]), split(xm_ref[0:BLOCK, state:])
        wide_b = wide(top_b)
        scores = mm3(top_b, first_c, NT)
        causal = iota((16, BLOCK), 0) <= iota((16, BLOCK), 1)
        if first:
            d_b, dsc = jnp.zeros((16, state), F32), jnp.zeros((16, BLOCK), F32)
        else:
            d_b, dsc = top_old[:, :state], top_old[:, state:]
        zero, blank = jnp.zeros((BLOCK, LANES), BF16), jnp.zeros((16, LANES), BF16)
        left, left_top = iota((BLOCK, LANES), 1) < HEAD, iota((16, LANES), 1) < HEAD
        for i in range(width // LANES):
            at, head = slice(i * LANES, (i + 1) * LANES), stage.head + 2 * i
            among = slice(head * HEAD, head * HEAD + LANES)
            step_x, shrunk_x = expand(step, head), expand(shrunk, head)
            xs = x_ref[top, among] * step_x
            gy = gy_ref[0:BLOCK, among]
            decays, mh, ml = [], [], []
            for h in (head, head + 1):
                spread = cum_t[h : h + 1, :] - jnp.broadcast_to(cum[:, h : h + 1], (16, BLOCK))
                decay = jnp.exp(jnp.where(causal, spread, NEG))
                high, low = split(scores * decay)
                decays.append(decay)
                mh.append(high)
                ml.append(low)
            gs = jnp.concatenate([jnp.where(left, gy, zero), jnp.where(left, zero, gy)], axis=0)
            dxs = mm(jnp.concatenate(mh, axis=1), gs) + mm(jnp.concatenate(ml, axis=1), gs)
            xh, xl = split(xs)
            rows = [jnp.where(left_top, xh, blank), jnp.where(left_top, blank, xh)]
            rows += [jnp.where(left_top, xl, blank), jnp.where(left_top, blank, xl)]
            dm = mm(jnp.concatenate(rows, axis=0), gy, NT)
            dsc = dsc + (dm[0:16] + dm[32:48]) * decays[0] + (dm[16:32] + dm[48:64]) * decays[1]
            leaving = split(gl_ref[BLOCK : 2 * BLOCK, at])
            dxs = dxs + shrunk_x * mm_wide(wide_b, leaving)
            d_b = d_b + mm_over(split(xs * shrunk_x), leaving)
            top_gy = gy[0:16].astype(F32)
            edge[0:PAD, at] = ((dxs * step_x + expand(skips, head) * top_gy) * ds_ref[top, among])[0:PAD]
            edge[stage.grown : stage.edge, at] = (top_gy * expand(grown, head))[0 : stage.edge - stage.grown]
        if last:
            parts = split(dsc)
            d_b = (d_b + mm3(parts, first_c)) * dm_ref[top, :state]
            d_c = mm3(parts, top_b, TN)
            silu_c = dm_ref[top, state:]
            edge[3:6, 0:state] = d_b[0:3]
            edge[6:8, 0:state] = silu_c[0:2]
            edge[11:14, 0:state] = d_c[0:3]
            edge[14:15, 0:state] = silu_c[2:3]
        else:
            top_ref[:, :state] = d_b
            top_ref[:, state:] = dsc


def within_kernel(stage, *refs):
    plan, first = stage.plan, stage.first
    x_ref, xm_ref, st_ref, cum_ref, gy_ref = refs[:5]
    refs = refs[5:]
    if not first:
        dsc_old, refs = refs[0], refs[1:]
    yw_ref, dw_ref, dsc_ref = refs
    width, state = plan.width, plan.state
    causal = iota((BLOCK, BLOCK), 0) >= iota((BLOCK, BLOCK), 1)
    left = iota((BLOCK, LANES), 1) < HEAD

    def body(b, carry):
        rows = pl.ds(pl.multiple_of(b * BLOCK, BLOCK), BLOCK)
        cum = cum_ref[rows, :]
        cum_t = cum.T
        step = st_ref[rows, :]
        b_maps = split(xm_ref[rows, :state])
        c_maps = split(xm_ref[rows, state:])
        scores = mm3(c_maps, b_maps, NT)
        total = jnp.zeros((BLOCK, BLOCK), F32) if first else dsc_old[rows, :]
        zero = jnp.zeros((BLOCK, LANES), BF16)
        for i in range(width // LANES):
            at, head = slice(i * LANES, (i + 1) * LANES), stage.head + 2 * i
            xs = x_ref[rows, head * HEAD : head * HEAD + LANES] * expand(step, head)
            xh, xl = split(xs)
            gy = gy_ref[rows, head * HEAD : head * HEAD + LANES]
            g0, g1 = jnp.where(left, gy, zero), jnp.where(left, zero, gy)
            decays, mh, ml = [], [], []
            for h in (head, head + 1):
                spread = jnp.broadcast_to(cum[:, h : h + 1], (BLOCK, BLOCK)) - cum_t[h : h + 1, :]
                decay = jnp.exp(jnp.where(causal, spread, NEG))
                high, low = split(scores * decay)
                decays.append(decay)
                mh.append(high)
                ml.append(low)
            both = jnp.concatenate(
                [
                    jnp.concatenate([jnp.where(left, xh, zero), jnp.where(left, xl, zero)], axis=1),
                    jnp.concatenate([jnp.where(left, zero, xh), jnp.where(left, zero, xl)], axis=1),
                ],
                axis=0,
            )
            high = mm(jnp.concatenate(mh, axis=1), both)
            low = mm(jnp.concatenate(ml, axis=1), both[:, :LANES])
            yw_ref[rows, at] = high[:, :LANES] + (high[:, LANES:] + low)
            gs = jnp.concatenate([g0, g1], axis=0)
            dw_ref[rows, at] = mm(jnp.concatenate(mh, axis=0), gs, TN) + mm(jnp.concatenate(ml, axis=0), gs, TN)
            dm = mm(jnp.concatenate([gs, gs], axis=1), jnp.concatenate([xh, xl], axis=1), NT)
            total = total + dm[:BLOCK] * decays[0] + dm[BLOCK:] * decays[1]
        dsc_ref[rows, :] = total
        return carry

    lax.fori_loop(0, plan.blocks, body, 0)


def final_kernel(stage, *refs):
    plan, first, last = stage.plan, stage.first, stage.last
    half, width, blocks, state, tile, maps = plan.half, plan.width, plan.blocks, plan.state, plan.tile, plan.maps
    (both_ref, x_ref, xm_ref, ds_ref, st_ref, sg_ref, cum_ref, el_ref, gl_ref, gy_ref, yw_ref, dw_ref,
     cw_ref, dl_ref, sk_ref) = refs[:15]
    refs = refs[15:]
    got_ref, edge_ref = both_ref.at[0:BLOCK, :], both_ref.at[BLOCK : BLOCK + stage.edge, :]
    if last:
        dsc_ref, dm_ref, refs = refs[0], refs[1], refs[2:]
    if not first:
        bc_old, ac_old, dst_old, refs = refs[0], refs[1], refs[2], refs[3:]
    outs, refs = refs[:half], refs[half:]
    if not last:
        bc_ref, ac_ref, dst_ref, refs = refs[0], refs[1], refs[2], refs[3:]
    prm, dz, nxt_dz, carry_ref, o_sc, lc_sc = refs[:6]
    if last:
        s_sc = refs[6]
        s_sc[...] = jnp.zeros_like(s_sc)
    conv = width + maps if last else width
    own, late = place(plan)
    is_late = late.astype(F32)
    rates, skips = head_rows(plan, prm, [-jnp.exp(dl_ref[...]), sk_ref[...]], own)
    upper = (iota((BLOCK, BLOCK), 0) <= iota((BLOCK, BLOCK), 1)).astype(F32).astype(BF16)
    after_c = jnp.zeros((16, state), F32) if first else ac_old[...]
    for at, among, _ in stage.steps():
        rows = edge_ref[:, at]
        if not last:
            rows = jnp.concatenate([jnp.zeros((PAD, tile), F32), rows[3:6], jnp.zeros((5, tile), F32)], axis=0)
        after_c = after_c + mm_over(split(rows), split(el_ref[blocks * BLOCK :, among]))
    early = iota((PAD, LANES), 0) * 0 + late == 0
    for c in range(0, width, LANES):
        nxt_dz[:, c : c + LANES] = jnp.where(early, edge_ref[0:PAD, c : c + LANES], 0.0)
    if last:
        rest = jnp.zeros((PAD - 3, state), F32)
        nxt_dz[:, width : width + state] = jnp.where(early, jnp.concatenate([edge_ref[3:6, 0:state], rest], axis=0), 0.0)
        silu_c = jnp.concatenate([edge_ref[6:8, 0:state], edge_ref[14:15, 0:state]], axis=0)
        after_c = (after_c[PAD : PAD + 3] + edge_ref[11:14, 0:state]) * silu_c
        nxt_dz[:, width + state :] = jnp.where(early, jnp.concatenate([after_c, rest], axis=0), 0.0)
    else:
        ac_ref[...] = after_c
    lc_sc[...] = jnp.zeros_like(lc_sc)
    for b in range(1, blocks):
        lc_sc[b : b + 1, :] = lc_sc[b - 1 : b, :] + cum_ref[b * BLOCK - 1 : b * BLOCK, :]
    whole = lc_sc[blocks - 1 : blocks, :] + cum_ref[blocks * BLOCK - 1 :, :]
    ends = jnp.zeros((8, LANES), F32)
    ontos = {head: onto_heads(head, tile) for _, _, head in stage.steps()}
    for at, among, head in stage.steps():
        product = jnp.sum(got_ref[:, at] * el_ref[blocks * BLOCK :, among], axis=0, keepdims=True)
        ends = ends + head_sums([jnp.broadcast_to(product, (16, tile))], ontos[head])[0][0:8]
    carry_ref[...] = ends * (1.0 - is_late)

    def body(t, carry):
        b = blocks - 1 - t
        row = pl.multiple_of(b * BLOCK, BLOCK)
        rows = pl.ds(row, BLOCK)
        nxt = pl.ds(pl.multiple_of(row + BLOCK, BLOCK), BLOCK)
        cum, step = cum_ref[rows, :], st_ref[rows, :]
        total = cum[BLOCK - 1 :, :]
        grown, shrunk = jnp.exp(cum), jnp.exp(total - cum)
        before = lc_sc[pl.ds(b, 1), :]
        from_first = jnp.exp(before) * is_late
        to_last = jnp.exp(whole - before - total) * (1.0 - is_late)
        b_maps, c_maps = split(xm_ref[rows, :state]), split(xm_ref[rows, state:])
        b_wide, c_wide = wide(b_maps), wide(c_maps)
        if first:
            d_b = d_c = jnp.zeros((BLOCK, state), F32)
        else:
            d_b, d_c = bc_old[rows, :state], bc_old[rows, state:]
        if last:
            dsc = dsc_ref[rows, :]
            d_c = d_c + mm3(split(dsc), b_maps)
            d_b = d_b + mm3(split(dsc.T), c_maps)
        sums = jnp.zeros((BLOCK, LANES), F32)
        direct = jnp.zeros((BLOCK, LANES), F32)
        for at, among, head in stage.steps():
            got = got_ref[:, at]
            entering = split(el_ref[rows, among] + got * expand(from_first, head, tile))
            leaving = split(gl_ref[nxt, at] + got * expand(to_last, head, tile))
            x = x_ref[rows, among]
            step_x, shrunk_x, grown_x = expand(step, head, tile), expand(shrunk, head, tile), expand(grown, head, tile)
            xs = x * step_x
            gy = gy_ref[rows, among].astype(F32)
            y = yw_ref[rows, at] + grown_x * mm_wide(c_wide, entering)
            dxs = dw_ref[rows, at] + shrunk_x * mm_wide(b_wide, leaving)
            d_c = d_c + mm_over(split(gy * grown_x), entering)
            d_b = d_b + mm_over(split(xs * shrunk_x), leaving)
            both = head_sums([gy * y - xs * dxs, dxs * x], ontos[head])
            sums, direct = sums + both[0], direct + both[1]
            dz[0:BLOCK, at] = (dxs * step_x + expand(skips, head, tile) * gy) * ds_ref[rows, among]
        sums_high, sums_low = split(sums)
        d_log = mm(upper, sums_high) + mm(upper, sums_low) + carry_ref[0:1, :]
        carry_ref[...] = jnp.broadcast_to(d_log[0:1, :], (8, LANES))
        d_step = (d_log * rates + direct) * sg_ref[rows, :]
        lane = iota((BLOCK, LANES), 1)
        d_step = jnp.where((lane >= stage.head) & (lane < stage.head + width // HEAD), d_step, 0.0)
        if not first:
            d_step = d_step + dst_old[rows, :]
        if last:
            turned = d_step.T
            for n in range(plan.spans):
                s_sc[pl.ds(b * PAD, PAD), n * LANES : (n + 1) * LANES] = turned[n * PAD : (n + 1) * PAD]
            dz[0:BLOCK, width : width + state] = d_b * dm_ref[rows, :state]
            dz[0:BLOCK, width + state :] = d_c * dm_ref[rows, state:]
        else:
            dst_ref[rows, :] = d_step
            bc_ref[rows, :state] = d_b
            bc_ref[rows, state:] = d_c
        dz[BLOCK:, :] = nxt_dz[...]
        for c in range(0, conv, LANES):
            window = dz[:, c : c + LANES]
            if c < width:
                cols = pl.ds(pl.multiple_of(own * plan.all + stage.start + c, LANES), LANES)
            else:
                cols = slice(plan.inner + c - width, plan.inner + c - width + LANES)
            weight = cw_ref[:, cols]
            grad = weight[0:1, :] * window[0:BLOCK, :]
            for k in range(1, weight.shape[0]):
                grad = grad + weight[k : k + 1, :] * window[k : k + BLOCK, :]
            if c < width:
                o_sc[rows, c : c + LANES] = grad.astype(BF16)
            else:
                high, low = split(grad)
                o_sc[rows, c : c + LANES] = high
                o_sc[rows, maps + c : maps + c + LANES] = low
        nxt_dz[...] = dz[0:PAD, :]
        return carry

    each_block(blocks, body)
    for k in range(half):
        to = jnp.bitwise_xor(own, k)
        outs[k][0:BLOCK, :] = o_sc[pl.ds(pl.multiple_of(to * BLOCK, BLOCK), BLOCK), :]
        if last:
            outs[k][BLOCK:, :] = s_sc[pl.ds(pl.multiple_of(to * PAD, PAD), PAD), :].astype(BF16)


def owner_kernel(stage, *refs):
    plan, last, maps = stage.plan, stage.last, stage.plan.maps
    half, width = plan.half, plan.width
    outs, refs = refs[:half], refs[half:]
    if stage.part:
        refs = refs[1:]
    f_ref = refs[0]
    own, _ = place(plan)
    pairs = []
    for k in range(half):
        start = pl.multiple_of(jnp.bitwise_xor(own, k) * plan.all + stage.start, LANES)
        pairs.append((outs[k].at[pl.ds(0, BLOCK), pl.ds(0, width)], f_ref.at[:, pl.ds(start, width)]))
    copies = [pltpu.make_async_copy(source, target, refs[-1].at[n]) for n, (source, target) in enumerate(pairs)]
    for copy in copies:
        copy.start()
    if last:
        m_ref, s_ref = refs[1:3]
        total = jnp.zeros((BLOCK, maps), F32)
        steps = jnp.zeros((LANES, BLOCK), F32)
        for k in range(half):
            part, end = jnp.bitwise_xor(own, k), outs[k]
            turned = end[BLOCK:, :].astype(F32)
            mine = [turned[:, n * LANES : (n + 1) * LANES] for n in range(plan.spans)]
            mine.append(jnp.zeros((LANES - plan.spans * PAD, LANES), F32))
            steps = steps + pltpu.roll(jnp.concatenate(mine, axis=0), part * plan.heads, 0)
            high, low = end[0:BLOCK, width : width + maps], end[0:BLOCK, width + maps :]
            total = total + (high.astype(F32) + low.astype(F32))
        m_ref[...] = total.astype(BF16)
        s_ref[...] = steps[: s_ref.shape[0]].astype(BF16)
    for copy in copies:
        copy.wait()


def per_device(sections, devices, features, state_maps, step_raw, conv_weight, conv_bias, decay_log, step_bias, skip_gain, output_grads):
    state = state_maps.shape[2] // 2
    heads = decay_log.shape[1]
    plan = Plan(devices, features.shape[2], state, heads)
    half, width, tokens, parts, maps = plan.half, plan.width, plan.tokens, plan.parts, plan.maps
    weight = conv_weight[0]
    stages = [Stage(plan, p) for p in range(parts)]

    def partner(array, k):
        return lax.ppermute(array, "ctx", [(i, i ^ k) for i in range(devices)])

    def shifted(array, k):
        route = [
            (((p + 1) % sections) * devices + i, p * devices + (i ^ k))
            for p in range(sections)
            for i in range(devices)
        ]
        return lax.ppermute(array, ("pipe", "ctx"), route)

    conv = plan.all + maps
    away = pl.BlockSpec(memory_space=pl.ANY)
    far = pl.BlockSpec(memory_space=pltpu.HBM)

    def hold(array):
        return pltpu.with_memory_space_constraint(array, pltpu.HBM)

    packed = call(
        pack_kernel,
        plan,
        [struct(BLOCK, conv + LANES, dtype=BF16)] * half + [struct(16, conv, dtype=BF16)] * half,
        [pltpu.SemaphoreType.DMA((half * (4 + BLOCK // heads),))],
        work=3.0,
        in_specs=[far] * 3,
    )(hold(features[0]), hold(state_maps[0]), hold(step_raw[0].T))
    cuts = call(
        cut_kernel,
        plan,
        [struct(BLOCK, plan.all, dtype=BF16)] * half,
        [pltpu.SemaphoreType.DMA((half,))],
        work=2.2,
        in_specs=[far],
    )(hold(output_grads[0]))
    pays = [packed[0]] + [partner(packed[k], k) for k in range(1, half)]
    edges = [lax.ppermute(e, "ctx", [(half - 1, half + k)]) for k, e in enumerate(packed[half:])]
    grads = [shifted(cuts[k], k) for k in range(half)]
    done = []
    small = pltpu.VMEM((8, LANES), F32)
    x_conv, dsilu, states, x_maps, d_maps, steps, sigmoids, cums = call(
        forward_kernel,
        plan,
        [near(tokens, plan.all), near(tokens, plan.all), near(tokens + BLOCK, plan.all), near(tokens, maps),
         near(tokens, maps)] + [near(tokens, LANES)] * 3,
        [pltpu.VMEM((tokens + PAD, conv), F32), pltpu.VMEM((tokens, LANES), F32), small],
        work=5.0,
    )(*pays, *edges, weight, conv_bias, decay_log, step_bias)
    for stage in stages:
        first = stage.first
        args = [] if first else [gy, top, scores]
        args += [*(grads if first else ()), x_maps, cums, states, x_conv, dsilu, d_maps, steps, skip_gain]
        outs = [near(tokens + BLOCK, width), struct(BLOCK + stage.edge, width)]
        if not stage.last:
            outs += [near(16, state + BLOCK)]
        if first:
            outs += [near(tokens, plan.all, dtype=BF16)]
        back, send, *rest = call(gradient_kernel, stage, outs, [small], work=2.1)(*args)
        if first:
            top, gy = rest
            within = []
            for other in stages:
                outs = [near(tokens, width), near(tokens, width), near(tokens, BLOCK)]
                args = [x_conv, x_maps, steps, cums, gy] + ([] if other.first else [scores])
                y_within, d_within, scores = call(within_kernel, other, outs, work=2.0)(*args)
                within.append((y_within, d_within))
        got = partner(send, half)
        done.append((got, x_conv, x_maps, dsilu, steps, sigmoids, cums, states, back, gy, *within[stage.part]))
    feature_parts = []
    for stage, arrays in zip(stages, done):
        first, last = stage.first, stage.last
        conv = width + maps if last else width
        out = width + 2 * maps if last else width
        args = [*arrays, weight, decay_log, skip_gain]
        outs = [struct(BLOCK + (PAD if last else 0), out, dtype=BF16)] * half
        scratch = [small, pltpu.VMEM((BLOCK + PAD, conv), F32), pltpu.VMEM((PAD, conv), F32), small,
                   pltpu.VMEM((tokens, out), BF16), pltpu.VMEM((max(8, plan.blocks), LANES), F32)]
        if last:
            args += [scores, d_maps]
            scratch += [pltpu.VMEM((PAD * plan.blocks, out), F32)]
        else:
            outs += [near(tokens, maps), near(16, state), near(tokens, LANES)]
        if not first:
            args += carried
        result = call(final_kernel, stage, outs, scratch, work=5.8)(*args)
        feature_parts += [result[0]] + [partner(result[k], k) for k in range(1, half)]
        carried = result[half:]
    inside = pl.BlockSpec(memory_space=pltpu.VMEM)
    for stage in stages:
        more = [feature_grads] if stage.part else []
        outs = [struct(BLOCK, plan.inner, dtype=BF16)]
        if stage.last:
            outs += [struct(BLOCK, maps, dtype=BF16), struct(heads, BLOCK, dtype=BF16)]
        feature_grads, *others = call(
            owner_kernel,
            stage,
            outs,
            [pltpu.SemaphoreType.DMA((half,))],
            work=2.0,
            in_specs=[inside] * half + [away] * len(more),
            out_specs=[away] + [inside] * (len(outs) - 1),
            input_output_aliases={half: 0} if more else {},
        )(*feature_parts[stage.part * half : (stage.part + 1) * half], *more)
    map_grads, step_grads = others
    return (feature_grads[None], map_grads[None], step_grads.T[None])


def solution(mesh):
    return jax.shard_map(
        functools.partial(per_device, mesh.shape["pipe"], mesh.shape["ctx"]),
        mesh=mesh,
        in_specs=(
            P("pipe", "ctx", None),
            P("pipe", "ctx", None),
            P("pipe", "ctx", None),
            P("pipe", None, None),
            P("pipe", None),
            P("pipe", None),
            P("pipe", None),
            P("pipe", None),
            P("pipe", "ctx", None),
        ),
        out_specs=(P("pipe", "ctx", None), P("pipe", "ctx", None), P("pipe", "ctx", None)),
        check_vma=False,
    )
```

```python
import functools

import jax
import jax.numpy as jnp
from jax import lax
from jax.experimental import pallas as pl
from jax.experimental.pallas import tpu as pltpu
from jax.sharding import PartitionSpec as P

BLOCK = 128
LANES = 128
HEAD = 64
PAD = 8
PARTS = 2
UNROLL = 4
F32 = jnp.float32
BF16 = jnp.bfloat16
NEG = -1e30
NN = (((1,), (0,)), ((), ()))
NT = (((1,), (1,)), ((), ()))
TN = (((0,), (0,)), ((), ()))


def mm(a, b, dims=NN):
    return lax.dot_general(a, b, dims, preferred_element_type=F32)


def split(a):
    high = a.astype(BF16)
    return high, (a - high.astype(F32)).astype(BF16)


def mm3(a, b, dims=NN):
    (ah, al), (bh, bl) = a, b
    return mm(ah, bh, dims) + (mm(ah, bl, dims) + mm(al, bh, dims))


def iota(shape, axis):
    return lax.broadcasted_iota(jnp.int32, shape, axis)


def wide(a):
    high, low = a
    return jnp.concatenate([high, low], axis=1), high


def mm_wide(a, b):
    (both, high), (bh, bl) = a, b
    return mm(both, jnp.concatenate([bh, bh], axis=0)) + mm(high, bl)


def mm_over(a, b):
    (ah, al), (bh, bl) = a, b
    n = bh.shape[0]
    both = mm(ah, jnp.concatenate([bh, bl], axis=0), NT)
    return both[:, :n] + (both[:, n:] + mm(al, bh, NT))


def expand(values, head, count=LANES):
    rows = values.shape[0]
    left = iota((rows, LANES), 1) < HEAD
    tiles = []
    for h in range(head, head + count // HEAD, 2):
        first = jnp.broadcast_to(values[:, h : h + 1], (rows, LANES))
        second = jnp.broadcast_to(values[:, h + 1 : h + 2], (rows, LANES))
        tiles.append(jnp.where(left, first, second))
    return tiles[0] if len(tiles) == 1 else jnp.concatenate(tiles, axis=1)


def onto_heads(head, count):
    shape = (count, LANES)
    return (iota(shape, 1) == head + iota(shape, 0) // HEAD).astype(F32).astype(BF16)


def head_sums(values, onto):
    rows = values[0].shape[0]
    sums = mm(jnp.concatenate([part for value in values for part in split(value)], axis=0), onto)
    return [sums[2 * n * rows : (2 * n + 1) * rows] + sums[(2 * n + 1) * rows : (2 * n + 2) * rows] for n in range(len(values))]


class Plan:
    def __init__(self, devices, inner, state, heads):
        self.half = devices // 2
        self.inner = inner
        self.state = state
        self.maps = 2 * state
        self.heads = heads // self.half
        self.all = inner // self.half
        self.parts = PARTS
        self.width = self.all // PARTS
        self.tile = 2 * LANES if self.width % (2 * LANES) == 0 else LANES
        self.tiles = self.width // self.tile
        self.blocks = self.half
        self.spans = -(-self.heads // PAD)
        self.tokens = self.half * BLOCK
        self.lots = (self.all + self.maps) // LANES
        self.below = PAD * -(-(heads // PAD) // self.lots)

    def lot(self, n):
        return slice(BLOCK + n // self.lots * PAD, BLOCK + (n // self.lots + 1) * PAD), n % self.lots * LANES


class Stage:
    def __init__(self, plan, part):
        self.plan = plan
        self.part = part
        self.first = part == 0
        self.last = part == plan.parts - 1
        self.head = part * plan.width // HEAD
        self.start = part * plan.width

        self.edge = 2 * PAD if self.last else PAD
        self.grown = PAD if self.last else 3

    def steps(self):
        tile = self.plan.tile
        for i in range(self.plan.tiles):
            lane = self.start + i * tile
            yield slice(i * tile, (i + 1) * tile), slice(lane, lane + tile), lane // HEAD


def each_block(blocks, body):
    if blocks <= UNROLL:
        for b in range(blocks):
            body(b, 0)
    else:
        lax.fori_loop(0, blocks, body, 0)


def place(plan):
    rank = lax.axis_index("ctx")
    return lax.rem(rank, plan.half), lax.div(rank, plan.half)


def call(kernel, stage, out_shape, scratch=(), work=1.0, **more):
    return pl.pallas_call(
        functools.partial(kernel, stage),
        out_shape=out_shape,
        scratch_shapes=list(scratch),
        compiler_params=pltpu.CompilerParams(vmem_limit_bytes=32 * 1024 * 1024),
        cost_estimate=pl.CostEstimate(flops=int(work * 1.15e9), transcendentals=0, bytes_accessed=1 << 20),
        **more,
    )


def struct(*shape, dtype=F32):
    return jax.ShapeDtypeStruct(shape, dtype)


def near(*shape, dtype=F32):
    return pltpu.VMEM(shape, dtype)


def head_rows(plan, prm, refs, own):
    prm[...] = jnp.zeros_like(prm)
    for row, values in enumerate(refs):
        prm[row : row + 1, 0 : values.shape[1]] = values
    local = pltpu.roll(prm[...], lax.rem(LANES - own * plan.heads, LANES), 1)
    return [local[row : row + 1, :] for row in range(len(refs))]


def run_copies(pairs, sems):
    copies = [pltpu.make_async_copy(source, target, sems.at[n]) for n, (source, target) in enumerate(pairs)]
    for copy in copies:
        copy.start()
    for copy in copies:
        copy.wait()


def pack_kernel(plan, f_ref, m_ref, s_ref, *refs):
    pays, edges, sems = refs[: plan.half], refs[plan.half : -1], refs[-1]
    own, _ = place(plan)
    whole, heads = plan.all, s_ref.shape[0]
    pairs = []
    for k in range(plan.half):
        start = pl.multiple_of(jnp.bitwise_xor(own, k) * whole, LANES)
        pairs.append((f_ref.at[:, pl.ds(start, whole)], pays[k].at[pl.ds(0, BLOCK), pl.ds(0, whole)]))
        pairs.append((m_ref, pays[k].at[pl.ds(0, BLOCK), pl.ds(whole, plan.maps)]))
        for n in range(heads // PAD):
            rows, lane = plan.lot(n)
            pairs.append((s_ref.at[pl.ds(n * PAD, PAD), :], pays[k].at[rows, pl.ds(lane, LANES)]))
        tail = pl.ds(BLOCK - 16, 16)
        pairs.append((f_ref.at[tail, pl.ds(k * whole, whole)], edges[k].at[:, pl.ds(0, whole)]))
        pairs.append((m_ref.at[tail, :], edges[k].at[:, pl.ds(whole, plan.maps)]))
    run_copies(pairs, sems)


def cut_kernel(plan, o_ref, *refs):
    own, _ = place(plan)
    pairs = []
    for k in range(plan.half):
        start = pl.multiple_of(jnp.bitwise_xor(own, k) * plan.all, LANES)
        pairs.append((o_ref.at[:, pl.ds(start, plan.all)], refs[k]))
    run_copies(pairs, refs[-1])


def forward_kernel(plan, *refs):
    half, width, maps, tile = plan.half, plan.all, plan.maps, plan.tile
    conv = width + maps
    pays, edges = refs[:half], refs[half : 2 * half]
    (cw_ref, cb_ref, dl_ref, sb_ref, x_ref, ds_ref, el_ref, xm_ref, dm_ref, st_ref, sg_ref, cum_ref,
     raw, sraw, prm) = refs[2 * half :]
    own, _ = place(plan)
    heads = dl_ref.shape[1]
    halo = edges[0][...].astype(F32)
    for k in range(1, half):
        halo = halo + edges[k][...].astype(F32)
    raw[0:PAD, :] = halo[16 - PAD :, :]
    sraw[...] = jnp.zeros_like(sraw)
    for k in range(half):
        block = jnp.bitwise_xor(own, k) * BLOCK
        raw[pl.ds(pl.multiple_of(block + PAD, 8), BLOCK), :] = pays[k][0:BLOCK, :].astype(F32)
        lots = [plan.lot(n) for n in range(heads // PAD)]
        turned = jnp.concatenate([pays[k][rows, lane : lane + LANES].astype(F32) for rows, lane in lots], axis=0)
        sraw[pl.ds(pl.multiple_of(block, 8), BLOCK), 0:heads] = turned.T
    rates, offsets = head_rows(plan, prm, [-jnp.exp(dl_ref[...]), sb_ref[...]], own)
    shift = lax.rem(LANES - own * plan.heads, LANES)
    lower = (iota((BLOCK, BLOCK), 0) >= iota((BLOCK, BLOCK), 1)).astype(F32)
    el_ref[0:BLOCK, :] = jnp.zeros((BLOCK, width), F32)

    def body(b, carry):
        row = pl.multiple_of(b * BLOCK, BLOCK)
        rows = pl.ds(row, BLOCK)
        for c in range(0, conv, tile):
            window = raw[pl.ds(row, BLOCK + PAD), c : c + tile]
            if c < width:
                cols = pl.ds(pl.multiple_of(own * width + c, LANES), tile)
                to_x, to_d, at = x_ref, ds_ref, c
            else:
                cols = slice(plan.inner + c - width, plan.inner + c - width + tile)
                to_x, to_d, at = xm_ref, dm_ref, c - width
            weight = cw_ref[:, cols]
            v = jnp.broadcast_to(cb_ref[:, cols], (BLOCK, tile))
            for k in range(weight.shape[0]):
                v = v + weight[k : k + 1, :] * window[PAD - k : PAD - k + BLOCK, :]
            s = 1.0 / (1.0 + jnp.exp(-v))
            to_x[rows, at : at + tile] = v * s
            to_d[rows, at : at + tile] = s * (1.0 + v * (1.0 - s))
        a = pltpu.roll(sraw[rows, :], shift, 1) + offsets
        e = jnp.exp(-jnp.abs(a))
        u = 1.0 + e
        d = u - 1.0
        step = jnp.maximum(a, 0.0) + jnp.where(d == 0.0, e, jnp.log(u) * (e / jnp.where(d == 0.0, 1.0, d)))
        st_ref[rows, :] = step
        sg_ref[rows, :] = jnp.where(a >= 0.0, 1.0, e) / u
        cum = lax.dot_general(lower, step * rates, NN, precision=lax.Precision.HIGHEST, preferred_element_type=F32)
        cum_ref[rows, :] = cum
        total = cum[BLOCK - 1 :, :]
        weighted = jnp.exp(total - cum) * step
        decay = jnp.exp(total)
        bt = wide(split(xm_ref[rows, : plan.state].T))
        nxt = pl.ds(pl.multiple_of(row + BLOCK, BLOCK), BLOCK)
        for c in range(0, width, tile):
            at, head = slice(c, c + tile), c // HEAD
            wx = split(x_ref[rows, at] * expand(weighted, head, tile))
            el_ref[nxt, at] = el_ref[rows, at] * expand(decay, head, tile) + mm_wide(bt, wx)
        return carry

    lax.fori_loop(0, plan.blocks, body, 0)


def gradient_kernel(stage, *refs):
    plan, first, last = stage.plan, stage.first, stage.last
    half, width, blocks, tile, state = plan.half, plan.width, plan.blocks, plan.tile, plan.state
    if first:
        grads, refs = refs[:half], refs[half:]
    else:
        gy_ref, top_old, after, refs = refs[0], refs[1], refs[2], refs[3:]
    xm_ref, cum_ref, el_ref, x_ref, ds_ref, dm_ref, st_ref, sk_ref, gl_ref, send_ref = refs[:10]
    if not last:
        top_ref = refs[10]
    if first:
        gy_ref = refs[11]
    prm = refs[-1]
    own, late = place(plan)
    if first:
        for k in range(half):
            block = pl.multiple_of(jnp.bitwise_xor(own, k) * BLOCK, BLOCK)
            gy_ref[pl.ds(block, BLOCK), :] = grads[k][...]
    gl_ref[blocks * BLOCK :, :] = jnp.zeros((BLOCK, width), F32)

    def body(t, carry):
        row = pl.multiple_of((blocks - 1 - t) * BLOCK, BLOCK)
        rows = pl.ds(row, BLOCK)
        nxt = pl.ds(pl.multiple_of(row + BLOCK, BLOCK), BLOCK)
        cum = cum_ref[rows, :]
        grown, decay = jnp.exp(cum), jnp.exp(cum[BLOCK - 1 :, :])
        ct = wide(split(xm_ref[rows, plan.state :].T))
        for at, among, head in stage.steps():
            ge = split(gy_ref[rows, among].astype(F32) * expand(grown, head, tile))
            gl_ref[rows, at] = gl_ref[nxt, at] * expand(decay, head, tile) + mm_wide(ct, ge)
        return carry

    each_block(blocks, body)

    @pl.when(late == 0)
    def _():
        send_ref[0:BLOCK, :] = el_ref[blocks * BLOCK :, stage.start : stage.start + width]
        send_ref[BLOCK:, :] = jnp.zeros((stage.edge, width), F32)
        if not last:
            top_ref[...] = jnp.zeros_like(top_ref)

    @pl.when(late != 0)
    def _():
        send_ref[0:BLOCK, :] = gl_ref[0:BLOCK, :]
        (skips,) = head_rows(plan, prm, [sk_ref[...]], own)
        top = slice(0, 16)
        edge = send_ref.at[BLOCK : BLOCK + stage.edge, :]
        cum, step, cum_t = cum_ref[top, :], st_ref[top, :], cum_ref[0:BLOCK, :].T
        shrunk, grown = jnp.exp(cum_ref[BLOCK - 1 : BLOCK, :] - cum), jnp.exp(cum)
        top_b, first_c = split(xm_ref[top, :state]), split(xm_ref[0:BLOCK, state:])
        wide_b = wide(top_b)
        scores = mm3(top_b, first_c, NT)
        causal = iota((16, BLOCK), 0) <= iota((16, BLOCK), 1)
        if first:
            d_b, dsc = jnp.zeros((16, state), F32), jnp.zeros((16, BLOCK), F32)
        else:
            d_b, dsc = top_old[:, :state], top_old[:, state:]
        zero, blank = jnp.zeros((BLOCK, LANES), BF16), jnp.zeros((16, LANES), BF16)
        left, left_top = iota((BLOCK, LANES), 1) < HEAD, iota((16, LANES), 1) < HEAD
        for i in range(width // LANES):
            at, head = slice(i * LANES, (i + 1) * LANES), stage.head + 2 * i
            among = slice(head * HEAD, head * HEAD + LANES)
            step_x, shrunk_x = expand(step, head), expand(shrunk, head)
            xs = x_ref[top, among] * step_x
            gy = gy_ref[0:BLOCK, among]
            decays, mh, ml = [], [], []
            for h in (head, head + 1):
                spread = cum_t[h : h + 1, :] - jnp.broadcast_to(cum[:, h : h + 1], (16, BLOCK))
                decay = jnp.exp(jnp.where(causal, spread, NEG))
                high, low = split(scores * decay)
                decays.append(decay)
                mh.append(high)
                ml.append(low)
            gs = jnp.concatenate([jnp.where(left, gy, zero), jnp.where(left, zero, gy)], axis=0)
            dxs = mm(jnp.concatenate(mh, axis=1), gs) + mm(jnp.concatenate(ml, axis=1), gs)
            xh, xl = split(xs)
            rows = [jnp.where(left_top, xh, blank), jnp.where(left_top, blank, xh)]
            rows += [jnp.where(left_top, xl, blank), jnp.where(left_top, blank, xl)]
            dm = mm(jnp.concatenate(rows, axis=0), gy, NT)
            dsc = dsc + (dm[0:16] + dm[32:48]) * decays[0] + (dm[16:32] + dm[48:64]) * decays[1]
            leaving = split(gl_ref[BLOCK : 2 * BLOCK, at])
            dxs = dxs + shrunk_x * mm_wide(wide_b, leaving)
            d_b = d_b + mm_over(split(xs * shrunk_x), leaving)
            top_gy = gy[0:16].astype(F32)
            edge[0:PAD, at] = ((dxs * step_x + expand(skips, head) * top_gy) * ds_ref[top, among])[0:PAD]
            edge[stage.grown : stage.edge, at] = (top_gy * expand(grown, head))[0 : stage.edge - stage.grown]
        if last:
            parts = split(dsc)
            d_b = (d_b + mm3(parts, first_c)) * dm_ref[top, :state]
            d_c = mm3(parts, top_b, TN)
            silu_c = dm_ref[top, state:]
            edge[3:6, 0:state] = d_b[0:3]
            edge[6:8, 0:state] = silu_c[0:2]
            edge[11:14, 0:state] = d_c[0:3]
            edge[14:15, 0:state] = silu_c[2:3]
        else:
            top_ref[:, :state] = d_b
            top_ref[:, state:] = dsc


def within_kernel(stage, *refs):
    plan, first = stage.plan, stage.first
    x_ref, xm_ref, st_ref, cum_ref, gy_ref = refs[:5]
    refs = refs[5:]
    if not first:
        dsc_old, refs = refs[0], refs[1:]
    yw_ref, dw_ref, dsc_ref = refs
    width, state = plan.width, plan.state
    causal = iota((BLOCK, BLOCK), 0) >= iota((BLOCK, BLOCK), 1)
    left = iota((BLOCK, LANES), 1) < HEAD

    def body(b, carry):
        rows = pl.ds(pl.multiple_of(b * BLOCK, BLOCK), BLOCK)
        cum = cum_ref[rows, :]
        cum_t = cum.T
        step = st_ref[rows, :]
        b_maps = split(xm_ref[rows, :state])
        c_maps = split(xm_ref[rows, state:])
        scores = mm3(c_maps, b_maps, NT)
        total = jnp.zeros((BLOCK, BLOCK), F32) if first else dsc_old[rows, :]
        zero = jnp.zeros((BLOCK, LANES), BF16)
        for i in range(width // LANES):
            at, head = slice(i * LANES, (i + 1) * LANES), stage.head + 2 * i
            xs = x_ref[rows, head * HEAD : head * HEAD + LANES] * expand(step, head)
            xh, xl = split(xs)
            gy = gy_ref[rows, head * HEAD : head * HEAD + LANES]
            g0, g1 = jnp.where(left, gy, zero), jnp.where(left, zero, gy)
            decays, mh, ml = [], [], []
            for h in (head, head + 1):
                spread = jnp.broadcast_to(cum[:, h : h + 1], (BLOCK, BLOCK)) - cum_t[h : h + 1, :]
                decay = jnp.exp(jnp.where(causal, spread, NEG))
                high, low = split(scores * decay)
                decays.append(decay)
                mh.append(high)
                ml.append(low)
            both = jnp.concatenate(
                [
                    jnp.concatenate([jnp.where(left, xh, zero), jnp.where(left, xl, zero)], axis=1),
                    jnp.concatenate([jnp.where(left, zero, xh), jnp.where(left, zero, xl)], axis=1),
                ],
                axis=0,
            )
            high = mm(jnp.concatenate(mh, axis=1), both)
            low = mm(jnp.concatenate(ml, axis=1), both[:, :LANES])
            yw_ref[rows, at] = high[:, :LANES] + (high[:, LANES:] + low)
            gs = jnp.concatenate([g0, g1], axis=0)
            dw_ref[rows, at] = mm(jnp.concatenate(mh, axis=0), gs, TN) + mm(jnp.concatenate(ml, axis=0), gs, TN)
            dm = mm(jnp.concatenate([gs, gs], axis=1), jnp.concatenate([xh, xl], axis=1), NT)
            total = total + dm[:BLOCK] * decays[0] + dm[BLOCK:] * decays[1]
        dsc_ref[rows, :] = total
        return carry

    lax.fori_loop(0, plan.blocks, body, 0)


def final_kernel(stage, *refs):
    plan, first, last = stage.plan, stage.first, stage.last
    half, width, blocks, state, tile, maps = plan.half, plan.width, plan.blocks, plan.state, plan.tile, plan.maps
    (both_ref, x_ref, xm_ref, ds_ref, st_ref, sg_ref, cum_ref, el_ref, gl_ref, gy_ref, yw_ref, dw_ref,
     cw_ref, dl_ref, sk_ref) = refs[:15]
    refs = refs[15:]
    got_ref, edge_ref = both_ref.at[0:BLOCK, :], both_ref.at[BLOCK : BLOCK + stage.edge, :]
    if last:
        dsc_ref, dm_ref, refs = refs[0], refs[1], refs[2:]
    if not first:
        bc_old, ac_old, dst_old, refs = refs[0], refs[1], refs[2], refs[3:]
    outs, refs = refs[:half], refs[half:]
    if not last:
        bc_ref, ac_ref, dst_ref, refs = refs[0], refs[1], refs[2], refs[3:]
    prm, dz, nxt_dz, carry_ref, o_sc, lc_sc = refs[:6]
    if last:
        s_sc = refs[6]
        s_sc[...] = jnp.zeros_like(s_sc)
    conv = width + maps if last else width
    own, late = place(plan)
    is_late = late.astype(F32)
    rates, skips = head_rows(plan, prm, [-jnp.exp(dl_ref[...]), sk_ref[...]], own)
    upper = (iota((BLOCK, BLOCK), 0) <= iota((BLOCK, BLOCK), 1)).astype(F32).astype(BF16)
    after_c = jnp.zeros((16, state), F32) if first else ac_old[...]
    for at, among, _ in stage.steps():
        rows = edge_ref[:, at]
        if not last:
            rows = jnp.concatenate([jnp.zeros((PAD, tile), F32), rows[3:6], jnp.zeros((5, tile), F32)], axis=0)
        after_c = after_c + mm_over(split(rows), split(el_ref[blocks * BLOCK :, among]))
    early = iota((PAD, LANES), 0) * 0 + late == 0
    for c in range(0, width, LANES):
        nxt_dz[:, c : c + LANES] = jnp.where(early, edge_ref[0:PAD, c : c + LANES], 0.0)
    if last:
        rest = jnp.zeros((PAD - 3, state), F32)
        nxt_dz[:, width : width + state] = jnp.where(early, jnp.concatenate([edge_ref[3:6, 0:state], rest], axis=0), 0.0)
        silu_c = jnp.concatenate([edge_ref[6:8, 0:state], edge_ref[14:15, 0:state]], axis=0)
        after_c = (after_c[PAD : PAD + 3] + edge_ref[11:14, 0:state]) * silu_c
        nxt_dz[:, width + state :] = jnp.where(early, jnp.concatenate([after_c, rest], axis=0), 0.0)
    else:
        ac_ref[...] = after_c
    lc_sc[...] = jnp.zeros_like(lc_sc)
    for b in range(1, blocks):
        lc_sc[b : b + 1, :] = lc_sc[b - 1 : b, :] + cum_ref[b * BLOCK - 1 : b * BLOCK, :]
    whole = lc_sc[blocks - 1 : blocks, :] + cum_ref[blocks * BLOCK - 1 :, :]
    ends = jnp.zeros((8, LANES), F32)
    ontos = {head: onto_heads(head, tile) for _, _, head in stage.steps()}
    for at, among, head in stage.steps():
        product = jnp.sum(got_ref[:, at] * el_ref[blocks * BLOCK :, among], axis=0, keepdims=True)
        ends = ends + head_sums([jnp.broadcast_to(product, (16, tile))], ontos[head])[0][0:8]
    carry_ref[...] = ends * (1.0 - is_late)

    def body(t, carry):
        b = blocks - 1 - t
        row = pl.multiple_of(b * BLOCK, BLOCK)
        rows = pl.ds(row, BLOCK)
        nxt = pl.ds(pl.multiple_of(row + BLOCK, BLOCK), BLOCK)
        cum, step = cum_ref[rows, :], st_ref[rows, :]
        total = cum[BLOCK - 1 :, :]
        grown, shrunk = jnp.exp(cum), jnp.exp(total - cum)
        before = lc_sc[pl.ds(b, 1), :]
        from_first = jnp.exp(before) * is_late
        to_last = jnp.exp(whole - before - total) * (1.0 - is_late)
        b_maps, c_maps = split(xm_ref[rows, :state]), split(xm_ref[rows, state:])
        b_wide, c_wide = wide(b_maps), wide(c_maps)
        if first:
            d_b = d_c = jnp.zeros((BLOCK, state), F32)
        else:
            d_b, d_c = bc_old[rows, :state], bc_old[rows, state:]
        if last:
            dsc = dsc_ref[rows, :]
            d_c = d_c + mm3(split(dsc), b_maps)
            d_b = d_b + mm3(split(dsc.T), c_maps)
        sums = jnp.zeros((BLOCK, LANES), F32)
        direct = jnp.zeros((BLOCK, LANES), F32)
        for at, among, head in stage.steps():
            got = got_ref[:, at]
            entering = split(el_ref[rows, among] + got * expand(from_first, head, tile))
            leaving = split(gl_ref[nxt, at] + got * expand(to_last, head, tile))
            x = x_ref[rows, among]
            step_x, shrunk_x, grown_x = expand(step, head, tile), expand(shrunk, head, tile), expand(grown, head, tile)
            xs = x * step_x
            gy = gy_ref[rows, among].astype(F32)
            y = yw_ref[rows, at] + grown_x * mm_wide(c_wide, entering)
            dxs = dw_ref[rows, at] + shrunk_x * mm_wide(b_wide, leaving)
            d_c = d_c + mm_over(split(gy * grown_x), entering)
            d_b = d_b + mm_over(split(xs * shrunk_x), leaving)
            both = head_sums([gy * y - xs * dxs, dxs * x], ontos[head])
            sums, direct = sums + both[0], direct + both[1]
            dz[0:BLOCK, at] = (dxs * step_x + expand(skips, head, tile) * gy) * ds_ref[rows, among]
        sums_high, sums_low = split(sums)
        d_log = mm(upper, sums_high) + mm(upper, sums_low) + carry_ref[0:1, :]
        carry_ref[...] = jnp.broadcast_to(d_log[0:1, :], (8, LANES))
        d_step = (d_log * rates + direct) * sg_ref[rows, :]
        lane = iota((BLOCK, LANES), 1)
        d_step = jnp.where((lane >= stage.head) & (lane < stage.head + width // HEAD), d_step, 0.0)
        if not first:
            d_step = d_step + dst_old[rows, :]
        if last:
            turned = d_step.T
            for n in range(plan.spans):
                s_sc[pl.ds(b * PAD, PAD), n * LANES : (n + 1) * LANES] = turned[n * PAD : (n + 1) * PAD]
            dz[0:BLOCK, width : width + state] = d_b * dm_ref[rows, :state]
            dz[0:BLOCK, width + state :] = d_c * dm_ref[rows, state:]
        else:
            dst_ref[rows, :] = d_step
            bc_ref[rows, :state] = d_b
            bc_ref[rows, state:] = d_c
        dz[BLOCK:, :] = nxt_dz[...]
        for c in range(0, conv, LANES):
            window = dz[:, c : c + LANES]
            if c < width:
                cols = pl.ds(pl.multiple_of(own * plan.all + stage.start + c, LANES), LANES)
            else:
                cols = slice(plan.inner + c - width, plan.inner + c - width + LANES)
            weight = cw_ref[:, cols]
            grad = weight[0:1, :] * window[0:BLOCK, :]
            for k in range(1, weight.shape[0]):
                grad = grad + weight[k : k + 1, :] * window[k : k + BLOCK, :]
            if c < width:
                o_sc[rows, c : c + LANES] = grad.astype(BF16)
            else:
                high, low = split(grad)
                o_sc[rows, c : c + LANES] = high
                o_sc[rows, maps + c : maps + c + LANES] = low
        nxt_dz[...] = dz[0:PAD, :]
        return carry

    each_block(blocks, body)
    for k in range(half):
        to = jnp.bitwise_xor(own, k)
        outs[k][0:BLOCK, :] = o_sc[pl.ds(pl.multiple_of(to * BLOCK, BLOCK), BLOCK), :]
        if last:
            outs[k][BLOCK:, :] = s_sc[pl.ds(pl.multiple_of(to * PAD, PAD), PAD), :].astype(BF16)


def owner_kernel(stage, *refs):
    plan, last, maps = stage.plan, stage.last, stage.plan.maps
    half, width = plan.half, plan.width
    outs, refs = refs[:half], refs[half:]
    if stage.part:
        refs = refs[1:]
    f_ref = refs[0]
    own, _ = place(plan)
    pairs = []
    for k in range(half):
        start = pl.multiple_of(jnp.bitwise_xor(own, k) * plan.all + stage.start, LANES)
        pairs.append((outs[k].at[pl.ds(0, BLOCK), pl.ds(0, width)], f_ref.at[:, pl.ds(start, width)]))
    copies = [pltpu.make_async_copy(source, target, refs[-1].at[n]) for n, (source, target) in enumerate(pairs)]
    for copy in copies:
        copy.start()
    if last:
        m_ref, s_ref = refs[1:3]
        total = jnp.zeros((BLOCK, maps), F32)
        steps = jnp.zeros((LANES, BLOCK), F32)
        for k in range(half):
            part, end = jnp.bitwise_xor(own, k), outs[k]
            turned = end[BLOCK:, :].astype(F32)
            mine = [turned[:, n * LANES : (n + 1) * LANES] for n in range(plan.spans)]
            mine.append(jnp.zeros((LANES - plan.spans * PAD, LANES), F32))
            steps = steps + pltpu.roll(jnp.concatenate(mine, axis=0), part * plan.heads, 0)
            high, low = end[0:BLOCK, width : width + maps], end[0:BLOCK, width + maps :]
            total = total + (high.astype(F32) + low.astype(F32))
        m_ref[...] = total.astype(BF16)
        s_ref[...] = steps[: s_ref.shape[0]].astype(BF16)
    for copy in copies:
        copy.wait()


def per_device(sections, devices, features, state_maps, step_raw, conv_weight, conv_bias, decay_log, step_bias, skip_gain, output_grads):
    state = state_maps.shape[2] // 2
    heads = decay_log.shape[1]
    plan = Plan(devices, features.shape[2], state, heads)
    half, width, tokens, parts, maps = plan.half, plan.width, plan.tokens, plan.parts, plan.maps
    weight = conv_weight[0]
    stages = [Stage(plan, p) for p in range(parts)]

    def partner(array, k):
        return lax.ppermute(array, "ctx", [(i, i ^ k) for i in range(devices)])

    def shifted(array, k):
        route = [
            (((p + 1) % sections) * devices + i, p * devices + (i ^ k))
            for p in range(sections)
            for i in range(devices)
        ]
        return lax.ppermute(array, ("pipe", "ctx"), route)

    conv = plan.all + maps
    away = pl.BlockSpec(memory_space=pl.ANY)
    far = pl.BlockSpec(memory_space=pltpu.HBM)

    def hold(array):
        return pltpu.with_memory_space_constraint(array, pltpu.HBM)

    packed = call(
        pack_kernel,
        plan,
        [struct(BLOCK + plan.below, conv, dtype=BF16)] * half + [struct(16, conv, dtype=BF16)] * half,
        [pltpu.SemaphoreType.DMA((half * (4 + heads // PAD),))],
        work=3.0,
        in_specs=[far] * 3,
    )(hold(features[0]), hold(state_maps[0]), hold(step_raw[0].T))
    cuts = call(
        cut_kernel,
        plan,
        [struct(BLOCK, plan.all, dtype=BF16)] * half,
        [pltpu.SemaphoreType.DMA((half,))],
        work=2.2,
        in_specs=[far],
    )(hold(output_grads[0]))
    pays = [packed[0]] + [partner(packed[k], k) for k in range(1, half)]
    edges = [lax.ppermute(e, "ctx", [(half - 1, half + k)]) for k, e in enumerate(packed[half:])]
    grads = [shifted(cuts[k], k) for k in range(half)]
    done = []
    small = pltpu.VMEM((8, LANES), F32)
    x_conv, dsilu, states, x_maps, d_maps, steps, sigmoids, cums = call(
        forward_kernel,
        plan,
        [near(tokens, plan.all), near(tokens, plan.all), near(tokens + BLOCK, plan.all), near(tokens, maps),
         near(tokens, maps)] + [near(tokens, LANES)] * 3,
        [pltpu.VMEM((tokens + PAD, conv), F32), pltpu.VMEM((tokens, LANES), F32), small],
        work=5.0,
    )(*pays, *edges, weight, conv_bias, decay_log, step_bias)
    for stage in stages:
        first = stage.first
        args = [] if first else [gy, top, scores]
        args += [*(grads if first else ()), x_maps, cums, states, x_conv, dsilu, d_maps, steps, skip_gain]
        outs = [near(tokens + BLOCK, width), struct(BLOCK + stage.edge, width)]
        if not stage.last:
            outs += [near(16, state + BLOCK)]
        if first:
            outs += [near(tokens, plan.all, dtype=BF16)]
        back, send, *rest = call(gradient_kernel, stage, outs, [small], work=2.1)(*args)
        if first:
            top, gy = rest
            within = []
            for other in stages:
                outs = [near(tokens, width), near(tokens, width), near(tokens, BLOCK)]
                args = [x_conv, x_maps, steps, cums, gy] + ([] if other.first else [scores])
                y_within, d_within, scores = call(within_kernel, other, outs, work=2.0)(*args)
                within.append((y_within, d_within))
        got = partner(send, half)
        done.append((got, x_conv, x_maps, dsilu, steps, sigmoids, cums, states, back, gy, *within[stage.part]))
    feature_parts = []
    for stage, arrays in zip(stages, done):
        first, last = stage.first, stage.last
        conv = width + maps if last else width
        out = width + 2 * maps if last else width
        args = [*arrays, weight, decay_log, skip_gain]
        outs = [struct(BLOCK + (PAD if last else 0), out, dtype=BF16)] * half
        scratch = [small, pltpu.VMEM((BLOCK + PAD, conv), F32), pltpu.VMEM((PAD, conv), F32), small,
                   pltpu.VMEM((tokens, out), BF16), pltpu.VMEM((max(8, plan.blocks), LANES), F32)]
        if last:
            args += [scores, d_maps]
            scratch += [pltpu.VMEM((PAD * plan.blocks, out), F32)]
        else:
            outs += [near(tokens, maps), near(16, state), near(tokens, LANES)]
        if not first:
            args += carried
        result = call(final_kernel, stage, outs, scratch, work=5.8)(*args)
        feature_parts += [result[0]] + [partner(result[k], k) for k in range(1, half)]
        carried = result[half:]
    inside = pl.BlockSpec(memory_space=pltpu.VMEM)
    for stage in stages:
        more = [feature_grads] if stage.part else []
        outs = [struct(BLOCK, plan.inner, dtype=BF16)]
        if stage.last:
            outs += [struct(BLOCK, maps, dtype=BF16), struct(heads, BLOCK, dtype=BF16)]
        feature_grads, *others = call(
            owner_kernel,
            stage,
            outs,
            [pltpu.SemaphoreType.DMA((half,))],
            work=2.0,
            in_specs=[inside] * half + [away] * len(more),
            out_specs=[away] + [inside] * (len(outs) - 1),
            input_output_aliases={half: 0} if more else {},
        )(*feature_parts[stage.part * half : (stage.part + 1) * half], *more)
    map_grads, step_grads = others
    return (feature_grads[None], map_grads[None], step_grads.T[None])


def solution(mesh):
    return jax.shard_map(
        functools.partial(per_device, mesh.shape["pipe"], mesh.shape["ctx"]),
        mesh=mesh,
        in_specs=(
            P("pipe", "ctx", None),
            P("pipe", "ctx", None),
            P("pipe", "ctx", None),
            P("pipe", None, None),
            P("pipe", None),
            P("pipe", None),
            P("pipe", None),
            P("pipe", None),
            P("pipe", "ctx", None),
        ),
        out_specs=(P("pipe", "ctx", None), P("pipe", "ctx", None), P("pipe", "ctx", None)),
        check_vma=False,
    )
```
